32 devices in a mesh: sec: 8 (over y, x, core), cross: 4 (over z).
Axes of the slice: x: 2, y: 2, z: 4, core: 2. Of those that a mesh axis runs over, the one named last changes fastest.
Arguments:
- rhs_field: float32 [2, 8, 2, 512, 512], P(None, 'sec', None, 'cross'), may hold values from -1.5 to 1.5
- slowness: float32 [8, 512, 512], P('sec', 'cross'), may hold values from 0.25 to 4
- absorb_depth: int32 [8], P('sec'), may hold values from 8 to 64
- line_inverse: bfloat16 [8, 2, 512, 512], P('sec'), may hold values from -1 to 1
- cross_inverse: bfloat16 [8, 2, 512, 512], P('sec', None, 'cross'), may hold values from -1 to 1
Outputs:
- solution: float32 [2, 8, 2, 512, 512], P(None, 'sec', None, 'cross')
- residual: float32 [2, 8, 2, 512, 512], P(None, 'sec', None, 'cross')
The draws below stay inside these ranges and needn't reach their ends.
All inputs are finite; a program needn't handle non-finite values.
Results may differ from the reference program's by a relative error of at most 0.02.
Values may be sent and summed in bfloat16 or wider, within the bound.
A program may use at most 64 MiB of HBM per device.

```python
import math
import jax
import jax.numpy as jnp
from jax import lax

NX = 512
NY = 512
RHS = 2
LAY = 1
NZ = 8


def assemble(phase_key, magnitude, remainder):
    order = magnitude.shape[-1]
    phase = jax.random.uniform(phase_key, magnitude.shape, jnp.float32, -math.pi, math.pi)
    diagonal = jnp.stack([magnitude * jnp.cos(phase), magnitude * jnp.sin(phase)], axis=1)
    identity = jnp.eye(order, dtype=jnp.float32)
    return remainder * (1.0 - identity) + diagonal[..., None] * identity


def draw_line_inverse(key, part):
    phase_key = jax.random.fold_in(jax.random.fold_in(key, 11), 0)
    remainder_key = jax.random.fold_in(jax.random.fold_in(key, 11), 2)
    sections = NZ // LAY
    magnitude = jnp.full((sections, NX), math.sqrt(0.92), jnp.float32)
    remainder = jax.random.normal(remainder_key, (sections, 2, NX, NX), jnp.float32) * (0.2 / math.sqrt(NX))
    return assemble(phase_key, magnitude, remainder).astype(jnp.bfloat16)


def draw_cross_inverse(key, part):
    phase_key = jax.random.fold_in(jax.random.fold_in(key, 23), 0)
    remainder_key = jax.random.fold_in(jax.random.fold_in(key, 23), 2)
    magnitude = jnp.full((NZ, NY), math.sqrt(0.92), jnp.float32)
    remainder = jax.random.normal(remainder_key, (NZ, 2, NY, NY), jnp.float32) * (0.2 / math.sqrt(NY))
    return assemble(phase_key, magnitude, remainder).astype(jnp.bfloat16)


def draw_absorb_depth(key, part):
    value_key, place_key = jax.random.split(jax.random.fold_in(key, 37))
    depth = jax.random.randint(value_key, (NZ,), 8, 65, dtype=jnp.int32)
    place = jax.random.randint(place_key, (), 0, NZ, dtype=jnp.int32)
    position = jnp.arange(NZ, dtype=jnp.int32)
    depth = jnp.where(position == place, 64, depth)
    depth = jnp.where(position == (place + 1) % NZ, 8, depth)
    return depth


def block_levels(stream_key, extent, cuts, low, largest):
    loudness, own = 1.0, jax.random.fold_in(stream_key, 6)
    for axis_at, shards_of in cuts:
        heights = jnp.exp(jax.random.uniform(jax.random.fold_in(own, axis_at), (shards_of,), jnp.float32, low / len(cuts), largest / len(cuts)))
        loudness = loudness * jnp.repeat(heights, extent[axis_at] // shards_of).reshape([-1 if axis == axis_at else 1 for axis in range(len(extent))])
    return loudness


def centred(stream_key, dims, width, most, pieces=(), kind=jnp.bfloat16):
    entries = jax.random.normal(stream_key, dims, jnp.float32) * width
    if len(pieces) > 0:
        entries = block_levels(stream_key, dims, pieces, -0.22, 0.18) * entries
    return jnp.clip(entries, min=-most, max=most).astype(kind)


def setup_inputs(seed: int = 0) -> dict:
    key_list = jax.random.split(jax.random.key(seed), 6)
    rhs_field = centred(key_list[0], (2, NZ, RHS, NY, NX), 0.25, 1.5, ((1, 8), (3, 4)), jnp.float32)
    slowness = jnp.clip(jnp.exp(math.log(4.0) - 2.7725887 * jax.random.uniform(key_list[1], (NZ, NY, NX), jnp.float32) ** block_levels(key_list[1], (NZ, NY, NX), ((0, 8), (1, 4)), -0.2, 0.2)), 0.25, 4.0)
    absorb_depth = draw_absorb_depth(jax.random.fold_in(key_list[5], 71), 0)
    line_inverse = draw_line_inverse(jax.random.fold_in(key_list[5], 71), 0)
    cross_inverse = draw_cross_inverse(jax.random.fold_in(key_list[5], 71), 0)
    return {"rhs_field": rhs_field, "slowness": slowness, "absorb_depth": absorb_depth, "line_inverse": line_inverse, "cross_inverse": cross_inverse}


SIGMA_TOP = 2.0
CENTER = 128.0 / 30.0
FACE = 14.0 / 30.0
EDGE = 3.0 / 30.0
CORNER = 1.0 / 30.0


def complex_line(source, matrix):
    real_part = jnp.dot(source[0], matrix[0], preferred_element_type=jnp.float32) - jnp.dot(source[1], matrix[1], preferred_element_type=jnp.float32)
    imag_part = jnp.dot(source[0], matrix[1], preferred_element_type=jnp.float32) + jnp.dot(source[1], matrix[0], preferred_element_type=jnp.float32)
    return jnp.stack([real_part, imag_part]).astype(jnp.bfloat16)


def cross_mix(mixed, cross):
    field = mixed.astype(jnp.float32)
    coupling = cross.astype(jnp.float32)
    real_part = jnp.einsum('yk,rkx->ryx', coupling[0], field[0]) - jnp.einsum('yk,rkx->ryx', coupling[1], field[1])
    imag_part = jnp.einsum('yk,rkx->ryx', coupling[0], field[1]) + jnp.einsum('yk,rkx->ryx', coupling[1], field[0])
    return jnp.stack([real_part, imag_part])


def absorption(absorb_depth, column_count):
    column = jnp.arange(column_count, dtype=jnp.int32)
    distance = jnp.minimum(column, column_count - 1 - column).astype(jnp.float32)
    depth = absorb_depth.astype(jnp.float32)[:, None]
    ramp = jnp.maximum(depth - distance[None, :], 0.0) / depth
    return SIGMA_TOP * ramp * ramp


def operate(field, padded, slowness, absorb_depth):
    layer_count = field.shape[1]
    line_count = field.shape[3]
    column_count = field.shape[4]
    weights = (0.0, FACE, EDGE, CORNER)
    near = jnp.zeros(field.shape, jnp.float32)
    for depth_move in (-1, 0, 1):
        for line_move in (-1, 0, 1):
            for column_move in (-1, 0, 1):
                reach = abs(depth_move) + abs(line_move) + abs(column_move)
                if reach > 0:
                    near = near + weights[reach] * padded[:, 1 + depth_move:1 + depth_move + layer_count, :, 1 + line_move:1 + line_move + line_count, 1 + column_move:1 + column_move + column_count]
    damping = absorption(absorb_depth, column_count)
    wave_real = slowness[:, None, :, :]
    wave_imag = wave_real * damping[:, None, None, :]
    real_part = CENTER * field[0] - near[0] - (wave_real * field[0] - wave_imag * field[1])
    imag_part = CENTER * field[1] - near[1] - (wave_real * field[1] + wave_imag * field[0])
    return jnp.stack([real_part, imag_part])


def reference(rhs_field, slowness, absorb_depth, line_inverse, cross_inverse):
    def layer_step(prior, inputs):
        rhs_layer, coupling, index = inputs
        source = (rhs_layer + prior).astype(jnp.bfloat16)
        matrix = lax.dynamic_index_in_dim(line_inverse, index // LAY, 0, keepdims=False)
        mixed = complex_line(source.reshape(2, RHS * NY, NX), matrix).reshape(2, RHS, NY, NX)
        result = cross_mix(mixed, coupling)
        return result, result

    initial = jnp.zeros((2, RHS, NY, NX), jnp.float32)
    rhs_layers = jnp.moveaxis(rhs_field, 1, 0)
    indices = jnp.arange(NZ, dtype=jnp.int32)
    _, layers = lax.scan(layer_step, initial, (rhs_layers, cross_inverse, indices))
    solution = jnp.moveaxis(layers, 0, 1)
    padded = jnp.pad(solution, ((0, 0), (1, 1), (0, 0), (1, 1), (1, 1)))
    residual = rhs_field - operate(solution, padded, slowness, absorb_depth)
    return solution, residual
```

```python
import functools

import jax
import jax.numpy as jnp
from jax import lax
from jax.experimental import pallas as pl
from jax.experimental.pallas import tpu as pltpu
from jax.sharding import PartitionSpec as P

MESH = pl.DeviceIdType.MESH
SIGMA_TOP = 2.0
CENTER = 128.0 / 30.0
FACE = 14.0 / 30.0
EDGE = 3.0 / 30.0
CORNER = 1.0 / 30.0
PAD = 16
RHS = 2
SUB = 2
BF = jnp.bfloat16


def kernel(
    n_s, n_c,
    rhs_ref, slow_ref, depth_ref, line_ref, cross_ref,
    sol_ref, res_ref,
    r_out, s_full, c2, ce_full, l_in, l_pair, c_pair, t_buf, y_acc, y_out, y_in, x_full, xo, ext, ext_next, p_out, p_in,
    go, rx_send, rx_recv, rp_send, rp_recv, cx_send, cx_recv, ce_send, ce_recv, l_send, l_recv, y_send, y_recv,
    xs_send, xp_send, xe_send, x_recv, ec_send, ec_recv, h_send, h_recv, nc_send, nc_recv, nh_send, nh_recv,
    p_send, p_recv,
):
    rows, cols = slow_ref.shape[1], slow_ref.shape[2]
    height = rows * n_c
    group = n_c // RHS
    two = RHS * rows
    piece = rows // SUB
    sec = lax.axis_index("sec")
    p = lax.axis_index("cross")
    r = p // group
    h = p % group
    q = (p + group) % n_c
    odd = sec % 2
    partner = sec + 1 - 2 * odd
    first = sec < 2
    final = sec >= n_s - 2
    below = jnp.minimum(sec + 1, n_s - 1)
    above = jnp.maximum(sec - 1, 0)

    def at(s, c):
        return {"sec": s, "cross": c}

    def remote(source, target, send, recv, where):
        return pltpu.make_async_remote_copy(
            src_ref=source, dst_ref=target, send_sem=send, recv_sem=recv,
            device_id=where, device_id_type=MESH,
        )

    barrier = pltpu.get_barrier_semaphore()

    def greet(s, c):
        pl.semaphore_signal(barrier, inc=1, device_id=at(s, c), device_id_type=MESH)

    for d in range(1, n_c):
        greet(sec, (p + d) % n_c)
    for d in range(n_c):
        greet(partner, (p + d) % n_c)

    outward = jnp.where(odd == 1, below, above)
    has_outward = jnp.where(odd == 1, sec < n_s - 1, sec > 0)

    @pl.when(has_outward)
    def _():
        for d in range(n_c):
            greet(outward, (p + d) % n_c)

    takes = jnp.logical_and(odd == 1, sec >= 2)
    hands_on = jnp.logical_and(odd == 1, sec <= n_s - 3)

    @pl.when(takes)
    def _():
        greet(sec - 2, p)

    @pl.when(hands_on)
    def _():
        greet(sec + 2, p)

    def block(b):
        return pl.ds(pl.multiple_of(b * rows, rows), rows)

    def row_block(k):
        return k * group + h

    for c in range(2):
        r_out[c] = rhs_ref[c, 0, 1 - r].astype(BF)
        s_full[c, block(p), :] = rhs_ref[c, 0, r].astype(BF)
        c2[c, block(r), :] = cross_ref[0, c]

    zeros_pad = jnp.zeros((PAD, cols), BF)

    @pl.when(p == 0)
    def _():
        for b in range(RHS):
            for c in range(2):
                ext[b, c, 0:PAD, :] = zeros_pad
                ext_next[b, c, 0:PAD, :] = zeros_pad

    @pl.when(p == n_c - 1)
    def _():
        for b in range(RHS):
            for c in range(2):
                ext[b, c, PAD + rows : PAD + rows + PAD, :] = zeros_pad
                ext_next[b, c, PAD + rows : PAD + rows + PAD, :] = zeros_pad

    met = (
        2 * n_c - 1
        + n_c * has_outward.astype(jnp.int32)
        + takes.astype(jnp.int32)
        + hands_on.astype(jnp.int32)
    )
    pl.semaphore_wait(barrier, met)

    def peer(d):
        return r * group + (h + d) % group

    def rx_copy():
        return remote(r_out, s_full.at[:, block(p), :], rx_send, rx_recv, at(sec, q))

    def rx_arrival():
        return remote(r_out, s_full.at[:, block(q), :], rx_send, rx_recv, at(sec, q))

    def rp_copy(d, k):
        b = row_block(k)
        return remote(
            s_full.at[:, block(b), :], s_full.at[:, block(b), :], rp_send.at[d, k], rp_recv.at[b], at(sec, peer(d))
        )

    def rp_arrival(b):
        return remote(
            s_full.at[:, block(b), :], s_full.at[:, block(b), :], rp_send.at[0, 0], rp_recv.at[b], at(sec, q)
        )

    def cx_copy(k, whose):
        part = pl.ds(pl.multiple_of(whose * rows + k * piece, piece), piece)
        return remote(
            cross_ref.at[0, :, pl.ds(k * piece, piece), :], c2.at[:, part, :], cx_send.at[k], cx_recv.at[k], at(sec, q)
        )

    def ce_copy(d, k):
        b = row_block(k)
        return remote(
            c2.at[:, block(k), :], ce_full.at[:, block(b), :], ce_send.at[d, k], ce_recv.at[b], at(partner, peer(d))
        )

    def ce_arrival(b):
        return remote(
            ce_full.at[:, block(b), :], ce_full.at[:, block(b), :], ce_send.at[0, 0], ce_recv.at[b], at(partner, p)
        )

    def l_copy():
        return remote(line_ref.at[0], l_in, l_send, l_recv, at(partner, p))

    def y_copy(k):
        return remote(y_out.at[:, block(k), :], y_in.at[:, block(k), :], y_send.at[k], y_recv.at[k], at(partner, p))

    def bit(b, s):
        return pl.ds(pl.multiple_of(b * rows + s * piece, piece), piece)

    def xs_copy(k, s):
        return remote(
            xo.at[:, bit(k, s), :], x_full.at[:, bit(row_block(k), s), :], xs_send.at[k, s], x_recv.at[row_block(k), s],
            at(jnp.minimum(sec + 2, n_s - 1), p),
        )

    def xp_copy(d, k, s):
        b = row_block(k)
        return remote(
            x_full.at[:, bit(b, s), :], x_full.at[:, bit(b, s), :], xp_send.at[d, k, s], x_recv.at[b, s],
            at(sec, peer(d)),
        )

    def xe_copy(b, s):
        return remote(
            x_full.at[:, bit(b, s), :], x_full.at[:, bit(b, s), :], xe_send.at[b, s], x_recv.at[b, s], at(partner, p)
        )

    center = pl.ds(PAD, rows)

    def ec_copy(whose):
        return remote(xo.at[:, block(1 - r), :], ext.at[whose, :, center, :], ec_send, ec_recv, at(sec, q))

    def edge(k, side):
        b = row_block(k)
        start = k * rows + (rows - PAD) * side
        to = b - 1 + 2 * side
        exists = to >= 0 if side == 0 else to < n_c
        return pl.ds(pl.multiple_of(start, PAD), PAD), jnp.clip(to, 0, n_c - 1), exists

    def pad_at(side):
        return pl.ds((rows + PAD) * (1 - side), PAD)

    def h_copy(k, side):
        source, to, _ = edge(k, side)
        return remote(
            xo.at[:, source, :], ext.at[r, :, pad_at(side), :], h_send.at[k, side], h_recv.at[r, side], at(sec, to)
        )

    def h_arrival(b, side):
        return remote(
            ext.at[b, :, pad_at(side), :], ext.at[b, :, pad_at(side), :], h_send.at[0, side], h_recv.at[b, side], at(sec, q)
        )

    def nc_copy(k):
        to = row_block(k)
        return remote(
            xo.at[:, block(k), :], ext_next.at[r, :, center, :], nc_send.at[k], nc_recv.at[r], at(above, to)
        )

    def nc_arrival(b):
        return remote(
            ext_next.at[b, :, center, :], ext_next.at[b, :, center, :], nc_send.at[0], nc_recv.at[b], at(below, p)
        )

    def nh_copy(k, side):
        source, to, _ = edge(k, side)
        return remote(
            xo.at[:, source, :], ext_next.at[r, :, pad_at(side), :], nh_send.at[k, side], nh_recv.at[r, side],
            at(above, to),
        )

    def nh_arrival(b, side):
        return remote(
            ext_next.at[b, :, pad_at(side), :], ext_next.at[b, :, pad_at(side), :], nh_send.at[0, side],
            nh_recv.at[b, side], at(below, p),
        )

    def p_copy(way):
        return remote(p_out, p_in.at[way], p_send.at[way], p_recv.at[way], at(below if way == 0 else above, p))

    def times(left, w0, w1):
        one = jnp.dot(left, w0, preferred_element_type=jnp.float32)
        other = jnp.dot(left, w1, preferred_element_type=jnp.float32)
        half = left.shape[0] // 2
        return one[:half] - other[half:], other[:half] + one[half:]

    def stacked(ref, where):
        part = ref[:, where, :]
        return part.reshape(2 * part.shape[1], part.shape[2])

    def product(out, left, right, length):
        tile = min(128, length)

        def some(i, _):
            where = pl.ds(pl.multiple_of(i * tile, tile), tile)
            re, im = times(stacked(left, where), right[0], right[1])
            out[0, where, :] = re.astype(out.dtype)
            out[1, where, :] = im.astype(out.dtype)
            return 0

        lax.fori_loop(0, length // tile, some, 0)

    class First:
        def __init__(self, ref):
            self.ref = ref

        def __getitem__(self, c):
            return self.ref[0, c]

    line = First(line_ref)

    def groups():
        for d in range(1, group):
            for k in range(RHS):
                yield k * group + (h + d) % group

    def put(k):
        @pl.when(hands_on)
        def _():
            for s in range(SUB):
                xs_copy(k, s).start()

        @pl.when(k != r)
        def _():
            ec_copy(r).start()

        for side in range(2):
            @pl.when(edge(k, side)[2])
            def _():
                h_copy(k, side).start()

        @pl.when(jnp.logical_and(odd == 0, sec >= 2))
        def _():
            nc_copy(k).start()
            for side in range(2):
                @pl.when(edge(k, side)[2])
                def _():
                    nh_copy(k, side).start()

    def emit(left, right, base):
        for k in range(RHS):
            re, im = times(stacked(left, pl.ds(k * rows, rows)), right[0], right[1])
            if base:
                re, im = re + y_acc[0, k * rows : (k + 1) * rows, :], im + y_acc[1, k * rows : (k + 1) * rows, :]
            xo[0, k * rows : (k + 1) * rows, :] = re.astype(BF)
            xo[1, k * rows : (k + 1) * rows, :] = im.astype(BF)
            put(k)

    @pl.when(odd == 0)
    def _():
        rx_copy().start()
        for d in range(1, group):
            for k in range(RHS):
                @pl.when(k == r)
                def _():
                    rp_copy(d, k).start()
        for k in range(SUB):
            cx_copy(k, r).start()

        @pl.when(sec >= 2)
        def _():
            l_copy().start()

        rx_arrival().wait_recv()
        for d in range(1, group):
            for k in range(RHS):
                @pl.when(k != r)
                def _():
                    rp_copy(d, k).start()
        cx_copy(0, 1 - r).wait_recv()
        pl.semaphore_signal(go, inc=1, device_id=at(partner, p), device_id_type=MESH)
        for k in range(1, SUB):
            cx_copy(k, 1 - r).wait_recv()
        for b in groups():
            rp_arrival(b).wait_recv()
        product(t_buf, c2, s_full, two)
        for k in range(RHS):
            re, im = times(stacked(t_buf, pl.ds(k * rows, rows)), line[0], line[1])
            here = slice(k * rows, (k + 1) * rows)
            y_acc[0, here, :] = re
            y_acc[1, here, :] = im
            y_out[0, here, :] = re.astype(BF)
            y_out[1, here, :] = im.astype(BF)
            y_copy(k).start()

        @pl.when(first)
        def _():
            for k in range(RHS):
                here = slice(k * rows, (k + 1) * rows)
                for c in range(2):
                    xo[c, here, :] = y_out[c, here, :]
                put(k)

        @pl.when(sec >= 2)
        def _():
            for d in range(group):
                for k in range(RHS):
                    ce_copy(d, k).start()
            for b in range(n_c):
                for s in range(SUB):
                    xe_copy(b, s).wait_recv()
            product(t_buf, c2, x_full, two)
            emit(t_buf, line, True)

    @pl.when(odd == 1)
    def _():
        pl.semaphore_wait(go, 1)
        rx_copy().start()
        for k in range(SUB):
            cx_copy(k, r).start()

        @pl.when(sec >= 2)
        def _():
            l_copy().wait_recv()
            product(l_pair, l_in, line, cols)

        rx_arrival().wait_recv()
        for k in range(RHS):
            y_copy(k).wait_recv()
            for c in range(2):
                mine = s_full[c, block(row_block(k)), :].astype(jnp.float32)
                both = mine + y_in[c, k * rows : (k + 1) * rows, :].astype(jnp.float32)
                s_full[c, block(row_block(k)), :] = both.astype(BF)
            for d in range(1, group):
                rp_copy(d, k).start()
        for k in range(SUB):
            cx_copy(k, 1 - r).wait_recv()
        for b in groups():
            rp_arrival(b).wait_recv()
        product(t_buf, c2, s_full, two)

        @pl.when(first)
        def _():
            emit(t_buf, line, False)

        @pl.when(sec >= 2)
        def _():
            product(y_acc, t_buf, line, two)
            for b in range(n_c):
                ce_arrival(b).wait_recv()
            product(c_pair, c2, ce_full, two)
            for k in range(RHS):
                for s in range(SUB):
                    xe_copy(row_block(k), s).wait_recv()
                    for d in range(1, group):
                        xp_copy(d, k, s).start()
                    xe_copy(row_block(k), s).start()
            for b in groups():
                for s in range(SUB):
                    xe_copy(b, s).wait_recv()
                    xe_copy(b, s).start()
            product(t_buf, c_pair, x_full, two)
            emit(t_buf, l_pair, True)

    for c in range(2):
        ext[r, c, PAD : PAD + rows, :] = xo[c, block(r), :]

    column = lax.broadcasted_iota(jnp.int32, (rows, cols), 1)
    tall = rows + 2 * PAD

    def sideways(v):
        before = jnp.where(column == 0, 0.0, pltpu.roll(v, 1, 1))
        after = jnp.where(column == cols - 1, 0.0, pltpu.roll(v, cols - 1, 1))
        return before + after

    def plane(f):
        here = f[PAD : PAD + rows]
        updown = (pltpu.roll(f, 1, 0) + pltpu.roll(f, tall - 1, 0))[PAD : PAD + rows]
        faces = updown + sideways(here)
        corners = sideways(updown)
        return here, faces, corners

    line_at = lax.broadcasted_iota(jnp.int32, (1, cols), 1)
    distance = jnp.minimum(line_at, cols - 1 - line_at).astype(jnp.float32)
    depth = jnp.full((1, cols), depth_ref[0], jnp.int32).astype(jnp.float32)
    ramp = jnp.maximum(depth - distance, 0.0) / depth
    damping = SIGMA_TOP * ramp * ramp

    ec_copy(1 - r).wait_recv()
    for b in range(RHS):
        @pl.when(p > 0)
        def _():
            h_arrival(b, 1).wait_recv()

        @pl.when(p < n_c - 1)
        def _():
            h_arrival(b, 0).wait_recv()

    for b in range(RHS):
        for c in range(2):
            here, faces, corners = plane(ext[b, c].astype(jnp.float32))
            sol_ref[c, 0, b] = here
            p_out[c, b] = (FACE * here + EDGE * faces + CORNER * corners).astype(BF)
            res_ref[c, 0, b] = rhs_ref[c, 0, b] - CENTER * here + (FACE * faces + EDGE * corners)

    @pl.when(odd == 0)
    def _():
        p_copy(0).start()

    @pl.when(odd == 1)
    def _():
        p_copy(1).start()

        @pl.when(sec < n_s - 1)
        def _():
            p_copy(0).start()

    wave_real = slow_ref[0]
    wave_imag = wave_real * damping
    for b in range(RHS):
        re, im = sol_ref[0, 0, b], sol_ref[1, 0, b]
        res_ref[0, 0, b] += wave_real * re - wave_imag * im
        res_ref[1, 0, b] += wave_real * im + wave_imag * re

    def neighbour(way):
        p_copy(way).wait_recv()
        for b in range(RHS):
            for c in range(2):
                res_ref[c, 0, b] += p_in[way, c, b].astype(jnp.float32)

    @pl.when(sec > 0)
    def _():
        neighbour(0)

    @pl.when(odd == 0)
    def _():
        neighbour(1)

    @pl.when(jnp.logical_and(odd == 1, sec < n_s - 1))
    def _():
        for b in range(RHS):
            nc_arrival(b).wait_recv()

            @pl.when(p > 0)
            def _():
                nh_arrival(b, 1).wait_recv()

            @pl.when(p < n_c - 1)
            def _():
                nh_arrival(b, 0).wait_recv()

            for c in range(2):
                here, faces, corners = plane(ext_next[b, c].astype(jnp.float32))
                res_ref[c, 0, b] += FACE * here + EDGE * faces + CORNER * corners

    rx_copy().wait_send()
    for k in range(SUB):
        cx_copy(k, r).wait_send()
    for d in range(1, group):
        for k in range(RHS):
            rp_copy(d, k).wait_send()
    ec_copy(r).wait_send()
    for k in range(RHS):
        for side in range(2):
            @pl.when(edge(k, side)[2])
            def _():
                h_copy(k, side).wait_send()

    @pl.when(odd == 0)
    def _():
        for k in range(RHS):
            y_copy(k).wait_send()
        p_copy(0).wait_send()

        @pl.when(sec >= 2)
        def _():
            l_copy().wait_send()
            for k in range(RHS):
                for d in range(group):
                    ce_copy(d, k).wait_send()
                nc_copy(k).wait_send()
                for side in range(2):
                    @pl.when(edge(k, side)[2])
                    def _():
                        nh_copy(k, side).wait_send()

    @pl.when(odd == 1)
    def _():
        p_copy(1).wait_send()

        @pl.when(sec < n_s - 1)
        def _():
            p_copy(0).wait_send()

    @pl.when(hands_on)
    def _():
        for k in range(RHS):
            for s in range(SUB):
                xs_copy(k, s).wait_send()

    @pl.when(takes)
    def _():
        for s in range(SUB):
            for k in range(RHS):
                for d in range(1, group):
                    xp_copy(d, k, s).wait_send()
            for b in range(n_c):
                xe_copy(b, s).wait_send()


def per_device(n_s, n_c, rhs_field, slowness, absorb_depth, line_inverse, cross_inverse):
    rows, cols = slowness.shape[1:]
    height = rows * n_c
    group = n_c // RHS
    two = RHS * rows
    tall = rows + 2 * PAD
    vmem = pl.BlockSpec(memory_space=pltpu.VMEM)
    dma = pltpu.SemaphoreType.DMA
    out = jax.ShapeDtypeStruct(rhs_field.shape, jnp.float32)
    return pl.pallas_call(
        functools.partial(kernel, n_s, n_c),
        out_shape=(out, out),
        in_specs=[vmem, vmem, pl.BlockSpec(memory_space=pltpu.SMEM), vmem, vmem],
        out_specs=(vmem, vmem),
        scratch_shapes=[
            pltpu.VMEM((2, rows, cols), BF),
            pltpu.VMEM((2, height, cols), BF),
            pltpu.VMEM((2, two, height), BF),
            pltpu.VMEM((2, height, height), BF),
            pltpu.VMEM((2, cols, cols), BF),
            pltpu.VMEM((2, cols, cols), BF),
            pltpu.VMEM((2, two, height), BF),
            pltpu.VMEM((2, two, cols), BF),
            pltpu.VMEM((2, two, cols), jnp.float32),
            pltpu.VMEM((2, two, cols), BF),
            pltpu.VMEM((2, two, cols), BF),
            pltpu.VMEM((2, height, cols), BF),
            pltpu.VMEM((2, two, cols), BF),
            pltpu.VMEM((RHS, 2, tall, cols), BF),
            pltpu.VMEM((RHS, 2, tall, cols), BF),
            pltpu.VMEM((2, RHS, rows, cols), BF),
            pltpu.VMEM((2, 2, RHS, rows, cols), BF),
            pltpu.SemaphoreType.REGULAR,
            dma, dma,
            dma((group, RHS)), dma((n_c,)),
            dma((SUB,)), dma((SUB,)),
            dma((group, RHS)), dma((n_c,)),
            dma, dma,
            dma((RHS,)), dma((RHS,)),
            dma((RHS, SUB)), dma((group, RHS, SUB)), dma((n_c, SUB)), dma((n_c, SUB)),
            dma, dma,
            dma((RHS, 2)), dma((RHS, 2)),
            dma((RHS,)), dma((RHS,)),
            dma((RHS, 2)), dma((RHS, 2)),
            dma((2,)), dma((2,)),
        ],
        compiler_params=pltpu.CompilerParams(
            collective_id=0, has_side_effects=True, vmem_limit_bytes=56 * 1024 * 1024
        ),
        name="sweep",
    )(rhs_field, slowness, absorb_depth, line_inverse, cross_inverse)


def solution(mesh):
    field = P(None, "sec", None, "cross", None)
    return jax.shard_map(
        functools.partial(per_device, mesh.shape["sec"], mesh.shape["cross"]),
        mesh=mesh,
        in_specs=(
            field,
            P("sec", "cross", None),
            P("sec"),
            P("sec", None, None, None),
            P("sec", None, "cross", None),
        ),
        out_specs=(field, field),
        check_vma=False,
    )
```

```python
import functools

import jax
import jax.numpy as jnp
from jax import lax
from jax.experimental import pallas as pl
from jax.experimental.pallas import tpu as pltpu
from jax.sharding import PartitionSpec as P

MESH = pl.DeviceIdType.MESH
SIGMA_TOP = 2.0
CENTER = 128.0 / 30.0
FACE = 14.0 / 30.0
EDGE = 3.0 / 30.0
CORNER = 1.0 / 30.0
PAD = 16
RHS = 2
SUB = 4
HALVES = 2
BF = jnp.bfloat16


def kernel(
    n_s, n_c,
    rhs_ref, slow_ref, depth_ref, line_ref, cross_ref,
    sol_ref, near_ref,
    r_out, s_full, c2, ce_full, l_in, l_pair, c_pair, t_buf, t_acc, y_acc, y_out, y_in, x_full, xo, ext, ext_next, passing,
    p_out, p_in,
    go, sent, rx_send, rx_recv, rp_send, rp_recv, cx_send, cx_recv, ce_send, ce_recv, l_send, l_recv, y_send, y_recv,
    xs_send, xp_send, xe_send, x_recv, ec_send, ec_recv, h_send, h_recv, nc_send, nc_recv, nr_send, nr_recv, nh_send, nh_recv,
    p_send, p_recv,
):
    rows, cols = rhs_ref.shape[3], rhs_ref.shape[4]
    height = rows * n_c
    group = n_c // RHS
    two = RHS * rows
    piece = rows // SUB
    half_block = rows // HALVES
    sec = lax.axis_index("sec")
    p = lax.axis_index("cross")
    r = p // group
    h = p % group
    q = (p + group) % n_c
    odd = sec % 2
    partner = sec + 1 - 2 * odd
    first = sec < 2
    final = sec >= n_s - 2
    below = jnp.minimum(sec + 1, n_s - 1)
    above = jnp.maximum(sec - 1, 0)

    def at(s, c):
        return {"sec": s, "cross": c}

    def remote(source, target, send, recv, where):
        return pltpu.make_async_remote_copy(
            src_ref=source, dst_ref=target, send_sem=send, recv_sem=recv,
            device_id=where, device_id_type=MESH,
        )

    barrier = pltpu.get_barrier_semaphore()

    def greet(s, c):
        pl.semaphore_signal(barrier, inc=1, device_id=at(s, c), device_id_type=MESH)

    for d in range(1, n_c):
        greet(sec, (p + d) % n_c)
    for d in range(n_c):
        greet(partner, (p + d) % n_c)

    outward = jnp.where(odd == 1, below, above)
    has_outward = jnp.where(odd == 1, sec < n_s - 1, sec > 0)

    @pl.when(has_outward)
    def _():
        for d in range(n_c):
            greet(outward, (p + d) % n_c)

    takes = jnp.logical_and(odd == 1, sec >= 2)
    hands_on = jnp.logical_and(odd == 1, sec <= n_s - 3)

    @pl.when(takes)
    def _():
        greet(sec - 2, p)

    @pl.when(hands_on)
    def _():
        greet(sec + 2, p)

    def block(b):
        return pl.ds(pl.multiple_of(b * rows, rows), rows)

    def row_block(k):
        return k * group + h

    for c in range(2):
        r_out[c] = rhs_ref[c, 0, 1 - r].astype(BF)
        s_full[c, block(p), :] = rhs_ref[c, 0, r].astype(BF)
        c2[c, block(r), :] = cross_ref[0, c]

    zeros_pad = jnp.zeros((PAD, cols), BF)

    @pl.when(p == 0)
    def _():
        for b in range(RHS):
            for c in range(2):
                ext[b, c, 0:PAD, :] = zeros_pad
                ext_next[b, c, 0:PAD, :] = zeros_pad

    @pl.when(p == n_c - 1)
    def _():
        for b in range(RHS):
            for c in range(2):
                ext[b, c, PAD + rows : PAD + rows + PAD, :] = zeros_pad
                ext_next[b, c, PAD + rows : PAD + rows + PAD, :] = zeros_pad

    met = (
        2 * n_c - 1
        + n_c * has_outward.astype(jnp.int32)
        + takes.astype(jnp.int32)
        + hands_on.astype(jnp.int32)
    )
    pl.semaphore_wait(barrier, met)

    def peer(d):
        return r * group + (h + d) % group

    def rx_copy():
        return remote(r_out, s_full.at[:, block(p), :], rx_send, rx_recv, at(sec, q))

    def rx_arrival():
        return remote(r_out, s_full.at[:, block(q), :], rx_send, rx_recv, at(sec, q))

    def rp_copy(d, k):
        b = row_block(k)
        return remote(
            s_full.at[:, block(b), :], s_full.at[:, block(b), :], rp_send.at[d, k], rp_recv.at[b], at(sec, peer(d))
        )

    def rp_arrival(b):
        return remote(
            s_full.at[:, block(b), :], s_full.at[:, block(b), :], rp_send.at[0, 0], rp_recv.at[b], at(sec, q)
        )

    def cx_copy(k, whose):
        part = pl.ds(pl.multiple_of(whose * rows + k * half_block, half_block), half_block)
        return remote(
            cross_ref.at[0, :, pl.ds(k * half_block, half_block), :], c2.at[:, part, :], cx_send.at[k], cx_recv.at[k], at(sec, q)
        )

    def ce_copy(d, k):
        b = row_block(k)
        return remote(
            c2.at[:, block(k), :], ce_full.at[:, block(b), :], ce_send.at[d, k], ce_recv.at[b], at(partner, peer(d))
        )

    def ce_arrival(b):
        return remote(
            ce_full.at[:, block(b), :], ce_full.at[:, block(b), :], ce_send.at[0, 0], ce_recv.at[b], at(partner, p)
        )

    def l_copy():
        return remote(line_ref.at[0], l_in, l_send, l_recv, at(partner, p))

    def y_copy(k):
        return remote(y_out.at[:, block(k), :], y_in.at[:, block(k), :], y_send.at[k], y_recv.at[k], at(partner, p))

    def bit(b, s):
        return pl.ds(pl.multiple_of(b * rows + s * piece, piece), piece)

    def xs_copy(k, s):
        return remote(
            xo.at[:, bit(k, s), :], x_full.at[:, bit(row_block(k), s), :], xs_send.at[k, s], x_recv.at[row_block(k), s],
            at(jnp.minimum(sec + 2, n_s - 1), p),
        )

    def xp_copy(d, k, s):
        b = row_block(k)
        return remote(
            x_full.at[:, bit(b, s), :], x_full.at[:, bit(b, s), :], xp_send.at[d, k, s], x_recv.at[b, s],
            at(sec, peer(d)),
        )

    def xe_copy(b, s):
        return remote(
            x_full.at[:, bit(b, s), :], x_full.at[:, bit(b, s), :], xe_send.at[b, s], x_recv.at[b, s], at(partner, p)
        )

    center = pl.ds(PAD, rows)

    def ec_copy(whose):
        return remote(xo.at[:, block(1 - r), :], ext.at[whose, :, center, :], ec_send, ec_recv, at(sec, q))

    def edge(k, side):
        b = row_block(k)
        start = k * rows + (rows - PAD) * side
        to = b - 1 + 2 * side
        exists = to >= 0 if side == 0 else to < n_c
        return pl.ds(pl.multiple_of(start, PAD), PAD), jnp.clip(to, 0, n_c - 1), exists

    def pad_at(side):
        return pl.ds((rows + PAD) * (1 - side), PAD)

    def h_copy(k, side):
        source, to, _ = edge(k, side)
        return remote(
            xo.at[:, source, :], ext.at[r, :, pad_at(side), :], h_send.at[k, side], h_recv.at[r, side], at(sec, to)
        )

    def h_arrival(b, side):
        return remote(
            ext.at[b, :, pad_at(side), :], ext.at[b, :, pad_at(side), :], h_send.at[0, side], h_recv.at[b, side], at(sec, q)
        )

    def nc_copy():
        return remote(xo.at[:, block(r), :], ext_next.at[r, :, center, :], nc_send.at[0], nc_recv.at[r], at(above, p))

    def np_copy():
        return remote(xo.at[:, block(1 - r), :], passing, nc_send.at[1], nr_recv, at(above, p))

    def nr_copy():
        return remote(passing, ext_next.at[r, :, center, :], nr_send, nc_recv.at[r], at(sec, q))

    def nc_arrival(b):
        return remote(
            ext_next.at[b, :, center, :], ext_next.at[b, :, center, :], nc_send.at[0], nc_recv.at[b], at(below, p)
        )

    def nh_copy(k, side):
        source, to, _ = edge(k, side)
        return remote(
            xo.at[:, source, :], ext_next.at[r, :, pad_at(side), :], nh_send.at[k, side], nh_recv.at[r, side],
            at(above, to),
        )

    def nh_arrival(b, side):
        return remote(
            ext_next.at[b, :, pad_at(side), :], ext_next.at[b, :, pad_at(side), :], nh_send.at[0, side],
            nh_recv.at[b, side], at(below, p),
        )

    def p_copy(way, j, b):
        return remote(
            p_out.at[b], p_in.at[way, b], p_send.at[way, j], p_recv.at[way, b], at(below if way == 0 else above, p)
        )

    def times(left, w0, w1):
        one = jnp.dot(left, w0, preferred_element_type=jnp.float32)
        other = jnp.dot(left, w1, preferred_element_type=jnp.float32)
        half = left.shape[0] // 2
        return one[:half] - other[half:], other[:half] + one[half:]

    def stacked(ref, where):
        part = ref[:, where, :]
        return part.reshape(2 * part.shape[1], part.shape[2])

    def product(out, left, right, length):
        tile = min(128, length)

        def some(i, _):
            where = pl.ds(pl.multiple_of(i * tile, tile), tile)
            re, im = times(stacked(left, where), right[0], right[1])
            out[0, where, :] = re.astype(out.dtype)
            out[1, where, :] = im.astype(out.dtype)
            return 0

        lax.fori_loop(0, length // tile, some, 0)

    class First:
        def __init__(self, ref):
            self.ref = ref

        def __getitem__(self, c):
            return self.ref[0, c]

    line = First(line_ref)
    splits = rows % 128 == 0

    def own_part():
        for i in range(RHS):
            here = pl.ds(i * rows, rows)
            w = [jnp.concatenate([x_full[c, block(row_block(k)), :] for k in range(RHS)], axis=0) for c in range(2)]
            left = jnp.concatenate(
                [jnp.concatenate([c_pair[c, here, block(row_block(k))] for k in range(RHS)], axis=1) for c in range(2)],
                axis=0,
            )
            re, im = times(left, w[0], w[1])
            t_acc[0, here, :] = re
            t_acc[1, here, :] = im

    def peer_part():
        for i in range(RHS):
            here = pl.ds(i * rows, rows)
            re, im = t_acc[0, here, :], t_acc[1, here, :]
            for d in range(1, group):
                at_block = [k * group + (h + d) % group for k in range(RHS)]
                w = [jnp.concatenate([x_full[c, block(b), :] for b in at_block], axis=0) for c in range(2)]
                left = jnp.concatenate(
                    [jnp.concatenate([c_pair[c, here, block(b)] for b in at_block], axis=1) for c in range(2)], axis=0
                )
                more_re, more_im = times(left, w[0], w[1])
                re, im = re + more_re, im + more_im
            t_buf[0, here, :] = re.astype(BF)
            t_buf[1, here, :] = im.astype(BF)

    def groups():
        for d in range(1, group):
            for k in range(RHS):
                yield k * group + (h + d) % group

    def put(k):
        @pl.when(hands_on)
        def _():
            for s in range(SUB):
                xs_copy(k, s).start()

        @pl.when(k != r)
        def _():
            ec_copy(r).start()

        for side in range(2):
            @pl.when(edge(k, side)[2])
            def _():
                h_copy(k, side).start()

    def emit(left, right, base):
        for k in range(RHS):
            re, im = times(stacked(left, pl.ds(k * rows, rows)), right[0], right[1])
            if base:
                re, im = re + y_acc[0, k * rows : (k + 1) * rows, :], im + y_acc[1, k * rows : (k + 1) * rows, :]
            xo[0, k * rows : (k + 1) * rows, :] = re.astype(BF)
            xo[1, k * rows : (k + 1) * rows, :] = im.astype(BF)
            put(k)

    @pl.when(odd == 0)
    def _():
        rx_copy().start()
        for d in range(1, group):
            for k in range(RHS):
                @pl.when(k == r)
                def _():
                    rp_copy(d, k).start()

        @pl.when(sec >= 2)
        def _():
            l_copy().start()

        rx_copy().wait_send()
        for k in range(HALVES):
            cx_copy(k, r).start()
        rx_arrival().wait_recv()
        for d in range(1, group):
            for k in range(RHS):
                @pl.when(k != r)
                def _():
                    rp_copy(d, k).start()
        cx_copy(0, 1 - r).wait_recv()
        pl.semaphore_signal(go, inc=1, device_id=at(partner, p), device_id_type=MESH)
        for k in range(1, HALVES):
            cx_copy(k, 1 - r).wait_recv()
        for b in groups():
            rp_arrival(b).wait_recv()
        product(t_buf, c2, s_full, two)
        for k in range(RHS):
            re, im = times(stacked(t_buf, pl.ds(k * rows, rows)), line[0], line[1])
            here = slice(k * rows, (k + 1) * rows)
            y_acc[0, here, :] = re
            y_acc[1, here, :] = im
            y_out[0, here, :] = re.astype(BF)
            y_out[1, here, :] = im.astype(BF)
            y_copy(k).start()

        @pl.when(first)
        def _():
            for k in range(RHS):
                here = slice(k * rows, (k + 1) * rows)
                for c in range(2):
                    xo[c, here, :] = y_out[c, here, :]
                put(k)

        @pl.when(sec >= 2)
        def _():
            for d in range(group):
                for k in range(RHS):
                    ce_copy(d, k).start()
            for b in range(n_c):
                for s in range(SUB):
                    xe_copy(b, s).wait_recv()
            product(t_buf, c2, x_full, two)
            emit(t_buf, line, True)

            @pl.when(jnp.logical_not(final))
            def _():
                pl.semaphore_wait(sent, 1)

            np_copy().start()
            nc_copy().start()
            for k in range(RHS):
                for side in range(2):
                    @pl.when(edge(k, side)[2])
                    def _():
                        nh_copy(k, side).start()

    @pl.when(odd == 1)
    def _():
        pl.semaphore_wait(go, 1)
        rx_copy().start()
        for k in range(HALVES):
            cx_copy(k, r).start()

        @pl.when(sec >= 2)
        def _():
            l_copy().wait_recv()
            product(l_pair, l_in, line, cols)

        rx_arrival().wait_recv()
        for k in range(RHS):
            y_copy(k).wait_recv()
            for c in range(2):
                mine = s_full[c, block(row_block(k)), :].astype(jnp.float32)
                both = mine + y_in[c, k * rows : (k + 1) * rows, :].astype(jnp.float32)
                s_full[c, block(row_block(k)), :] = both.astype(BF)
            for d in range(1, group):
                rp_copy(d, k).start()
        for k in range(HALVES):
            cx_copy(k, 1 - r).wait_recv()
        for b in groups():
            rp_arrival(b).wait_recv()
        product(t_buf, c2, s_full, two)

        @pl.when(first)
        def _():
            emit(t_buf, line, False)

        @pl.when(sec >= 2)
        def _():
            product(y_acc, t_buf, line, two)
            for b in range(n_c):
                ce_arrival(b).wait_recv()
            product(c_pair, c2, ce_full, two)
            for k in range(RHS):
                for s in range(SUB):
                    xe_copy(row_block(k), s).wait_recv()
                    for d in range(1, group):
                        xp_copy(d, k, s).start()
                    xe_copy(row_block(k), s).start()
            if splits:
                own_part()
            for b in groups():
                for s in range(SUB):
                    xe_copy(b, s).wait_recv()
                    xe_copy(b, s).start()
            if splits:
                peer_part()
            else:
                product(t_buf, c_pair, x_full, two)
            emit(t_buf, l_pair, True)

            @pl.when(hands_on)
            def _():
                for k in range(RHS):
                    for s in range(SUB):
                        xs_copy(k, s).wait_send()
                pl.semaphore_signal(sent, inc=1, device_id=at(partner, p), device_id_type=MESH)

    for c in range(2):
        ext[r, c, PAD : PAD + rows, :] = xo[c, block(r), :]

    column = lax.broadcasted_iota(jnp.int32, (rows, cols), 1)
    tall = rows + 2 * PAD

    def sideways(v):
        before = jnp.where(column == 0, 0.0, pltpu.roll(v, 1, 1))
        after = jnp.where(column == cols - 1, 0.0, pltpu.roll(v, cols - 1, 1))
        return before + after

    def plane(f):
        here = f[PAD : PAD + rows]
        updown = (pltpu.roll(f, 1, 0) + pltpu.roll(f, tall - 1, 0))[PAD : PAD + rows]
        faces = updown + sideways(here)
        corners = sideways(updown)
        return here, faces, corners

    for j in range(2):
        b = r if j == 0 else 1 - r
        if j == 1:
            ec_copy(1 - r).wait_recv()

        @pl.when(p > 0)
        def _():
            h_arrival(b, 1).wait_recv()

        @pl.when(p < n_c - 1)
        def _():
            h_arrival(b, 0).wait_recv()

        for c in range(2):
            here, faces, corners = plane(ext[b, c].astype(jnp.float32))
            sol_ref[c, 0, b] = here.astype(BF)
            p_out[b, c] = (FACE * here + EDGE * faces + CORNER * corners).astype(BF)
            near_ref[c, 0, b] = FACE * faces + EDGE * corners - CENTER * here

        @pl.when(odd == 0)
        def _():
            p_copy(0, j, b).start()

        @pl.when(odd == 1)
        def _():
            p_copy(1, j, b).start()

            @pl.when(sec < n_s - 1)
            def _():
                p_copy(0, j, b).start()

    line_at = lax.broadcasted_iota(jnp.int32, (1, cols), 1)
    distance = jnp.minimum(line_at, cols - 1 - line_at).astype(jnp.float32)
    depth = jnp.full((1, cols), depth_ref[0], jnp.int32).astype(jnp.float32)
    ramp = jnp.maximum(depth - distance, 0.0) / depth
    damping = SIGMA_TOP * ramp * ramp
    wave_real = slow_ref[0]
    wave_imag = wave_real * damping
    for b in range(RHS):
        re, im = (ext[b, c, PAD : PAD + rows, :].astype(jnp.float32) for c in range(2))
        near_ref[0, 0, b] += wave_real * re - wave_imag * im
        near_ref[1, 0, b] += wave_real * im + wave_imag * re

    def neighbour(way):
        for j in range(2):
            b = r if j == 0 else 1 - r
            p_copy(way, j, b).wait_recv()
            for c in range(2):
                near_ref[c, 0, b] += p_in[way, b, c].astype(jnp.float32)

    @pl.when(sec > 0)
    def _():
        neighbour(0)

    @pl.when(odd == 0)
    def _():
        neighbour(1)

    @pl.when(jnp.logical_and(odd == 1, sec < n_s - 1))
    def _():
        np_copy().wait_recv()
        nr_copy().start()
        for j in range(2):
            b = r if j == 0 else 1 - r
            nc_arrival(b).wait_recv()

            @pl.when(p > 0)
            def _():
                nh_arrival(b, 1).wait_recv()

            @pl.when(p < n_c - 1)
            def _():
                nh_arrival(b, 0).wait_recv()

            for c in range(2):
                here, faces, corners = plane(ext_next[b, c].astype(jnp.float32))
                near_ref[c, 0, b] += FACE * here + EDGE * faces + CORNER * corners

        nr_copy().wait_send()

    @pl.when(odd == 1)
    def _():
        rx_copy().wait_send()

    for k in range(HALVES):
        cx_copy(k, r).wait_send()
    for d in range(1, group):
        for k in range(RHS):
            rp_copy(d, k).wait_send()
    ec_copy(r).wait_send()
    for k in range(RHS):
        for side in range(2):
            @pl.when(edge(k, side)[2])
            def _():
                h_copy(k, side).wait_send()

    @pl.when(odd == 0)
    def _():
        for k in range(RHS):
            y_copy(k).wait_send()
        for j in range(2):
            p_copy(0, j, r).wait_send()

        @pl.when(sec >= 2)
        def _():
            l_copy().wait_send()
            nc_copy().wait_send()
            np_copy().wait_send()
            for k in range(RHS):
                for d in range(group):
                    ce_copy(d, k).wait_send()
                for side in range(2):
                    @pl.when(edge(k, side)[2])
                    def _():
                        nh_copy(k, side).wait_send()

    @pl.when(odd == 1)
    def _():
        for j in range(2):
            p_copy(1, j, r).wait_send()

        @pl.when(sec < n_s - 1)
        def _():
            for j in range(2):
                p_copy(0, j, r).wait_send()

    @pl.when(jnp.logical_and(hands_on, first))
    def _():
        for k in range(RHS):
            for s in range(SUB):
                xs_copy(k, s).wait_send()

    @pl.when(takes)
    def _():
        for s in range(SUB):
            for k in range(RHS):
                for d in range(1, group):
                    xp_copy(d, k, s).wait_send()
            for b in range(n_c):
                xe_copy(b, s).wait_send()


def per_device(n_s, n_c, rhs_field, slowness, absorb_depth, line_inverse, cross_inverse):
    rows, cols = slowness.shape[1:]
    height = rows * n_c
    group = n_c // RHS
    two = RHS * rows
    tall = rows + 2 * PAD
    vmem = pl.BlockSpec(memory_space=pltpu.VMEM)
    dma = pltpu.SemaphoreType.DMA
    field, near = pl.pallas_call(
        functools.partial(kernel, n_s, n_c),
        out_shape=(
            jax.ShapeDtypeStruct(rhs_field.shape, BF),
            jax.ShapeDtypeStruct(rhs_field.shape, jnp.float32),
        ),
        in_specs=[vmem, vmem, pl.BlockSpec(memory_space=pltpu.SMEM), vmem, vmem],
        out_specs=(vmem, vmem),
        scratch_shapes=[
            pltpu.VMEM((2, rows, cols), BF),
            pltpu.VMEM((2, height, cols), BF),
            pltpu.VMEM((2, two, height), BF),
            pltpu.VMEM((2, height, height), BF),
            pltpu.VMEM((2, cols, cols), BF),
            pltpu.VMEM((2, cols, cols), BF),
            pltpu.VMEM((2, two, height), BF),
            pltpu.VMEM((2, two, cols), BF),
            pltpu.VMEM((2, two, cols), jnp.float32),
            pltpu.VMEM((2, two, cols), jnp.float32),
            pltpu.VMEM((2, two, cols), BF),
            pltpu.VMEM((2, two, cols), BF),
            pltpu.VMEM((2, height, cols), BF),
            pltpu.VMEM((2, two, cols), BF),
            pltpu.VMEM((RHS, 2, tall, cols), BF),
            pltpu.VMEM((RHS, 2, tall, cols), BF),
            pltpu.VMEM((2, rows, cols), BF),
            pltpu.VMEM((RHS, 2, rows, cols), BF),
            pltpu.VMEM((2, RHS, 2, rows, cols), BF),
            pltpu.SemaphoreType.REGULAR, pltpu.SemaphoreType.REGULAR,
            dma, dma,
            dma((group, RHS)), dma((n_c,)),
            dma((HALVES,)), dma((HALVES,)),
            dma((group, RHS)), dma((n_c,)),
            dma, dma,
            dma((RHS,)), dma((RHS,)),
            dma((RHS, SUB)), dma((group, RHS, SUB)), dma((n_c, SUB)), dma((n_c, SUB)),
            dma, dma,
            dma((RHS, 2)), dma((RHS, 2)),
            dma((2,)), dma((RHS,)), dma, dma,
            dma((RHS, 2)), dma((RHS, 2)),
            dma((2, 2)), dma((2, RHS)),
        ],
        compiler_params=pltpu.CompilerParams(
            collective_id=0, has_side_effects=True, vmem_limit_bytes=56 * 1024 * 1024
        ),
        name="sweep",
    )(rhs_field, slowness, absorb_depth, line_inverse, cross_inverse)
    return field.astype(jnp.float32), rhs_field + near


def solution(mesh):
    field = P(None, "sec", None, "cross", None)
    return jax.shard_map(
        functools.partial(per_device, mesh.shape["sec"], mesh.shape["cross"]),
        mesh=mesh,
        in_specs=(
            field,
            P("sec", "cross", None),
            P("sec"),
            P("sec", None, None, None),
            P("sec", None, "cross", None),
        ),
        out_specs=(field, field),
        check_vma=False,
    )
```

```python
import functools

import jax
import jax.numpy as jnp
from jax import lax
from jax.experimental import pallas as pl
from jax.experimental.pallas import tpu as pltpu
from jax.sharding import PartitionSpec as P

MESH = pl.DeviceIdType.MESH
SIGMA_TOP = 2.0
CENTER = 128.0 / 30.0
FACE = 14.0 / 30.0
EDGE = 3.0 / 30.0
CORNER = 1.0 / 30.0
PAD = 16
RHS = 2
SUB = 4
HALVES = 2
BF = jnp.bfloat16


def kernel(
    n_s, n_c,
    rhs_ref, slow_ref, depth_ref, line_ref, cross_ref,
    sol_ref, near_ref,
    r_out, s_full, c2, ce_full, l_in, l_pair, c_pair, t_buf, t_acc, y_acc, y_out, y_in, x_low, x_far, cl_full, ll_full, l_quad, c_quad, xo, ext, ext_next, passing,
    p_out, p_in,
    go, sent, rx_send, rx_recv, rp_send, rp_recv, cx_send, cx_recv, ce_send, ce_recv, l_send, l_recv, y_send, y_recv,
    ls_send, le_send, ls_recv, xs_send, xf_send, xp_send, xe_send, x_recv, ec_send, ec_recv, h_send, h_recv, nc_send, nc_recv, nr_send, nr_recv, nh_send, nh_recv,
    p_send, p_recv,
):
    rows, cols = rhs_ref.shape[3], rhs_ref.shape[4]
    height = rows * n_c
    group = n_c // RHS
    two = RHS * rows
    piece = rows // SUB
    half_block = rows // HALVES
    sec = lax.axis_index("sec")
    p = lax.axis_index("cross")
    r = p // group
    h = p % group
    q = (p + group) % n_c
    odd = sec % 2
    partner = sec + 1 - 2 * odd
    spot = sec % 4
    upper = spot >= 2
    first = sec < 2
    begin = sec < 4
    final = sec >= n_s - 2
    below = jnp.minimum(sec + 1, n_s - 1)
    above = jnp.maximum(sec - 1, 0)

    def at(s, c):
        return {"sec": s, "cross": c}

    def remote(source, target, send, recv, where):
        return pltpu.make_async_remote_copy(
            src_ref=source, dst_ref=target, send_sem=send, recv_sem=recv,
            device_id=where, device_id_type=MESH,
        )

    barrier = pltpu.get_barrier_semaphore()

    def greet(s, c):
        pl.semaphore_signal(barrier, inc=1, device_id=at(s, c), device_id_type=MESH)

    for d in range(1, n_c):
        greet(sec, (p + d) % n_c)
    for d in range(n_c):
        greet(partner, (p + d) % n_c)

    outward = jnp.where(odd == 1, below, above)
    has_outward = jnp.where(odd == 1, sec < n_s - 1, sec > 0)

    @pl.when(has_outward)
    def _():
        for d in range(n_c):
            greet(outward, (p + d) % n_c)

    tops = spot == 3
    links = (
        (-2, jnp.logical_and(odd == 1, sec >= 2)),
        (2, jnp.logical_and(odd == 1, sec <= n_s - 3)),
        (-4, jnp.logical_and(tops, sec >= 4)),
        (4, jnp.logical_and(tops, sec <= n_s - 5)),
    )
    for way, there in links:
        @pl.when(there)
        def _():
            greet(sec + way, p)

    hands_on = jnp.logical_and(tops, sec <= n_s - 3)

    def block(b):
        return pl.ds(pl.multiple_of(b * rows, rows), rows)

    def row_block(k):
        return k * group + h

    for c in range(2):
        r_out[c] = rhs_ref[c, 0, 1 - r].astype(BF)
        s_full[c, block(p), :] = rhs_ref[c, 0, r].astype(BF)
        c2[c, block(r), :] = cross_ref[0, c]

    zeros_pad = jnp.zeros((PAD, cols), BF)

    @pl.when(p == 0)
    def _():
        for b in range(RHS):
            for c in range(2):
                ext[b, c, 0:PAD, :] = zeros_pad
                ext_next[b, c, 0:PAD, :] = zeros_pad

    @pl.when(p == n_c - 1)
    def _():
        for b in range(RHS):
            for c in range(2):
                ext[b, c, PAD + rows : PAD + rows + PAD, :] = zeros_pad
                ext_next[b, c, PAD + rows : PAD + rows + PAD, :] = zeros_pad

    met = (
        2 * n_c - 1
        + n_c * has_outward.astype(jnp.int32)
        + sum(there.astype(jnp.int32) for _, there in links)
    )
    pl.semaphore_wait(barrier, met)

    def peer(d):
        return r * group + (h + d) % group

    def rx_copy():
        return remote(r_out, s_full.at[:, block(p), :], rx_send, rx_recv, at(sec, q))

    def rx_arrival():
        return remote(r_out, s_full.at[:, block(q), :], rx_send, rx_recv, at(sec, q))

    def rp_copy(d, k):
        b = row_block(k)
        return remote(
            s_full.at[:, block(b), :], s_full.at[:, block(b), :], rp_send.at[d, k], rp_recv.at[b], at(sec, peer(d))
        )

    def rp_arrival(b):
        return remote(
            s_full.at[:, block(b), :], s_full.at[:, block(b), :], rp_send.at[0, 0], rp_recv.at[b], at(sec, q)
        )

    def cx_copy(k, whose):
        part = pl.ds(pl.multiple_of(whose * rows + k * half_block, half_block), half_block)
        return remote(
            cross_ref.at[0, :, pl.ds(k * half_block, half_block), :], c2.at[:, part, :], cx_send.at[k], cx_recv.at[k], at(sec, q)
        )

    def ce_copy(d, k):
        b = row_block(k)
        return remote(
            c2.at[:, block(k), :], ce_full.at[:, block(b), :], ce_send.at[d, k], ce_recv.at[b], at(partner, peer(d))
        )

    def ce_arrival(b):
        return remote(
            ce_full.at[:, block(b), :], ce_full.at[:, block(b), :], ce_send.at[0, 0], ce_recv.at[b], at(partner, p)
        )

    def l_copy():
        return remote(line_ref.at[0], l_in, l_send, l_recv, at(partner, p))

    def y_copy(k):
        return remote(y_out.at[:, block(k), :], y_in.at[:, block(k), :], y_send.at[k], y_recv.at[k], at(partner, p))

    def bit(b, s):
        return pl.ds(pl.multiple_of(b * rows + s * piece, piece), piece)

    spread_into = (x_low, x_far, cl_full)
    LOW, FAR, MIX = range(3)

    def xs_copy(a, k, s):
        source = (y_out, xo, c_pair)[a]
        b = row_block(k)
        return remote(
            source.at[:, bit(k, s), :], spread_into[a].at[:, bit(b, s), :], xs_send.at[a, k, s], x_recv.at[a, b, s],
            at(jnp.minimum(sec + 2, n_s - 1), p),
        )

    def xf_copy(k, s):
        b = row_block(k)
        return remote(
            xo.at[:, bit(k, s), :], x_far.at[:, bit(b, s), :], xf_send.at[k, s], x_recv.at[FAR, b, s],
            at(jnp.minimum(sec + 4, n_s - 1), p),
        )

    def xp_copy(a, d, k, s):
        b = row_block(k)
        here = spread_into[a].at[:, bit(b, s), :]
        return remote(here, here, xp_send.at[a, d, k, s], x_recv.at[a, b, s], at(sec, peer(d)))

    def xe_copy(a, b, s):
        here = spread_into[a].at[:, bit(b, s), :]
        return remote(here, here, xe_send.at[a, b, s], x_recv.at[a, b, s], at(partner, p))

    def ls_copy():
        return remote(l_pair, ll_full, ls_send, ls_recv, at(jnp.minimum(sec + 2, n_s - 1), p))

    def le_copy():
        return remote(ll_full, ll_full, le_send, ls_recv, at(partner, p))

    center = pl.ds(PAD, rows)

    def ec_copy(whose):
        return remote(xo.at[:, block(1 - r), :], ext.at[whose, :, center, :], ec_send, ec_recv, at(sec, q))

    def edge(k, side):
        b = row_block(k)
        start = k * rows + (rows - PAD) * side
        to = b - 1 + 2 * side
        exists = to >= 0 if side == 0 else to < n_c
        return pl.ds(pl.multiple_of(start, PAD), PAD), jnp.clip(to, 0, n_c - 1), exists

    def pad_at(side):
        return pl.ds((rows + PAD) * (1 - side), PAD)

    def h_copy(k, side):
        source, to, _ = edge(k, side)
        return remote(
            xo.at[:, source, :], ext.at[r, :, pad_at(side), :], h_send.at[k, side], h_recv.at[r, side], at(sec, to)
        )

    def h_arrival(b, side):
        return remote(
            ext.at[b, :, pad_at(side), :], ext.at[b, :, pad_at(side), :], h_send.at[0, side], h_recv.at[b, side], at(sec, q)
        )

    def nc_copy():
        return remote(xo.at[:, block(r), :], ext_next.at[r, :, center, :], nc_send.at[0], nc_recv.at[r], at(above, p))

    def np_copy():
        return remote(xo.at[:, block(1 - r), :], passing, nc_send.at[1], nr_recv, at(above, p))

    def nr_copy():
        return remote(passing, ext_next.at[r, :, center, :], nr_send, nc_recv.at[r], at(sec, q))

    def nc_arrival(b):
        return remote(
            ext_next.at[b, :, center, :], ext_next.at[b, :, center, :], nc_send.at[0], nc_recv.at[b], at(below, p)
        )

    def nh_copy(k, side):
        source, to, _ = edge(k, side)
        return remote(
            xo.at[:, source, :], ext_next.at[r, :, pad_at(side), :], nh_send.at[k, side], nh_recv.at[r, side],
            at(above, to),
        )

    def nh_arrival(b, side):
        return remote(
            ext_next.at[b, :, pad_at(side), :], ext_next.at[b, :, pad_at(side), :], nh_send.at[0, side],
            nh_recv.at[b, side], at(below, p),
        )

    def p_copy(way, j, b):
        return remote(
            p_out.at[b], p_in.at[way, b], p_send.at[way, j], p_recv.at[way, b], at(below if way == 0 else above, p)
        )

    def times(left, w0, w1):
        one = jnp.dot(left, w0, preferred_element_type=jnp.float32)
        other = jnp.dot(left, w1, preferred_element_type=jnp.float32)
        half = left.shape[0] // 2
        return one[:half] - other[half:], other[:half] + one[half:]

    def stacked(ref, where):
        part = ref[:, where, :]
        return part.reshape(2 * part.shape[1], part.shape[2])

    def product(out, left, right, length):
        tile = min(128, length)

        def some(i, _):
            where = pl.ds(pl.multiple_of(i * tile, tile), tile)
            re, im = times(stacked(left, where), right[0], right[1])
            out[0, where, :] = re.astype(out.dtype)
            out[1, where, :] = im.astype(out.dtype)
            return 0

        lax.fori_loop(0, length // tile, some, 0)

    class First:
        def __init__(self, ref):
            self.ref = ref

        def __getitem__(self, c):
            return self.ref[0, c]

    line = First(line_ref)
    splits = rows % 128 == 0

    def arrive(a):
        for k in range(RHS):
            for s in range(SUB):
                xe_copy(a, row_block(k), s).wait_recv()
                for d in range(1, group):
                    xp_copy(a, d, k, s).start()
                xe_copy(a, row_block(k), s).start()

    def arrive_peers(a):
        for b in groups():
            for s in range(SUB):
                xe_copy(a, b, s).wait_recv()
                xe_copy(a, b, s).start()

    def arrive_even(a):
        for b in range(n_c):
            for s in range(SUB):
                xe_copy(a, b, s).wait_recv()

    def add_on(left, right):
        for k in range(RHS):
            here = slice(k * rows, (k + 1) * rows)
            re, im = times(stacked(left, pl.ds(k * rows, rows)), right[0], right[1])
            y_acc[0, here, :] += re
            y_acc[1, here, :] += im

    def gather_product(a, mat):
        arrive(a)
        if splits:
            own_part(mat, spread_into[a])
        arrive_peers(a)
        if splits:
            peer_part(mat, spread_into[a])
        else:
            product(t_buf, mat, spread_into[a], two)

    def own_part(mat, x_full):
        for i in range(RHS):
            here = pl.ds(i * rows, rows)
            w = [jnp.concatenate([x_full[c, block(row_block(k)), :] for k in range(RHS)], axis=0) for c in range(2)]
            left = jnp.concatenate(
                [jnp.concatenate([mat[c, here, block(row_block(k))] for k in range(RHS)], axis=1) for c in range(2)],
                axis=0,
            )
            re, im = times(left, w[0], w[1])
            t_acc[0, here, :] = re
            t_acc[1, here, :] = im

    def peer_part(mat, x_full):
        for i in range(RHS):
            here = pl.ds(i * rows, rows)
            re, im = t_acc[0, here, :], t_acc[1, here, :]
            for d in range(1, group):
                at_block = [k * group + (h + d) % group for k in range(RHS)]
                w = [jnp.concatenate([x_full[c, block(b), :] for b in at_block], axis=0) for c in range(2)]
                left = jnp.concatenate(
                    [jnp.concatenate([mat[c, here, block(b)] for b in at_block], axis=1) for c in range(2)], axis=0
                )
                more_re, more_im = times(left, w[0], w[1])
                re, im = re + more_re, im + more_im
            t_buf[0, here, :] = re.astype(BF)
            t_buf[1, here, :] = im.astype(BF)

    def groups():
        for d in range(1, group):
            for k in range(RHS):
                yield k * group + (h + d) % group

    def put(k):
        @pl.when(hands_on)
        def _():
            for s in range(SUB):
                xf_copy(k, s).start()
                xs_copy(FAR, k, s).start()

        @pl.when(k != r)
        def _():
            ec_copy(r).start()

        for side in range(2):
            @pl.when(edge(k, side)[2])
            def _():
                h_copy(k, side).start()

    def emit(left, right, base):
        for k in range(RHS):
            re, im = times(stacked(left, pl.ds(k * rows, rows)), right[0], right[1])
            if base:
                re, im = re + y_acc[0, k * rows : (k + 1) * rows, :], im + y_acc[1, k * rows : (k + 1) * rows, :]
            xo[0, k * rows : (k + 1) * rows, :] = re.astype(BF)
            xo[1, k * rows : (k + 1) * rows, :] = im.astype(BF)
            put(k)

    @pl.when(odd == 0)
    def _():
        rx_copy().start()
        for d in range(1, group):
            for k in range(RHS):
                @pl.when(k == r)
                def _():
                    rp_copy(d, k).start()

        @pl.when(sec >= 2)
        def _():
            l_copy().start()

        rx_copy().wait_send()
        for k in range(HALVES):
            cx_copy(k, r).start()
        rx_arrival().wait_recv()
        for d in range(1, group):
            for k in range(RHS):
                @pl.when(k != r)
                def _():
                    rp_copy(d, k).start()
        cx_copy(0, 1 - r).wait_recv()
        pl.semaphore_signal(go, inc=1, device_id=at(partner, p), device_id_type=MESH)
        for k in range(1, HALVES):
            cx_copy(k, 1 - r).wait_recv()
        for b in groups():
            rp_arrival(b).wait_recv()
        product(t_buf, c2, s_full, two)
        for k in range(RHS):
            re, im = times(stacked(t_buf, pl.ds(k * rows, rows)), line[0], line[1])
            here = slice(k * rows, (k + 1) * rows)
            y_acc[0, here, :] = re
            y_acc[1, here, :] = im
            y_out[0, here, :] = re.astype(BF)
            y_out[1, here, :] = im.astype(BF)
            y_copy(k).start()

        @pl.when(first)
        def _():
            for k in range(RHS):
                here = slice(k * rows, (k + 1) * rows)
                for c in range(2):
                    xo[c, here, :] = y_out[c, here, :]
                put(k)

        @pl.when(sec >= 2)
        def _():
            for d in range(group):
                for k in range(RHS):
                    ce_copy(d, k).start()

            @pl.when(upper)
            def _():
                arrive_even(LOW)
                product(t_buf, c2, x_low, two)

                @pl.when(begin)
                def _():
                    emit(t_buf, line, True)

                @pl.when(jnp.logical_not(begin))
                def _():
                    add_on(t_buf, line)
                    le_copy().wait_recv()
                    product(l_quad, ll_full, line, cols)
                    arrive_even(MIX)
                    product(c_quad, c2, cl_full, two)
                    arrive_even(FAR)
                    product(t_buf, c_quad, x_far, two)
                    emit(t_buf, l_quad, True)

            @pl.when(jnp.logical_not(upper))
            def _():
                arrive_even(FAR)
                product(t_buf, c2, x_far, two)
                emit(t_buf, line, True)

            @pl.when(jnp.logical_and(upper, jnp.logical_not(final)))
            def _():
                pl.semaphore_wait(sent, 1)

            np_copy().start()
            nc_copy().start()
            for k in range(RHS):
                for side in range(2):
                    @pl.when(edge(k, side)[2])
                    def _():
                        nh_copy(k, side).start()

    @pl.when(odd == 1)
    def _():
        pl.semaphore_wait(go, 1)
        rx_copy().start()
        for k in range(HALVES):
            cx_copy(k, r).start()

        @pl.when(sec >= 2)
        def _():
            l_copy().wait_recv()
            product(l_pair, l_in, line, cols)

            @pl.when(spot == 1)
            def _():
                ls_copy().start()

        rx_arrival().wait_recv()
        for k in range(RHS):
            y_copy(k).wait_recv()
            for c in range(2):
                mine = s_full[c, block(row_block(k)), :].astype(jnp.float32)
                both = mine + y_in[c, k * rows : (k + 1) * rows, :].astype(jnp.float32)
                s_full[c, block(row_block(k)), :] = both.astype(BF)
            for d in range(1, group):
                rp_copy(d, k).start()
        for k in range(HALVES):
            cx_copy(k, 1 - r).wait_recv()
        for b in groups():
            rp_arrival(b).wait_recv()
        product(t_buf, c2, s_full, two)

        @pl.when(spot == 1)
        def _():
            for k in range(RHS):
                re, im = times(stacked(t_buf, pl.ds(k * rows, rows)), line[0], line[1])
                here = slice(k * rows, (k + 1) * rows)
                y_acc[0, here, :] = re
                y_acc[1, here, :] = im
                y_out[0, here, :] = re.astype(BF)
                y_out[1, here, :] = im.astype(BF)
                for s in range(SUB):
                    xs_copy(LOW, k, s).start()

                @pl.when(first)
                def _():
                    for c in range(2):
                        xo[c, here, :] = y_out[c, here, :]
                    put(k)

        @pl.when(tops)
        def _():
            product(y_acc, t_buf, line, two)

        @pl.when(sec >= 2)
        def _():
            for b in range(n_c):
                ce_arrival(b).wait_recv()
            product(c_pair, c2, ce_full, two)

            @pl.when(spot == 1)
            def _():
                for k in range(RHS):
                    for s in range(SUB):
                        xs_copy(MIX, k, s).start()
                gather_product(FAR, c_pair)
                emit(t_buf, l_pair, True)

            @pl.when(tops)
            def _():
                @pl.when(jnp.logical_not(begin))
                def _():
                    ls_copy().wait_recv()
                    le_copy().start()
                    product(l_quad, ll_full, l_pair, cols)

                gather_product(LOW, c_pair)

                @pl.when(begin)
                def _():
                    emit(t_buf, l_pair, True)

                @pl.when(jnp.logical_not(begin))
                def _():
                    add_on(t_buf, l_pair)
                    arrive(MIX)
                    arrive_peers(MIX)
                    product(c_quad, c_pair, cl_full, two)
                    gather_product(FAR, c_quad)
                    emit(t_buf, l_quad, True)

                @pl.when(hands_on)
                def _():
                    for k in range(RHS):
                        for s in range(SUB):
                            xf_copy(k, s).wait_send()
                            xs_copy(FAR, k, s).wait_send()
                    pl.semaphore_signal(sent, inc=1, device_id=at(partner, p), device_id_type=MESH)

    for c in range(2):
        ext[r, c, PAD : PAD + rows, :] = xo[c, block(r), :]

    column = lax.broadcasted_iota(jnp.int32, (rows, cols), 1)
    tall = rows + 2 * PAD

    def sideways(v):
        before = jnp.where(column == 0, 0.0, pltpu.roll(v, 1, 1))
        after = jnp.where(column == cols - 1, 0.0, pltpu.roll(v, cols - 1, 1))
        return before + after

    def plane(f):
        here = f[PAD : PAD + rows]
        updown = (pltpu.roll(f, 1, 0) + pltpu.roll(f, tall - 1, 0))[PAD : PAD + rows]
        faces = updown + sideways(here)
        corners = sideways(updown)
        return here, faces, corners

    for j in range(2):
        b = r if j == 0 else 1 - r
        if j == 1:
            ec_copy(1 - r).wait_recv()

        @pl.when(p > 0)
        def _():
            h_arrival(b, 1).wait_recv()

        @pl.when(p < n_c - 1)
        def _():
            h_arrival(b, 0).wait_recv()

        for c in range(2):
            here, faces, corners = plane(ext[b, c].astype(jnp.float32))
            sol_ref[c, 0, b] = here.astype(BF)
            p_out[b, c] = (FACE * here + EDGE * faces + CORNER * corners).astype(BF)
            near_ref[c, 0, b] = FACE * faces + EDGE * corners - CENTER * here

        @pl.when(odd == 0)
        def _():
            p_copy(0, j, b).start()

        @pl.when(odd == 1)
        def _():
            p_copy(1, j, b).start()

            @pl.when(sec < n_s - 1)
            def _():
                p_copy(0, j, b).start()

    line_at = lax.broadcasted_iota(jnp.int32, (1, cols), 1)
    distance = jnp.minimum(line_at, cols - 1 - line_at).astype(jnp.float32)
    depth = jnp.full((1, cols), depth_ref[0], jnp.int32).astype(jnp.float32)
    ramp = jnp.maximum(depth - distance, 0.0) / depth
    damping = SIGMA_TOP * ramp * ramp
    wave_real = slow_ref[0]
    wave_imag = wave_real * damping
    for b in range(RHS):
        re, im = (ext[b, c, PAD : PAD + rows, :].astype(jnp.float32) for c in range(2))
        near_ref[0, 0, b] += wave_real * re - wave_imag * im
        near_ref[1, 0, b] += wave_real * im + wave_imag * re

    def neighbour(way):
        for j in range(2):
            b = r if j == 0 else 1 - r
            p_copy(way, j, b).wait_recv()
            for c in range(2):
                near_ref[c, 0, b] += p_in[way, b, c].astype(jnp.float32)

    @pl.when(sec > 0)
    def _():
        neighbour(0)

    @pl.when(odd == 0)
    def _():
        neighbour(1)

    @pl.when(jnp.logical_and(odd == 1, sec < n_s - 1))
    def _():
        np_copy().wait_recv()
        nr_copy().start()
        for j in range(2):
            b = r if j == 0 else 1 - r
            nc_arrival(b).wait_recv()

            @pl.when(p > 0)
            def _():
                nh_arrival(b, 1).wait_recv()

            @pl.when(p < n_c - 1)
            def _():
                nh_arrival(b, 0).wait_recv()

            for c in range(2):
                here, faces, corners = plane(ext_next[b, c].astype(jnp.float32))
                near_ref[c, 0, b] += FACE * here + EDGE * faces + CORNER * corners

        nr_copy().wait_send()

    @pl.when(odd == 1)
    def _():
        rx_copy().wait_send()

    for k in range(HALVES):
        cx_copy(k, r).wait_send()
    for d in range(1, group):
        for k in range(RHS):
            rp_copy(d, k).wait_send()
    ec_copy(r).wait_send()
    for k in range(RHS):
        for side in range(2):
            @pl.when(edge(k, side)[2])
            def _():
                h_copy(k, side).wait_send()

    @pl.when(odd == 0)
    def _():
        for k in range(RHS):
            y_copy(k).wait_send()
        for j in range(2):
            p_copy(0, j, r).wait_send()

        @pl.when(sec >= 2)
        def _():
            l_copy().wait_send()
            nc_copy().wait_send()
            np_copy().wait_send()
            for k in range(RHS):
                for d in range(group):
                    ce_copy(d, k).wait_send()
                for side in range(2):
                    @pl.when(edge(k, side)[2])
                    def _():
                        nh_copy(k, side).wait_send()

    @pl.when(odd == 1)
    def _():
        for j in range(2):
            p_copy(1, j, r).wait_send()

        @pl.when(sec < n_s - 1)
        def _():
            for j in range(2):
                p_copy(0, j, r).wait_send()

    def spread_sent(a):
        for s in range(SUB):
            for k in range(RHS):
                for d in range(1, group):
                    xp_copy(a, d, k, s).wait_send()
            for b in range(n_c):
                xe_copy(a, b, s).wait_send()

    def passed_on(a):
        for k in range(RHS):
            for s in range(SUB):
                xs_copy(a, k, s).wait_send()

    @pl.when(spot == 1)
    def _():
        passed_on(LOW)

        @pl.when(sec >= 2)
        def _():
            ls_copy().wait_send()
            passed_on(MIX)
            spread_sent(FAR)

    @pl.when(tops)
    def _():
        spread_sent(LOW)

        @pl.when(jnp.logical_not(begin))
        def _():
            le_copy().wait_send()
            spread_sent(MIX)
            spread_sent(FAR)


def per_device(n_s, n_c, rhs_field, slowness, absorb_depth, line_inverse, cross_inverse):
    rows, cols = slowness.shape[1:]
    height = rows * n_c
    group = n_c // RHS
    two = RHS * rows
    tall = rows + 2 * PAD
    vmem = pl.BlockSpec(memory_space=pltpu.VMEM)
    dma = pltpu.SemaphoreType.DMA
    field, near = pl.pallas_call(
        functools.partial(kernel, n_s, n_c),
        out_shape=(
            jax.ShapeDtypeStruct(rhs_field.shape, BF),
            jax.ShapeDtypeStruct(rhs_field.shape, jnp.float32),
        ),
        in_specs=[vmem, vmem, pl.BlockSpec(memory_space=pltpu.SMEM), vmem, vmem],
        out_specs=(vmem, vmem),
        scratch_shapes=[
            pltpu.VMEM((2, rows, cols), BF),
            pltpu.VMEM((2, height, cols), BF),
            pltpu.VMEM((2, two, height), BF),
            pltpu.VMEM((2, height, height), BF),
            pltpu.VMEM((2, cols, cols), BF),
            pltpu.VMEM((2, cols, cols), BF),
            pltpu.VMEM((2, two, height), BF),
            pltpu.VMEM((2, two, cols), BF),
            pltpu.VMEM((2, two, cols), jnp.float32),
            pltpu.VMEM((2, two, cols), jnp.float32),
            pltpu.VMEM((2, two, cols), BF),
            pltpu.VMEM((2, two, cols), BF),
            pltpu.VMEM((2, height, cols), BF),
            pltpu.VMEM((2, height, cols), BF),
            pltpu.VMEM((2, height, height), BF),
            pltpu.VMEM((2, cols, cols), BF),
            pltpu.VMEM((2, cols, cols), BF),
            pltpu.VMEM((2, two, height), BF),
            pltpu.VMEM((2, two, cols), BF),
            pltpu.VMEM((RHS, 2, tall, cols), BF),
            pltpu.VMEM((RHS, 2, tall, cols), BF),
            pltpu.VMEM((2, rows, cols), BF),
            pltpu.VMEM((RHS, 2, rows, cols), BF),
            pltpu.VMEM((2, RHS, 2, rows, cols), BF),
            pltpu.SemaphoreType.REGULAR, pltpu.SemaphoreType.REGULAR,
            dma, dma,
            dma((group, RHS)), dma((n_c,)),
            dma((HALVES,)), dma((HALVES,)),
            dma((group, RHS)), dma((n_c,)),
            dma, dma,
            dma((RHS,)), dma((RHS,)),
            dma, dma, dma,
            dma((3, RHS, SUB)), dma((RHS, SUB)), dma((3, group, RHS, SUB)), dma((3, n_c, SUB)), dma((3, n_c, SUB)),
            dma, dma,
            dma((RHS, 2)), dma((RHS, 2)),
            dma((2,)), dma((RHS,)), dma, dma,
            dma((RHS, 2)), dma((RHS, 2)),
            dma((2, 2)), dma((2, RHS)),
        ],
        compiler_params=pltpu.CompilerParams(
            collective_id=0, has_side_effects=True, vmem_limit_bytes=56 * 1024 * 1024
        ),
        name="sweep",
    )(rhs_field, slowness, absorb_depth, line_inverse, cross_inverse)
    return field.astype(jnp.float32), rhs_field + near


def solution(mesh):
    field = P(None, "sec", None, "cross", None)
    return jax.shard_map(
        functools.partial(per_device, mesh.shape["sec"], mesh.shape["cross"]),
        mesh=mesh,
        in_specs=(
            field,
            P("sec", "cross", None),
            P("sec"),
            P("sec", None, None, None),
            P("sec", None, "cross", None),
        ),
        out_specs=(field, field),
        check_vma=False,
    )
```

```python
import functools

import jax
import jax.numpy as jnp
from jax import lax
from jax.experimental import pallas as pl
from jax.experimental.pallas import tpu as pltpu
from jax.sharding import PartitionSpec as P

MESH = pl.DeviceIdType.MESH
SIGMA_TOP = 2.0
CENTER = 128.0 / 30.0
FACE = 14.0 / 30.0
EDGE = 3.0 / 30.0
CORNER = 1.0 / 30.0
PAD = 16
RHS = 2
SUB = 4
HALVES = 2
BF = jnp.bfloat16


def kernel(
    n_s, n_c,
    rhs_hbm, slow_hbm, depth_ref, line_hbm, cross_hbm,
    sol_ref, near_ref,
    rhs_ref, slow_ref, line_ref, cross_ref, r_out, s_full, c2, ce_full, l_in, l_pair, c_pair, t_buf, t_acc, y_acc, y_out, y_in, x_low, x_far, cl_full, ll_full, l_quad, c_quad, xo, ext, ext_next, passing,
    p_out, p_in,
    go, sent, rx_send, rx_recv, rp_send, rp_recv, cx_send, cx_recv, ce_send, ce_recv, l_send, l_recv, y_send, y_recv,
    ls_send, le_send, ls_recv, xs_send, xf_send, xp_send, xe_send, x_recv, ec_send, ec_recv, h_send, h_recv, nc_send, nc_recv, nr_send, nr_recv, nh_send, nh_recv,
    p_send, p_recv, in_sem,
):
    rows, cols = rhs_ref.shape[3], rhs_ref.shape[4]
    height = rows * n_c
    group = n_c // RHS
    two = RHS * rows
    piece = rows // SUB
    half_block = rows // HALVES
    sec = lax.axis_index("sec")
    p = lax.axis_index("cross")
    r = p // group
    h = p % group
    q = (p + group) % n_c
    odd = sec % 2
    partner = sec + 1 - 2 * odd
    spot = sec % 4
    upper = spot >= 2
    first = sec < 2
    begin = sec < 4
    early = jnp.logical_and(spot < 2, sec >= 2)
    final = sec >= n_s - 2
    below = jnp.minimum(sec + 1, n_s - 1)
    above = jnp.maximum(sec - 1, 0)

    def at(s, c):
        return {"sec": s, "cross": c}

    def remote(source, target, send, recv, where):
        return pltpu.make_async_remote_copy(
            src_ref=source, dst_ref=target, send_sem=send, recv_sem=recv,
            device_id=where, device_id_type=MESH,
        )

    loads = [
        pltpu.make_async_copy(source, target, in_sem.at[i])
        for i, (source, target) in enumerate(
            ((rhs_hbm, rhs_ref), (line_hbm, line_ref), (cross_hbm, cross_ref), (slow_hbm, slow_ref))
        )
    ]
    for load in loads:
        load.start()

    def times(left, w0, w1):
        one = jnp.dot(left, w0, preferred_element_type=jnp.float32)
        other = jnp.dot(left, w1, preferred_element_type=jnp.float32)
        half = left.shape[0] // 2
        return one[:half] - other[half:], other[:half] + one[half:]

    barrier = pltpu.get_barrier_semaphore()

    def greet(s, c):
        pl.semaphore_signal(barrier, inc=1, device_id=at(s, c), device_id_type=MESH)

    for d in range(1, n_c):
        greet(sec, (p + d) % n_c)
    for d in range(n_c):
        greet(partner, (p + d) % n_c)

    outward = jnp.where(odd == 1, below, above)
    has_outward = jnp.where(odd == 1, sec < n_s - 1, sec > 0)

    @pl.when(has_outward)
    def _():
        for d in range(n_c):
            greet(outward, (p + d) % n_c)

    tops = spot == 3
    links = (
        (-2, jnp.logical_and(odd == 1, sec >= 2)),
        (2, jnp.logical_and(odd == 1, sec <= n_s - 3)),
        (-4, jnp.logical_and(tops, sec >= 4)),
        (4, jnp.logical_and(tops, sec <= n_s - 5)),
    )
    for way, there in links:
        @pl.when(there)
        def _():
            greet(sec + way, p)

    hands_on = jnp.logical_and(tops, sec <= n_s - 3)

    def block(b):
        return pl.ds(pl.multiple_of(b * rows, rows), rows)

    def row_block(k):
        return k * group + h

    for load in loads[:3]:
        load.wait()
    for c in range(2):
        c2[c, block(r), :] = cross_ref[0, c]

    @pl.when(odd == 1)
    def _():
        for c in range(2):
            r_out[c] = rhs_ref[c, 0, 1 - r].astype(BF)
            s_full[c, block(p), :] = rhs_ref[c, 0, r].astype(BF)

    @pl.when(odd == 0)
    def _():
        for b in (1 - r, r):
            left = jnp.concatenate([rhs_ref[c, 0, b].astype(BF) for c in range(2)], axis=0)
            re, im = times(left, line_ref[0, 0], line_ref[0, 1])
            if b is r:
                s_full[0, block(p), :] = re.astype(BF)
                s_full[1, block(p), :] = im.astype(BF)
            else:
                r_out[0] = re.astype(BF)
                r_out[1] = im.astype(BF)

    zeros_pad = jnp.zeros((PAD, cols), BF)

    @pl.when(p == 0)
    def _():
        for b in range(RHS):
            for c in range(2):
                ext[b, c, 0:PAD, :] = zeros_pad
                ext_next[b, c, 0:PAD, :] = zeros_pad

    @pl.when(p == n_c - 1)
    def _():
        for b in range(RHS):
            for c in range(2):
                ext[b, c, PAD + rows : PAD + rows + PAD, :] = zeros_pad
                ext_next[b, c, PAD + rows : PAD + rows + PAD, :] = zeros_pad

    met = (
        2 * n_c - 1
        + n_c * has_outward.astype(jnp.int32)
        + sum(there.astype(jnp.int32) for _, there in links)
    )
    pl.semaphore_wait(barrier, met)

    def peer(d):
        return r * group + (h + d) % group

    def half(b, i):
        return pl.ds(pl.multiple_of(b * rows + i * half_block, half_block), half_block)

    def rx_copy(i):
        return remote(
            r_out.at[:, pl.ds(i * half_block, half_block), :], s_full.at[:, half(p, i), :], rx_send.at[i], rx_recv.at[i],
            at(sec, q),
        )

    def rp_copy(d, k, i):
        here = s_full.at[:, half(row_block(k), i), :]
        return remote(here, here, rp_send.at[d, k, i], rp_recv.at[row_block(k), i], at(sec, peer(d)))

    def rp_arrival(b, i):
        here = s_full.at[:, half(b, i), :]
        return remote(here, here, rp_send.at[0, 0, i], rp_recv.at[b, i], at(sec, q))

    def all_peers():
        for b in groups():
            for i in range(HALVES):
                rp_arrival(b, i).wait_recv()

    def cx_copy(k, whose):
        part = pl.ds(pl.multiple_of(whose * rows + k * half_block, half_block), half_block)
        return remote(
            cross_ref.at[0, :, pl.ds(k * half_block, half_block), :], c2.at[:, part, :], cx_send.at[k], cx_recv.at[k], at(sec, q)
        )

    def ce_copy(d, k):
        b = row_block(k)
        return remote(
            c2.at[:, block(k), :], ce_full.at[:, block(b), :], ce_send.at[d, k], ce_recv.at[b], at(partner, peer(d))
        )

    def ce_arrival(b):
        return remote(
            ce_full.at[:, block(b), :], ce_full.at[:, block(b), :], ce_send.at[0, 0], ce_recv.at[b], at(partner, p)
        )

    def l_copy():
        return remote(line_ref.at[0], l_in, l_send, l_recv, at(partner, p))

    def y_copy(k):
        return remote(y_out.at[:, block(k), :], y_in.at[:, block(k), :], y_send.at[k], y_recv.at[k], at(partner, p))

    def bit(b, s):
        return pl.ds(pl.multiple_of(b * rows + s * piece, piece), piece)

    spread_into = (x_low, x_far, cl_full)
    LOW, FAR, MIX = range(3)

    def xs_copy(a, k, s):
        source = (y_out, xo, c_pair)[a]
        b = row_block(k)
        return remote(
            source.at[:, bit(k, s), :], spread_into[a].at[:, bit(b, s), :], xs_send.at[a, k, s], x_recv.at[a, b, s],
            at(jnp.minimum(sec + 2, n_s - 1), p),
        )

    def xf_copy(k, s):
        b = row_block(k)
        return remote(
            xo.at[:, bit(k, s), :], x_far.at[:, bit(b, s), :], xf_send.at[k, s], x_recv.at[FAR, b, s],
            at(jnp.minimum(sec + 4, n_s - 1), p),
        )

    def xp_copy(a, d, k, s):
        b = row_block(k)
        here = spread_into[a].at[:, bit(b, s), :]
        return remote(here, here, xp_send.at[a, d, k, s], x_recv.at[a, b, s], at(sec, peer(d)))

    def xe_copy(a, b, s):
        here = spread_into[a].at[:, bit(b, s), :]
        return remote(here, here, xe_send.at[a, b, s], x_recv.at[a, b, s], at(partner, p))

    def ls_copy():
        return remote(l_pair, ll_full, ls_send, ls_recv, at(jnp.minimum(sec + 2, n_s - 1), p))

    def le_copy():
        return remote(ll_full, ll_full, le_send, ls_recv, at(partner, p))

    center = pl.ds(PAD, rows)

    def ec_copy(whose):
        return remote(xo.at[:, block(1 - r), :], ext.at[whose, :, center, :], ec_send, ec_recv, at(sec, q))

    def edge(k, side):
        b = row_block(k)
        start = k * rows + (rows - PAD) * side
        to = b - 1 + 2 * side
        exists = to >= 0 if side == 0 else to < n_c
        return pl.ds(pl.multiple_of(start, PAD), PAD), jnp.clip(to, 0, n_c - 1), exists

    def pad_at(side):
        return pl.ds((rows + PAD) * (1 - side), PAD)

    def h_copy(k, side):
        source, to, _ = edge(k, side)
        return remote(
            xo.at[:, source, :], ext.at[r, :, pad_at(side), :], h_send.at[k, side], h_recv.at[r, side], at(sec, to)
        )

    def h_arrival(b, side):
        return remote(
            ext.at[b, :, pad_at(side), :], ext.at[b, :, pad_at(side), :], h_send.at[0, side], h_recv.at[b, side], at(sec, q)
        )

    def nc_copy():
        return remote(xo.at[:, block(r), :], ext_next.at[r, :, center, :], nc_send.at[0], nc_recv.at[r], at(above, p))

    def np_copy():
        return remote(xo.at[:, block(1 - r), :], passing, nc_send.at[1], nr_recv, at(above, p))

    def nr_copy():
        return remote(passing, ext_next.at[r, :, center, :], nr_send, nc_recv.at[r], at(sec, q))

    def nc_arrival(b):
        return remote(
            ext_next.at[b, :, center, :], ext_next.at[b, :, center, :], nc_send.at[0], nc_recv.at[b], at(below, p)
        )

    def nh_copy(k, side):
        source, to, _ = edge(k, side)
        return remote(
            xo.at[:, source, :], ext_next.at[r, :, pad_at(side), :], nh_send.at[k, side], nh_recv.at[r, side],
            at(above, to),
        )

    def nh_arrival(b, side):
        return remote(
            ext_next.at[b, :, pad_at(side), :], ext_next.at[b, :, pad_at(side), :], nh_send.at[0, side],
            nh_recv.at[b, side], at(below, p),
        )

    def p_copy(way, j, b):
        return remote(
            p_out.at[b], p_in.at[way, b], p_send.at[way, j], p_recv.at[way, b], at(below if way == 0 else above, p)
        )

    def stacked(ref, where):
        part = ref[:, where, :]
        return part.reshape(2 * part.shape[1], part.shape[2])

    def product(out, left, right, length):
        tile = min(128, length)

        def some(i, _):
            where = pl.ds(pl.multiple_of(i * tile, tile), tile)
            re, im = times(stacked(left, where), right[0], right[1])
            out[0, where, :] = re.astype(out.dtype)
            out[1, where, :] = im.astype(out.dtype)
            return 0

        lax.fori_loop(0, length // tile, some, 0)

    class First:
        def __init__(self, ref):
            self.ref = ref

        def __getitem__(self, c):
            return self.ref[0, c]

    line = First(line_ref)
    splits = rows % 128 == 0

    def arrive(a):
        for k in range(RHS):
            for s in range(SUB):
                xe_copy(a, row_block(k), s).wait_recv()
                for d in range(1, group):
                    xp_copy(a, d, k, s).start()
                xe_copy(a, row_block(k), s).start()

    def arrive_peers(a):
        for b in groups():
            for s in range(SUB):
                xe_copy(a, b, s).wait_recv()
                xe_copy(a, b, s).start()

    def arrive_even(a):
        for b in range(n_c):
            for s in range(SUB):
                xe_copy(a, b, s).wait_recv()

    def add_on(left, right):
        for k in range(RHS):
            here = slice(k * rows, (k + 1) * rows)
            re, im = times(stacked(left, pl.ds(k * rows, rows)), right[0], right[1])
            y_acc[0, here, :] += re
            y_acc[1, here, :] += im

    def gather_product(a, mat):
        arrive(a)
        finish(a, mat)

    def finish(a, mat):
        if splits:
            own_part(mat, spread_into[a])
        arrive_peers(a)
        if splits:
            peer_part(mat, spread_into[a])
        else:
            product(t_buf, mat, spread_into[a], two)

    def own_part(mat, x_full):
        for i in range(RHS):
            here = pl.ds(i * rows, rows)
            w = [jnp.concatenate([x_full[c, block(row_block(k)), :] for k in range(RHS)], axis=0) for c in range(2)]
            left = jnp.concatenate(
                [jnp.concatenate([mat[c, here, block(row_block(k))] for k in range(RHS)], axis=1) for c in range(2)],
                axis=0,
            )
            re, im = times(left, w[0], w[1])
            t_acc[0, here, :] = re
            t_acc[1, here, :] = im

    def peer_part(mat, x_full):
        for i in range(RHS):
            here = pl.ds(i * rows, rows)
            re, im = t_acc[0, here, :], t_acc[1, here, :]
            for d in range(1, group):
                at_block = [k * group + (h + d) % group for k in range(RHS)]
                w = [jnp.concatenate([x_full[c, block(b), :] for b in at_block], axis=0) for c in range(2)]
                left = jnp.concatenate(
                    [jnp.concatenate([mat[c, here, block(b)] for b in at_block], axis=1) for c in range(2)], axis=0
                )
                more_re, more_im = times(left, w[0], w[1])
                re, im = re + more_re, im + more_im
            t_buf[0, here, :] = re.astype(BF)
            t_buf[1, here, :] = im.astype(BF)

    def groups():
        for d in range(1, group):
            for k in range(RHS):
                yield k * group + (h + d) % group

    def put(k):
        @pl.when(hands_on)
        def _():
            for s in range(SUB):
                xf_copy(k, s).start()
                xs_copy(FAR, k, s).start()

        @pl.when(k != r)
        def _():
            ec_copy(r).start()

        for side in range(2):
            @pl.when(edge(k, side)[2])
            def _():
                h_copy(k, side).start()

    def emit(left, right, base):
        for k in range(RHS):
            re, im = times(stacked(left, pl.ds(k * rows, rows)), right[0], right[1])
            if base:
                re, im = re + y_acc[0, k * rows : (k + 1) * rows, :], im + y_acc[1, k * rows : (k + 1) * rows, :]
            xo[0, k * rows : (k + 1) * rows, :] = re.astype(BF)
            xo[1, k * rows : (k + 1) * rows, :] = im.astype(BF)
            put(k)

    @pl.when(odd == 0)
    def _():
        for i in range(HALVES):
            rx_copy(i).start()
        for d in range(1, group):
            for k in range(RHS):
                @pl.when(k == r)
                def _():
                    for i in range(HALVES):
                        rp_copy(d, k, i).start()

        @pl.when(sec >= 2)
        def _():
            l_copy().start()

        for i in range(HALVES):
            rx_copy(i).wait_send()
        for k in range(HALVES):
            cx_copy(k, r).start()

        def ce_early(own):
            for k in range(RHS):
                @pl.when(jnp.logical_and(early, (k == r) == own))
                def _():
                    for d in range(group):
                        ce_copy(d, k).start()

        ce_early(True)
        for i in range(HALVES):
            rx_copy(i).wait_recv()
            for d in range(1, group):
                for k in range(RHS):
                    @pl.when(k != r)
                    def _():
                        rp_copy(d, k, i).start()
        cx_copy(0, 1 - r).wait_recv()
        pl.semaphore_signal(go, inc=1, device_id=at(partner, p), device_id_type=MESH)
        for k in range(1, HALVES):
            cx_copy(k, 1 - r).wait_recv()
        ce_early(False)
        all_peers()
        for k in range(RHS):
            re, im = times(stacked(c2, pl.ds(k * rows, rows)), s_full[0], s_full[1])
            here = slice(k * rows, (k + 1) * rows)
            y_acc[0, here, :] = re
            y_acc[1, here, :] = im
            y_out[0, here, :] = re.astype(BF)
            y_out[1, here, :] = im.astype(BF)
            y_copy(k).start()

        @pl.when(first)
        def _():
            for k in range(RHS):
                here = slice(k * rows, (k + 1) * rows)
                for c in range(2):
                    xo[c, here, :] = y_out[c, here, :]
                put(k)

        @pl.when(sec >= 2)
        def _():
            @pl.when(upper)
            def _():
                for d in range(group):
                    for k in range(RHS):
                        ce_copy(d, k).start()

            @pl.when(upper)
            def _():
                @pl.when(jnp.logical_not(begin))
                def _():
                    le_copy().wait_recv()
                    product(l_quad, ll_full, line, cols)
                    arrive_even(MIX)
                    product(c_quad, c2, cl_full, two)

                arrive_even(LOW)
                product(t_buf, c2, x_low, two)

                @pl.when(begin)
                def _():
                    emit(t_buf, line, True)

                @pl.when(jnp.logical_not(begin))
                def _():
                    add_on(t_buf, line)
                    arrive_even(FAR)
                    product(t_buf, c_quad, x_far, two)
                    emit(t_buf, l_quad, True)

            @pl.when(jnp.logical_not(upper))
            def _():
                arrive_even(FAR)
                product(t_buf, c2, x_far, two)
                emit(t_buf, line, True)

            @pl.when(jnp.logical_and(upper, jnp.logical_not(final)))
            def _():
                pl.semaphore_wait(sent, 1)

            np_copy().start()
            nc_copy().start()
            for k in range(RHS):
                for side in range(2):
                    @pl.when(edge(k, side)[2])
                    def _():
                        nh_copy(k, side).start()

    @pl.when(odd == 1)
    def _():
        pl.semaphore_wait(go, 1)
        for i in range(HALVES):
            rx_copy(i).start()
        for k in range(HALVES):
            cx_copy(k, r).start()

        @pl.when(sec >= 2)
        def _():
            l_copy().wait_recv()
            product(l_pair, l_in, line, cols)

            @pl.when(spot == 1)
            def _():
                ls_copy().start()

        for i in range(HALVES):
            rx_copy(i).wait_recv()
        for k in range(RHS):
            y_copy(k).wait_recv()
            here = block(row_block(k))
            both = [
                (s_full[c, here, :].astype(jnp.float32) + y_in[c, k * rows : (k + 1) * rows, :].astype(jnp.float32)).astype(BF)
                for c in range(2)
            ]
            re, im = times(jnp.concatenate(both, axis=0), line[0], line[1])
            s_full[0, here, :] = re.astype(BF)
            s_full[1, here, :] = im.astype(BF)
            for d in range(1, group):
                for i in range(HALVES):
                    rp_copy(d, k, i).start()

        @pl.when(jnp.logical_and(tops, jnp.logical_not(begin)))
        def _():
            ls_copy().wait_recv()
            le_copy().start()
            product(l_quad, ll_full, l_pair, cols)

        for k in range(HALVES):
            cx_copy(k, 1 - r).wait_recv()

        @pl.when(early)
        def _():
            for b in range(n_c):
                ce_arrival(b).wait_recv()
            product(c_pair, c2, ce_full, two)
            for k in range(RHS):
                for s in range(SUB):
                    xs_copy(MIX, k, s).start()

        all_peers()

        @pl.when(spot == 1)
        def _():
            for k in range(RHS):
                re, im = times(stacked(c2, pl.ds(k * rows, rows)), s_full[0], s_full[1])
                here = slice(k * rows, (k + 1) * rows)
                y_acc[0, here, :] = re
                y_acc[1, here, :] = im
                y_out[0, here, :] = re.astype(BF)
                y_out[1, here, :] = im.astype(BF)
                for s in range(SUB):
                    xs_copy(LOW, k, s).start()

                @pl.when(first)
                def _():
                    for c in range(2):
                        xo[c, here, :] = y_out[c, here, :]
                    put(k)

        @pl.when(tops)
        def _():
            product(y_acc, c2, s_full, two)

        @pl.when(sec >= 2)
        def _():
            @pl.when(spot == 1)
            def _():
                gather_product(FAR, c_pair)
                emit(t_buf, l_pair, True)

            @pl.when(tops)
            def _():
                @pl.when(jnp.logical_not(begin))
                def _():
                    arrive(MIX)

                arrive(LOW)
                for b in range(n_c):
                    ce_arrival(b).wait_recv()
                product(c_pair, c2, ce_full, two)

                @pl.when(jnp.logical_not(begin))
                def _():
                    arrive_peers(MIX)
                    product(c_quad, c_pair, cl_full, two)

                finish(LOW, c_pair)

                @pl.when(begin)
                def _():
                    emit(t_buf, l_pair, True)

                @pl.when(jnp.logical_not(begin))
                def _():
                    add_on(t_buf, l_pair)
                    gather_product(FAR, c_quad)
                    emit(t_buf, l_quad, True)

                @pl.when(hands_on)
                def _():
                    for k in range(RHS):
                        for s in range(SUB):
                            xf_copy(k, s).wait_send()
                            xs_copy(FAR, k, s).wait_send()
                    pl.semaphore_signal(sent, inc=1, device_id=at(partner, p), device_id_type=MESH)

    for c in range(2):
        ext[r, c, PAD : PAD + rows, :] = xo[c, block(r), :]

    column = lax.broadcasted_iota(jnp.int32, (rows, cols), 1)
    tall = rows + 2 * PAD

    def sideways(v):
        before = jnp.where(column == 0, 0.0, pltpu.roll(v, 1, 1))
        after = jnp.where(column == cols - 1, 0.0, pltpu.roll(v, cols - 1, 1))
        return before + after

    def plane(f):
        here = f[PAD : PAD + rows]
        updown = (pltpu.roll(f, 1, 0) + pltpu.roll(f, tall - 1, 0))[PAD : PAD + rows]
        faces = updown + sideways(here)
        corners = sideways(updown)
        return here, faces, corners

    for j in range(2):
        b = r if j == 0 else 1 - r
        if j == 1:
            ec_copy(1 - r).wait_recv()

        @pl.when(p > 0)
        def _():
            h_arrival(b, 1).wait_recv()

        @pl.when(p < n_c - 1)
        def _():
            h_arrival(b, 0).wait_recv()

        for c in range(2):
            here, faces, corners = plane(ext[b, c].astype(jnp.float32))
            sol_ref[c, 0, b] = here.astype(BF)
            p_out[b, c] = (FACE * here + EDGE * faces + CORNER * corners).astype(BF)
            near_ref[c, 0, b] = FACE * faces + EDGE * corners - CENTER * here

        @pl.when(odd == 0)
        def _():
            p_copy(0, j, b).start()

        @pl.when(odd == 1)
        def _():
            p_copy(1, j, b).start()

            @pl.when(sec < n_s - 1)
            def _():
                p_copy(0, j, b).start()

    line_at = lax.broadcasted_iota(jnp.int32, (1, cols), 1)
    distance = jnp.minimum(line_at, cols - 1 - line_at).astype(jnp.float32)
    depth = jnp.full((1, cols), depth_ref[0], jnp.int32).astype(jnp.float32)
    ramp = jnp.maximum(depth - distance, 0.0) / depth
    damping = SIGMA_TOP * ramp * ramp
    loads[3].wait()
    wave_real = slow_ref[0]
    wave_imag = wave_real * damping
    for b in range(RHS):
        re, im = (ext[b, c, PAD : PAD + rows, :].astype(jnp.float32) for c in range(2))
        near_ref[0, 0, b] += wave_real * re - wave_imag * im
        near_ref[1, 0, b] += wave_real * im + wave_imag * re

    def neighbour(way):
        for j in range(2):
            b = r if j == 0 else 1 - r
            p_copy(way, j, b).wait_recv()
            for c in range(2):
                near_ref[c, 0, b] += p_in[way, b, c].astype(jnp.float32)

    @pl.when(sec > 0)
    def _():
        neighbour(0)

    @pl.when(odd == 0)
    def _():
        neighbour(1)

    @pl.when(jnp.logical_and(odd == 1, sec < n_s - 1))
    def _():
        np_copy().wait_recv()
        nr_copy().start()
        for j in range(2):
            b = r if j == 0 else 1 - r
            nc_arrival(b).wait_recv()

            @pl.when(p > 0)
            def _():
                nh_arrival(b, 1).wait_recv()

            @pl.when(p < n_c - 1)
            def _():
                nh_arrival(b, 0).wait_recv()

            for c in range(2):
                here, faces, corners = plane(ext_next[b, c].astype(jnp.float32))
                near_ref[c, 0, b] += FACE * here + EDGE * faces + CORNER * corners

        nr_copy().wait_send()

    @pl.when(odd == 1)
    def _():
        for i in range(HALVES):
            rx_copy(i).wait_send()

    for k in range(HALVES):
        cx_copy(k, r).wait_send()
    for d in range(1, group):
        for k in range(RHS):
            for i in range(HALVES):
                rp_copy(d, k, i).wait_send()
    ec_copy(r).wait_send()
    for k in range(RHS):
        for side in range(2):
            @pl.when(edge(k, side)[2])
            def _():
                h_copy(k, side).wait_send()

    @pl.when(odd == 0)
    def _():
        for k in range(RHS):
            y_copy(k).wait_send()
        for j in range(2):
            p_copy(0, j, r).wait_send()

        @pl.when(sec >= 2)
        def _():
            l_copy().wait_send()
            nc_copy().wait_send()
            np_copy().wait_send()
            for k in range(RHS):
                for d in range(group):
                    ce_copy(d, k).wait_send()
                for side in range(2):
                    @pl.when(edge(k, side)[2])
                    def _():
                        nh_copy(k, side).wait_send()

    @pl.when(odd == 1)
    def _():
        for j in range(2):
            p_copy(1, j, r).wait_send()

        @pl.when(sec < n_s - 1)
        def _():
            for j in range(2):
                p_copy(0, j, r).wait_send()

    def spread_sent(a):
        for s in range(SUB):
            for k in range(RHS):
                for d in range(1, group):
                    xp_copy(a, d, k, s).wait_send()
            for b in range(n_c):
                xe_copy(a, b, s).wait_send()

    def passed_on(a):
        for k in range(RHS):
            for s in range(SUB):
                xs_copy(a, k, s).wait_send()

    @pl.when(spot == 1)
    def _():
        passed_on(LOW)

        @pl.when(sec >= 2)
        def _():
            ls_copy().wait_send()
            passed_on(MIX)
            spread_sent(FAR)

    @pl.when(tops)
    def _():
        spread_sent(LOW)

        @pl.when(jnp.logical_not(begin))
        def _():
            le_copy().wait_send()
            spread_sent(MIX)
            spread_sent(FAR)


def per_device(n_s, n_c, rhs_field, slowness, absorb_depth, line_inverse, cross_inverse):
    rows, cols = slowness.shape[1:]
    height = rows * n_c
    group = n_c // RHS
    two = RHS * rows
    tall = rows + 2 * PAD
    vmem = pl.BlockSpec(memory_space=pltpu.VMEM)
    hbm = pl.BlockSpec(memory_space=pl.ANY)
    dma = pltpu.SemaphoreType.DMA
    field, near = pl.pallas_call(
        functools.partial(kernel, n_s, n_c),
        out_shape=(
            jax.ShapeDtypeStruct(rhs_field.shape, BF),
            jax.ShapeDtypeStruct(rhs_field.shape, jnp.float32),
        ),
        in_specs=[hbm, hbm, pl.BlockSpec(memory_space=pltpu.SMEM), hbm, hbm],
        out_specs=(vmem, vmem),
        scratch_shapes=[
            pltpu.VMEM(rhs_field.shape, jnp.float32),
            pltpu.VMEM(slowness.shape, jnp.float32),
            pltpu.VMEM(line_inverse.shape, BF),
            pltpu.VMEM(cross_inverse.shape, BF),
            pltpu.VMEM((2, rows, cols), BF),
            pltpu.VMEM((2, height, cols), BF),
            pltpu.VMEM((2, two, height), BF),
            pltpu.VMEM((2, height, height), BF),
            pltpu.VMEM((2, cols, cols), BF),
            pltpu.VMEM((2, cols, cols), BF),
            pltpu.VMEM((2, two, height), BF),
            pltpu.VMEM((2, two, cols), BF),
            pltpu.VMEM((2, two, cols), jnp.float32),
            pltpu.VMEM((2, two, cols), jnp.float32),
            pltpu.VMEM((2, two, cols), BF),
            pltpu.VMEM((2, two, cols), BF),
            pltpu.VMEM((2, height, cols), BF),
            pltpu.VMEM((2, height, cols), BF),
            pltpu.VMEM((2, height, height), BF),
            pltpu.VMEM((2, cols, cols), BF),
            pltpu.VMEM((2, cols, cols), BF),
            pltpu.VMEM((2, two, height), BF),
            pltpu.VMEM((2, two, cols), BF),
            pltpu.VMEM((RHS, 2, tall, cols), BF),
            pltpu.VMEM((RHS, 2, tall, cols), BF),
            pltpu.VMEM((2, rows, cols), BF),
            pltpu.VMEM((RHS, 2, rows, cols), BF),
            pltpu.VMEM((2, RHS, 2, rows, cols), BF),
            pltpu.SemaphoreType.REGULAR, pltpu.SemaphoreType.REGULAR,
            dma((HALVES,)), dma((HALVES,)),
            dma((group, RHS, HALVES)), dma((n_c, HALVES)),
            dma((HALVES,)), dma((HALVES,)),
            dma((group, RHS)), dma((n_c,)),
            dma, dma,
            dma((RHS,)), dma((RHS,)),
            dma, dma, dma,
            dma((3, RHS, SUB)), dma((RHS, SUB)), dma((3, group, RHS, SUB)), dma((3, n_c, SUB)), dma((3, n_c, SUB)),
            dma, dma,
            dma((RHS, 2)), dma((RHS, 2)),
            dma((2,)), dma((RHS,)), dma, dma,
            dma((RHS, 2)), dma((RHS, 2)),
            dma((2, 2)), dma((2, RHS)), dma((4,)),
        ],
        compiler_params=pltpu.CompilerParams(
            collective_id=0, has_side_effects=True, vmem_limit_bytes=56 * 1024 * 1024
        ),
        name="sweep",
    )(rhs_field, slowness, absorb_depth, line_inverse, cross_inverse)
    return field.astype(jnp.float32), rhs_field + near


def solution(mesh):
    field = P(None, "sec", None, "cross", None)
    return jax.shard_map(
        functools.partial(per_device, mesh.shape["sec"], mesh.shape["cross"]),
        mesh=mesh,
        in_specs=(
            field,
            P("sec", "cross", None),
            P("sec"),
            P("sec", None, None, None),
            P("sec", None, "cross", None),
        ),
        out_specs=(field, field),
        check_vma=False,
    )
```

```python
import functools

import jax
import jax.numpy as jnp
from jax import lax
from jax.experimental import pallas as pl
from jax.experimental.pallas import tpu as pltpu
from jax.sharding import PartitionSpec as P

MESH = pl.DeviceIdType.MESH
SIGMA_TOP = 2.0
CENTER = 128.0 / 30.0
FACE = 14.0 / 30.0
EDGE = 3.0 / 30.0
CORNER = 1.0 / 30.0
PAD = 16
RHS = 2
SUB = 4
HALVES = 2
BF = jnp.bfloat16


def kernel(
    n_s, n_c,
    rhs_hbm, slow_hbm, depth_ref, line_hbm, cross_hbm,
    sol_ref, near_ref,
    rhs_ref, slow_ref, line_ref, cross_ref, r_out, s_full, c2, ce_full, l_in, l_pair, c_pair, t_buf, t_acc, y_acc, y_out, y_in, x_low, x_far, cl_full, ll_full, l_quad, c_quad, xo, ext, ext_next, passing,
    p_out, p_in,
    go, sent, rx_send, rx_recv, rp_send, rp_recv, cx_send, cx_recv, ce_send, ce_recv, l_send, l_recv, y_send, y_recv,
    ls_send, le_send, ls_recv, xs_send, xf_send, xp_send, xe_send, x_recv, ec_send, ec_recv, h_send, h_recv, nc_send, nc_recv, nr_send, nr_recv, nh_send, nh_recv,
    p_send, p_recv, in_sem,
):
    rows, cols = rhs_ref.shape[3], rhs_ref.shape[4]
    height = rows * n_c
    group = n_c // RHS
    two = RHS * rows
    piece = rows // SUB
    half_block = rows // HALVES
    sec = lax.axis_index("sec")
    p = lax.axis_index("cross")
    r = p // group
    h = p % group
    q = (p + group) % n_c
    odd = sec % 2
    partner = sec + 1 - 2 * odd
    spot = sec % 4
    upper = spot >= 2
    first = sec < 2
    begin = sec < 4
    early = jnp.logical_and(spot < 2, sec >= 2)
    final = sec >= n_s - 2
    below = jnp.minimum(sec + 1, n_s - 1)
    above = jnp.maximum(sec - 1, 0)

    def at(s, c):
        return {"sec": s, "cross": c}

    def remote(source, target, send, recv, where):
        return pltpu.make_async_remote_copy(
            src_ref=source, dst_ref=target, send_sem=send, recv_sem=recv,
            device_id=where, device_id_type=MESH,
        )

    loads = [
        pltpu.make_async_copy(source, target, in_sem.at[i])
        for i, (source, target) in enumerate(
            ((rhs_hbm, rhs_ref), (line_hbm, line_ref), (cross_hbm, cross_ref), (slow_hbm, slow_ref))
        )
    ]
    for load in loads:
        load.start()

    def times(left, w0, w1):
        one = jnp.dot(left, w0, preferred_element_type=jnp.float32)
        other = jnp.dot(left, w1, preferred_element_type=jnp.float32)
        half = left.shape[0] // 2
        return one[:half] - other[half:], other[:half] + one[half:]

    barrier = pltpu.get_barrier_semaphore()

    def greet(s, c):
        pl.semaphore_signal(barrier, inc=1, device_id=at(s, c), device_id_type=MESH)

    for d in range(1, n_c):
        greet(sec, (p + d) % n_c)
    for d in range(n_c):
        greet(partner, (p + d) % n_c)

    outward = jnp.where(odd == 1, below, above)
    has_outward = jnp.where(odd == 1, sec < n_s - 1, sec > 0)

    @pl.when(has_outward)
    def _():
        for d in range(n_c):
            greet(outward, (p + d) % n_c)

    tops = spot == 3
    links = (
        (-2, jnp.logical_and(odd == 1, sec >= 2)),
        (2, jnp.logical_and(odd == 1, sec <= n_s - 3)),
        (-4, jnp.logical_and(tops, sec >= 4)),
        (4, jnp.logical_and(tops, sec <= n_s - 5)),
    )
    for way, there in links:
        @pl.when(there)
        def _():
            greet(sec + way, p)

    hands_on = jnp.logical_and(tops, sec <= n_s - 3)

    def block(b):
        return pl.ds(pl.multiple_of(b * rows, rows), rows)

    def row_block(k):
        return k * group + h

    for load in loads[:3]:
        load.wait()
    for c in range(2):
        c2[c, block(r), :] = cross_ref[0, c]

    @pl.when(odd == 1)
    def _():
        for c in range(2):
            r_out[c] = rhs_ref[c, 0, 1 - r].astype(BF)
            s_full[c, block(p), :] = rhs_ref[c, 0, r].astype(BF)

    @pl.when(odd == 0)
    def _():
        for b in (1 - r, r):
            left = jnp.concatenate([rhs_ref[c, 0, b].astype(BF) for c in range(2)], axis=0)
            re, im = times(left, line_ref[0, 0], line_ref[0, 1])
            if b is r:
                s_full[0, block(p), :] = re.astype(BF)
                s_full[1, block(p), :] = im.astype(BF)
            else:
                r_out[0] = re.astype(BF)
                r_out[1] = im.astype(BF)

    zeros_pad = jnp.zeros((PAD, cols), BF)

    @pl.when(p == 0)
    def _():
        for b in range(RHS):
            for c in range(2):
                ext[b, c, 0:PAD, :] = zeros_pad
                ext_next[b, c, 0:PAD, :] = zeros_pad

    @pl.when(p == n_c - 1)
    def _():
        for b in range(RHS):
            for c in range(2):
                ext[b, c, PAD + rows : PAD + rows + PAD, :] = zeros_pad
                ext_next[b, c, PAD + rows : PAD + rows + PAD, :] = zeros_pad

    met = (
        2 * n_c - 1
        + n_c * has_outward.astype(jnp.int32)
        + sum(there.astype(jnp.int32) for _, there in links)
    )
    pl.semaphore_wait(barrier, met)

    def peer(d):
        return r * group + (h + d) % group

    def half(b, i):
        return pl.ds(pl.multiple_of(b * rows + i * half_block, half_block), half_block)

    def rx_copy(i):
        return remote(
            r_out.at[:, pl.ds(i * half_block, half_block), :], s_full.at[:, half(p, i), :], rx_send.at[i], rx_recv.at[i],
            at(sec, q),
        )

    def rp_copy(d, k, i):
        here = s_full.at[:, half(row_block(k), i), :]
        return remote(here, here, rp_send.at[d, k, i], rp_recv.at[row_block(k), i], at(sec, peer(d)))

    def rp_arrival(b, i):
        here = s_full.at[:, half(b, i), :]
        return remote(here, here, rp_send.at[0, 0, i], rp_recv.at[b, i], at(sec, q))

    def all_peers():
        for b in groups():
            for i in range(HALVES):
                rp_arrival(b, i).wait_recv()

    def cx_copy(k, whose):
        part = pl.ds(pl.multiple_of(whose * rows + k * half_block, half_block), half_block)
        return remote(
            cross_ref.at[0, :, pl.ds(k * half_block, half_block), :], c2.at[:, part, :], cx_send.at[k], cx_recv.at[k], at(sec, q)
        )

    def ce_copy(d, k):
        b = row_block(k)
        return remote(
            c2.at[:, block(k), :], ce_full.at[:, block(b), :], ce_send.at[d, k], ce_recv.at[b], at(partner, peer(d))
        )

    def ce_arrival(b):
        return remote(
            ce_full.at[:, block(b), :], ce_full.at[:, block(b), :], ce_send.at[0, 0], ce_recv.at[b], at(partner, p)
        )

    def l_copy():
        return remote(line_ref.at[0], l_in, l_send, l_recv, at(partner, p))

    def y_copy(k):
        return remote(y_out.at[:, block(k), :], y_in.at[:, block(k), :], y_send.at[k], y_recv.at[k], at(partner, p))

    def bit(b, s):
        return pl.ds(pl.multiple_of(b * rows + s * piece, piece), piece)

    spread_into = (x_low, x_far, cl_full)
    LOW, FAR, MIX = range(3)

    def xs_copy(a, k, s):
        source = (y_out, xo, c_pair)[a]
        b = row_block(k)
        return remote(
            source.at[:, bit(k, s), :], spread_into[a].at[:, bit(b, s), :], xs_send.at[a, k, s], x_recv.at[a, b, s],
            at(jnp.minimum(sec + 2, n_s - 1), p),
        )

    def xf_copy(k, s):
        b = row_block(k)
        return remote(
            xo.at[:, bit(k, s), :], x_far.at[:, bit(b, s), :], xf_send.at[k, s], x_recv.at[FAR, b, s],
            at(jnp.minimum(sec + 4, n_s - 1), p),
        )

    def xp_copy(a, d, k, s):
        b = row_block(k)
        here = spread_into[a].at[:, bit(b, s), :]
        return remote(here, here, xp_send.at[a, d, k, s], x_recv.at[a, b, s], at(sec, peer(d)))

    def xe_copy(a, b, s):
        here = spread_into[a].at[:, bit(b, s), :]
        return remote(here, here, xe_send.at[a, b, s], x_recv.at[a, b, s], at(partner, p))

    def ls_copy():
        return remote(l_pair, ll_full, ls_send, ls_recv, at(jnp.minimum(sec + 2, n_s - 1), p))

    def le_copy():
        return remote(ll_full, ll_full, le_send, ls_recv, at(partner, p))

    center = pl.ds(PAD, rows)

    def ec_copy(whose):
        return remote(xo.at[:, block(1 - r), :], ext.at[whose, :, center, :], ec_send, ec_recv, at(sec, q))

    def edge(k, side):
        b = row_block(k)
        start = k * rows + (rows - PAD) * side
        to = b - 1 + 2 * side
        exists = to >= 0 if side == 0 else to < n_c
        return pl.ds(pl.multiple_of(start, PAD), PAD), jnp.clip(to, 0, n_c - 1), exists

    def pad_at(side):
        return pl.ds((rows + PAD) * (1 - side), PAD)

    def h_copy(k, side):
        source, to, _ = edge(k, side)
        return remote(
            xo.at[:, source, :], ext.at[r, :, pad_at(side), :], h_send.at[k, side], h_recv.at[r, side], at(sec, to)
        )

    def h_arrival(b, side):
        return remote(
            ext.at[b, :, pad_at(side), :], ext.at[b, :, pad_at(side), :], h_send.at[0, side], h_recv.at[b, side], at(sec, q)
        )

    def nc_copy():
        return remote(xo.at[:, block(r), :], ext_next.at[r, :, center, :], nc_send.at[0], nc_recv.at[r], at(above, p))

    def np_copy():
        return remote(xo.at[:, block(1 - r), :], passing, nc_send.at[1], nr_recv, at(above, p))

    def nr_copy():
        return remote(passing, ext_next.at[r, :, center, :], nr_send, nc_recv.at[r], at(sec, q))

    def nc_arrival(b):
        return remote(
            ext_next.at[b, :, center, :], ext_next.at[b, :, center, :], nc_send.at[0], nc_recv.at[b], at(below, p)
        )

    def nh_copy(k, side):
        source, to, _ = edge(k, side)
        return remote(
            xo.at[:, source, :], ext_next.at[r, :, pad_at(side), :], nh_send.at[k, side], nh_recv.at[r, side],
            at(above, to),
        )

    def nh_arrival(b, side):
        return remote(
            ext_next.at[b, :, pad_at(side), :], ext_next.at[b, :, pad_at(side), :], nh_send.at[0, side],
            nh_recv.at[b, side], at(below, p),
        )

    def p_copy(way, j, b):
        return remote(
            p_out.at[b], p_in.at[way, b], p_send.at[way, j], p_recv.at[way, b], at(below if way == 0 else above, p)
        )

    def stacked(ref, where):
        part = ref[:, where, :]
        return part.reshape(2 * part.shape[1], part.shape[2])

    def product(out, left, right, length):
        tile = min(128, length)

        def some(i, _):
            where = pl.ds(pl.multiple_of(i * tile, tile), tile)
            re, im = times(stacked(left, where), right[0], right[1])
            out[0, where, :] = re.astype(out.dtype)
            out[1, where, :] = im.astype(out.dtype)
            return 0

        lax.fori_loop(0, length // tile, some, 0)

    class First:
        def __init__(self, ref):
            self.ref = ref

        def __getitem__(self, c):
            return self.ref[0, c]

    line = First(line_ref)
    splits = rows % 128 == 0

    def arrive(a):
        for k in range(RHS):
            for s in range(SUB):
                xe_copy(a, row_block(k), s).wait_recv()
                for d in range(1, group):
                    xp_copy(a, d, k, s).start()
                xe_copy(a, row_block(k), s).start()

    def arrive_peers(a):
        for b in groups():
            for s in range(SUB):
                xe_copy(a, b, s).wait_recv()
                xe_copy(a, b, s).start()

    def arrive_even(a):
        for b in range(n_c):
            for s in range(SUB):
                xe_copy(a, b, s).wait_recv()

    def add_on(left, right):
        for k in range(RHS):
            here = slice(k * rows, (k + 1) * rows)
            re, im = times(stacked(left, pl.ds(k * rows, rows)), right[0], right[1])
            y_acc[0, here, :] += re
            y_acc[1, here, :] += im

    def gather_product(a, mat):
        arrive(a)
        finish(a, mat)

    def finish(a, mat):
        if splits:
            own_part(mat, spread_into[a])
        arrive_peers(a)
        if splits:
            peer_part(mat, spread_into[a])
        else:
            product(t_buf, mat, spread_into[a], two)

    def own_part(mat, x_full):
        for i in range(RHS):
            here = pl.ds(i * rows, rows)
            w = [jnp.concatenate([x_full[c, block(row_block(k)), :] for k in range(RHS)], axis=0) for c in range(2)]
            left = jnp.concatenate(
                [jnp.concatenate([mat[c, here, block(row_block(k))] for k in range(RHS)], axis=1) for c in range(2)],
                axis=0,
            )
            re, im = times(left, w[0], w[1])
            t_acc[0, here, :] = re
            t_acc[1, here, :] = im

    def peer_part(mat, x_full):
        for i in range(RHS):
            here = pl.ds(i * rows, rows)
            re, im = t_acc[0, here, :], t_acc[1, here, :]
            for d in range(1, group):
                at_block = [k * group + (h + d) % group for k in range(RHS)]
                w = [jnp.concatenate([x_full[c, block(b), :] for b in at_block], axis=0) for c in range(2)]
                left = jnp.concatenate(
                    [jnp.concatenate([mat[c, here, block(b)] for b in at_block], axis=1) for c in range(2)], axis=0
                )
                more_re, more_im = times(left, w[0], w[1])
                re, im = re + more_re, im + more_im
            t_buf[0, here, :] = re.astype(BF)
            t_buf[1, here, :] = im.astype(BF)

    def groups():
        for d in range(1, group):
            for k in range(RHS):
                yield k * group + (h + d) % group

    def put(k):
        @pl.when(hands_on)
        def _():
            for s in range(SUB):
                xf_copy(k, s).start()
                xs_copy(FAR, k, s).start()

        @pl.when(k != r)
        def _():
            ec_copy(r).start()

        for side in range(2):
            @pl.when(edge(k, side)[2])
            def _():
                h_copy(k, side).start()

    def emit(left, right, base):
        for k in range(RHS):
            re, im = times(stacked(left, pl.ds(k * rows, rows)), right[0], right[1])
            if base:
                re, im = re + y_acc[0, k * rows : (k + 1) * rows, :], im + y_acc[1, k * rows : (k + 1) * rows, :]
            xo[0, k * rows : (k + 1) * rows, :] = re.astype(BF)
            xo[1, k * rows : (k + 1) * rows, :] = im.astype(BF)
            put(k)

    @pl.when(odd == 0)
    def _():
        for i in range(HALVES):
            rx_copy(i).start()
        for d in range(1, group):
            for k in range(RHS):
                @pl.when(k == r)
                def _():
                    for i in range(HALVES):
                        rp_copy(d, k, i).start()

        @pl.when(sec >= 2)
        def _():
            l_copy().start()

        for i in range(HALVES):
            rx_copy(i).wait_send()
        for k in range(HALVES):
            cx_copy(k, r).start()

        def ce_early(own):
            for k in range(RHS):
                @pl.when(jnp.logical_and(early, (k == r) == own))
                def _():
                    for d in range(group):
                        ce_copy(d, k).start()

        ce_early(True)
        for i in range(HALVES):
            rx_copy(i).wait_recv()
            for d in range(1, group):
                for k in range(RHS):
                    @pl.when(k != r)
                    def _():
                        rp_copy(d, k, i).start()
        cx_copy(0, 1 - r).wait_recv()
        pl.semaphore_signal(go, inc=1, device_id=at(partner, p), device_id_type=MESH)
        for k in range(1, HALVES):
            cx_copy(k, 1 - r).wait_recv()
        ce_early(False)
        all_peers()
        for k in range(RHS):
            re, im = times(stacked(c2, pl.ds(k * rows, rows)), s_full[0], s_full[1])
            here = slice(k * rows, (k + 1) * rows)
            y_acc[0, here, :] = re
            y_acc[1, here, :] = im
            y_out[0, here, :] = re.astype(BF)
            y_out[1, here, :] = im.astype(BF)
            y_copy(k).start()

        @pl.when(first)
        def _():
            for k in range(RHS):
                here = slice(k * rows, (k + 1) * rows)
                for c in range(2):
                    xo[c, here, :] = y_out[c, here, :]
                put(k)

        @pl.when(sec >= 2)
        def _():
            @pl.when(upper)
            def _():
                for d in range(group):
                    for k in range(RHS):
                        ce_copy(d, k).start()

            @pl.when(upper)
            def _():
                @pl.when(jnp.logical_not(begin))
                def _():
                    le_copy().wait_recv()
                    product(l_quad, ll_full, line, cols)
                    arrive_even(MIX)
                    product(c_quad, c2, cl_full, two)

                arrive_even(LOW)
                product(t_buf, c2, x_low, two)

                @pl.when(begin)
                def _():
                    emit(t_buf, line, True)

                @pl.when(jnp.logical_not(begin))
                def _():
                    add_on(t_buf, line)
                    arrive_even(FAR)
                    product(t_buf, c_quad, x_far, two)
                    emit(t_buf, l_quad, True)

            @pl.when(jnp.logical_not(upper))
            def _():
                arrive_even(FAR)
                product(t_buf, c2, x_far, two)
                emit(t_buf, line, True)

            @pl.when(jnp.logical_and(upper, jnp.logical_not(final)))
            def _():
                pl.semaphore_wait(sent, 1)

            np_copy().start()
            nc_copy().start()
            for k in range(RHS):
                for side in range(2):
                    @pl.when(edge(k, side)[2])
                    def _():
                        nh_copy(k, side).start()

    @pl.when(odd == 1)
    def _():
        pl.semaphore_wait(go, 1)
        for i in range(HALVES):
            rx_copy(i).start()
        for k in range(HALVES):
            cx_copy(k, r).start()

        @pl.when(sec >= 2)
        def _():
            l_copy().wait_recv()
            product(l_pair, l_in, line, cols)

            @pl.when(spot == 1)
            def _():
                ls_copy().start()

        for i in range(HALVES):
            rx_copy(i).wait_recv()
        for k in range(RHS):
            y_copy(k).wait_recv()
            here = block(row_block(k))
            both = [
                (s_full[c, here, :].astype(jnp.float32) + y_in[c, k * rows : (k + 1) * rows, :].astype(jnp.float32)).astype(BF)
                for c in range(2)
            ]
            re, im = times(jnp.concatenate(both, axis=0), line[0], line[1])
            s_full[0, here, :] = re.astype(BF)
            s_full[1, here, :] = im.astype(BF)
            for d in range(1, group):
                for i in range(HALVES):
                    rp_copy(d, k, i).start()

        @pl.when(jnp.logical_and(tops, jnp.logical_not(begin)))
        def _():
            ls_copy().wait_recv()
            le_copy().start()
            product(l_quad, ll_full, l_pair, cols)

        for k in range(HALVES):
            cx_copy(k, 1 - r).wait_recv()

        @pl.when(early)
        def _():
            for b in range(n_c):
                ce_arrival(b).wait_recv()
            product(c_pair, c2, ce_full, two)
            for k in range(RHS):
                for s in range(SUB):
                    xs_copy(MIX, k, s).start()

        all_peers()

        @pl.when(spot == 1)
        def _():
            for k in range(RHS):
                re, im = times(stacked(c2, pl.ds(k * rows, rows)), s_full[0], s_full[1])
                here = slice(k * rows, (k + 1) * rows)
                y_acc[0, here, :] = re
                y_acc[1, here, :] = im
                y_out[0, here, :] = re.astype(BF)
                y_out[1, here, :] = im.astype(BF)
                for s in range(SUB):
                    xs_copy(LOW, k, s).start()

                @pl.when(first)
                def _():
                    for c in range(2):
                        xo[c, here, :] = y_out[c, here, :]
                    put(k)

        @pl.when(tops)
        def _():
            product(y_acc, c2, s_full, two)

        @pl.when(sec >= 2)
        def _():
            @pl.when(spot == 1)
            def _():
                gather_product(FAR, c_pair)
                emit(t_buf, l_pair, True)

            @pl.when(tops)
            def _():
                @pl.when(jnp.logical_not(begin))
                def _():
                    arrive(MIX)

                arrive(LOW)
                for b in range(n_c):
                    ce_arrival(b).wait_recv()
                product(c_pair, c2, ce_full, two)

                @pl.when(jnp.logical_not(begin))
                def _():
                    arrive_peers(MIX)
                    product(c_quad, c_pair, cl_full, two)

                finish(LOW, c_pair)

                @pl.when(begin)
                def _():
                    emit(t_buf, l_pair, True)

                @pl.when(jnp.logical_not(begin))
                def _():
                    add_on(t_buf, l_pair)
                    gather_product(FAR, c_quad)
                    emit(t_buf, l_quad, True)

                @pl.when(hands_on)
                def _():
                    for k in range(RHS):
                        for s in range(SUB):
                            xf_copy(k, s).wait_send()
                            xs_copy(FAR, k, s).wait_send()
                    pl.semaphore_signal(sent, inc=1, device_id=at(partner, p), device_id_type=MESH)

    for c in range(2):
        ext[r, c, PAD : PAD + rows, :] = xo[c, block(r), :]

    column = lax.broadcasted_iota(jnp.int32, (rows, cols), 1)
    tall = rows + 2 * PAD

    def sideways(v):
        before = jnp.where(column == 0, 0.0, pltpu.roll(v, 1, 1))
        after = jnp.where(column == cols - 1, 0.0, pltpu.roll(v, cols - 1, 1))
        return before + after

    def plane(f):
        here = f[PAD : PAD + rows]
        updown = (pltpu.roll(f, 1, 0) + pltpu.roll(f, tall - 1, 0))[PAD : PAD + rows]
        faces = updown + sideways(here)
        corners = sideways(updown)
        return here, faces, corners

    for j in range(2):
        b = r if j == 0 else 1 - r
        if j == 1:
            @pl.when(jnp.logical_and(odd == 1, sec < n_s - 1))
            def _():
                np_copy().wait_recv()
                nr_copy().start()

            ec_copy(1 - r).wait_recv()

        @pl.when(p > 0)
        def _():
            h_arrival(b, 1).wait_recv()

        @pl.when(p < n_c - 1)
        def _():
            h_arrival(b, 0).wait_recv()

        for c in range(2):
            here, faces, corners = plane(ext[b, c].astype(jnp.float32))
            sol_ref[c, 0, b] = here.astype(BF)
            p_out[b, c] = (FACE * here + EDGE * faces + CORNER * corners).astype(BF)
            near_ref[c, 0, b] = FACE * faces + EDGE * corners - CENTER * here

        @pl.when(odd == 0)
        def _():
            p_copy(0, j, b).start()

        @pl.when(odd == 1)
        def _():
            p_copy(1, j, b).start()

            @pl.when(sec < n_s - 1)
            def _():
                p_copy(0, j, b).start()

    line_at = lax.broadcasted_iota(jnp.int32, (1, cols), 1)
    distance = jnp.minimum(line_at, cols - 1 - line_at).astype(jnp.float32)
    depth = jnp.full((1, cols), depth_ref[0], jnp.int32).astype(jnp.float32)
    ramp = jnp.maximum(depth - distance, 0.0) / depth
    damping = SIGMA_TOP * ramp * ramp
    loads[3].wait()
    wave_real = slow_ref[0]
    wave_imag = wave_real * damping
    for b in range(RHS):
        re, im = (ext[b, c, PAD : PAD + rows, :].astype(jnp.float32) for c in range(2))
        near_ref[0, 0, b] += wave_real * re - wave_imag * im
        near_ref[1, 0, b] += wave_real * im + wave_imag * re

    def neighbour(way):
        for j in range(2):
            b = r if j == 0 else 1 - r
            p_copy(way, j, b).wait_recv()
            for c in range(2):
                near_ref[c, 0, b] += p_in[way, b, c].astype(jnp.float32)

    @pl.when(sec > 0)
    def _():
        neighbour(0)

    @pl.when(odd == 0)
    def _():
        neighbour(1)

    @pl.when(jnp.logical_and(odd == 1, sec < n_s - 1))
    def _():
        for j in range(2):
            b = r if j == 0 else 1 - r
            nc_arrival(b).wait_recv()

            @pl.when(p > 0)
            def _():
                nh_arrival(b, 1).wait_recv()

            @pl.when(p < n_c - 1)
            def _():
                nh_arrival(b, 0).wait_recv()

            for c in range(2):
                here, faces, corners = plane(ext_next[b, c].astype(jnp.float32))
                near_ref[c, 0, b] += FACE * here + EDGE * faces + CORNER * corners

        nr_copy().wait_send()

    @pl.when(odd == 1)
    def _():
        for i in range(HALVES):
            rx_copy(i).wait_send()

    for k in range(HALVES):
        cx_copy(k, r).wait_send()
    for d in range(1, group):
        for k in range(RHS):
            for i in range(HALVES):
                rp_copy(d, k, i).wait_send()
    ec_copy(r).wait_send()
    for k in range(RHS):
        for side in range(2):
            @pl.when(edge(k, side)[2])
            def _():
                h_copy(k, side).wait_send()

    @pl.when(odd == 0)
    def _():
        for k in range(RHS):
            y_copy(k).wait_send()
        for j in range(2):
            p_copy(0, j, r).wait_send()

        @pl.when(sec >= 2)
        def _():
            l_copy().wait_send()
            nc_copy().wait_send()
            np_copy().wait_send()
            for k in range(RHS):
                for d in range(group):
                    ce_copy(d, k).wait_send()
                for side in range(2):
                    @pl.when(edge(k, side)[2])
                    def _():
                        nh_copy(k, side).wait_send()

    @pl.when(odd == 1)
    def _():
        for j in range(2):
            p_copy(1, j, r).wait_send()

        @pl.when(sec < n_s - 1)
        def _():
            for j in range(2):
                p_copy(0, j, r).wait_send()

    def spread_sent(a):
        for s in range(SUB):
            for k in range(RHS):
                for d in range(1, group):
                    xp_copy(a, d, k, s).wait_send()
            for b in range(n_c):
                xe_copy(a, b, s).wait_send()

    def passed_on(a):
        for k in range(RHS):
            for s in range(SUB):
                xs_copy(a, k, s).wait_send()

    @pl.when(spot == 1)
    def _():
        passed_on(LOW)

        @pl.when(sec >= 2)
        def _():
            ls_copy().wait_send()
            passed_on(MIX)
            spread_sent(FAR)

    @pl.when(tops)
    def _():
        spread_sent(LOW)

        @pl.when(jnp.logical_not(begin))
        def _():
            le_copy().wait_send()
            spread_sent(MIX)
            spread_sent(FAR)


def per_device(n_s, n_c, rhs_field, slowness, absorb_depth, line_inverse, cross_inverse):
    rows, cols = slowness.shape[1:]
    height = rows * n_c
    group = n_c // RHS
    two = RHS * rows
    tall = rows + 2 * PAD
    vmem = pl.BlockSpec(memory_space=pltpu.VMEM)
    hbm = pl.BlockSpec(memory_space=pl.ANY)
    dma = pltpu.SemaphoreType.DMA
    field, near = pl.pallas_call(
        functools.partial(kernel, n_s, n_c),
        out_shape=(
            jax.ShapeDtypeStruct(rhs_field.shape, BF),
            jax.ShapeDtypeStruct(rhs_field.shape, jnp.float32),
        ),
        in_specs=[hbm, hbm, pl.BlockSpec(memory_space=pltpu.SMEM), hbm, hbm],
        out_specs=(vmem, vmem),
        scratch_shapes=[
            pltpu.VMEM(rhs_field.shape, jnp.float32),
            pltpu.VMEM(slowness.shape, jnp.float32),
            pltpu.VMEM(line_inverse.shape, BF),
            pltpu.VMEM(cross_inverse.shape, BF),
            pltpu.VMEM((2, rows, cols), BF),
            pltpu.VMEM((2, height, cols), BF),
            pltpu.VMEM((2, two, height), BF),
            pltpu.VMEM((2, height, height), BF),
            pltpu.VMEM((2, cols, cols), BF),
            pltpu.VMEM((2, cols, cols), BF),
            pltpu.VMEM((2, two, height), BF),
            pltpu.VMEM((2, two, cols), BF),
            pltpu.VMEM((2, two, cols), jnp.float32),
            pltpu.VMEM((2, two, cols), jnp.float32),
            pltpu.VMEM((2, two, cols), BF),
            pltpu.VMEM((2, two, cols), BF),
            pltpu.VMEM((2, height, cols), BF),
            pltpu.VMEM((2, height, cols), BF),
            pltpu.VMEM((2, height, height), BF),
            pltpu.VMEM((2, cols, cols), BF),
            pltpu.VMEM((2, cols, cols), BF),
            pltpu.VMEM((2, two, height), BF),
            pltpu.VMEM((2, two, cols), BF),
            pltpu.VMEM((RHS, 2, tall, cols), BF),
            pltpu.VMEM((RHS, 2, tall, cols), BF),
            pltpu.VMEM((2, rows, cols), BF),
            pltpu.VMEM((RHS, 2, rows, cols), BF),
            pltpu.VMEM((2, RHS, 2, rows, cols), BF),
            pltpu.SemaphoreType.REGULAR, pltpu.SemaphoreType.REGULAR,
            dma((HALVES,)), dma((HALVES,)),
            dma((group, RHS, HALVES)), dma((n_c, HALVES)),
            dma((HALVES,)), dma((HALVES,)),
            dma((group, RHS)), dma((n_c,)),
            dma, dma,
            dma((RHS,)), dma((RHS,)),
            dma, dma, dma,
            dma((3, RHS, SUB)), dma((RHS, SUB)), dma((3, group, RHS, SUB)), dma((3, n_c, SUB)), dma((3, n_c, SUB)),
            dma, dma,
            dma((RHS, 2)), dma((RHS, 2)),
            dma((2,)), dma((RHS,)), dma, dma,
            dma((RHS, 2)), dma((RHS, 2)),
            dma((2, 2)), dma((2, RHS)), dma((4,)),
        ],
        compiler_params=pltpu.CompilerParams(
            collective_id=0, has_side_effects=True, vmem_limit_bytes=56 * 1024 * 1024
        ),
        name="sweep",
    )(rhs_field, slowness, absorb_depth, line_inverse, cross_inverse)
    return field.astype(jnp.float32), rhs_field + near


def solution(mesh):
    field = P(None, "sec", None, "cross", None)
    return jax.shard_map(
        functools.partial(per_device, mesh.shape["sec"], mesh.shape["cross"]),
        mesh=mesh,
        in_specs=(
            field,
            P("sec", "cross", None),
            P("sec"),
            P("sec", None, None, None),
            P("sec", None, "cross", None),
        ),
        out_specs=(field, field),
        check_vma=False,
    )
```

```python
import functools

import jax
import jax.numpy as jnp
from jax import lax
from jax.experimental import pallas as pl
from jax.experimental.pallas import tpu as pltpu
from jax.sharding import PartitionSpec as P

MESH = pl.DeviceIdType.MESH
SIGMA_TOP = 2.0
CENTER = 128.0 / 30.0
FACE = 14.0 / 30.0
EDGE = 3.0 / 30.0
CORNER = 1.0 / 30.0
PAD = 16
RHS = 2
SUB = 4
HALVES = 2
BF = jnp.bfloat16


def kernel(
    n_s, n_c,
    rhs_hbm, slow_hbm, depth_ref, line_hbm, cross_hbm,
    sol_ref, near_ref,
    near, rhs_ref, slow_ref, line_ref, cross_ref, r_out, s_full, c2, ce_full, l_in, l_pair, c_pair, t_buf, t_acc, y_acc, y_out, y_in, x_low, x_far, cl_full, ll_full, l_quad, c_quad, xo, ext,
    p_out, p_in,
    go, rx_send, rx_recv, rp_send, rp_recv, cx_send, cx_recv, ce_send, ce_recv, l_send, l_recv, y_send, y_recv,
    ls_send, le_send, ls_recv, xs_send, xf_send, xp_send, xe_send, x_recv, ec_send, ec_recv, h_send, h_recv,
    p_send, p_recv, in_sem,
):
    rows, cols = rhs_ref.shape[3], rhs_ref.shape[4]
    height = rows * n_c
    group = n_c // RHS
    two = RHS * rows
    piece = rows // SUB
    half_block = rows // HALVES
    sec = lax.axis_index("sec")
    p = lax.axis_index("cross")
    r = p // group
    h = p % group
    q = (p + group) % n_c
    odd = sec % 2
    partner = sec + 1 - 2 * odd
    spot = sec % 4
    upper = spot >= 2
    first = sec < 2
    begin = sec < 4
    early = jnp.logical_and(spot < 2, sec >= 2)
    below = jnp.minimum(sec + 1, n_s - 1)
    above = jnp.maximum(sec - 1, 0)

    def at(s, c):
        return {"sec": s, "cross": c}

    def remote(source, target, send, recv, where):
        return pltpu.make_async_remote_copy(
            src_ref=source, dst_ref=target, send_sem=send, recv_sem=recv,
            device_id=where, device_id_type=MESH,
        )

    loads = [
        pltpu.make_async_copy(source, target, in_sem.at[i])
        for i, (source, target) in enumerate(
            ((rhs_hbm, rhs_ref), (line_hbm, line_ref), (cross_hbm, cross_ref), (slow_hbm, slow_ref))
        )
    ]
    for load in loads:
        load.start()

    def times(left, w0, w1):
        one = jnp.dot(left, w0, preferred_element_type=jnp.float32)
        other = jnp.dot(left, w1, preferred_element_type=jnp.float32)
        half = left.shape[0] // 2
        return one[:half] - other[half:], other[:half] + one[half:]

    barrier = pltpu.get_barrier_semaphore()

    def greet(s, c):
        pl.semaphore_signal(barrier, inc=1, device_id=at(s, c), device_id_type=MESH)

    for d in range(1, n_c):
        greet(sec, (p + d) % n_c)
    for d in range(n_c):
        greet(partner, (p + d) % n_c)

    outward = jnp.where(odd == 1, below, above)
    has_outward = jnp.where(odd == 1, sec < n_s - 1, sec > 0)

    @pl.when(has_outward)
    def _():
        greet(outward, p)

    tops = spot == 3
    links = (
        (-2, jnp.logical_and(odd == 1, sec >= 2)),
        (2, jnp.logical_and(odd == 1, sec <= n_s - 3)),
        (-4, jnp.logical_and(tops, sec >= 4)),
        (4, jnp.logical_and(tops, sec <= n_s - 5)),
    )
    for way, there in links:
        @pl.when(there)
        def _():
            greet(sec + way, p)

    hands_on = jnp.logical_and(tops, sec <= n_s - 3)

    def block(b):
        return pl.ds(pl.multiple_of(b * rows, rows), rows)

    def row_block(k):
        return k * group + h

    for load in loads[:3]:
        load.wait()
    for c in range(2):
        c2[c, block(r), :] = cross_ref[0, c]

    @pl.when(odd == 1)
    def _():
        for c in range(2):
            r_out[c] = rhs_ref[c, 0, 1 - r].astype(BF)
            s_full[c, block(p), :] = rhs_ref[c, 0, r].astype(BF)

    @pl.when(odd == 0)
    def _():
        for b in (1 - r, r):
            left = jnp.concatenate([rhs_ref[c, 0, b].astype(BF) for c in range(2)], axis=0)
            re, im = times(left, line_ref[0, 0], line_ref[0, 1])
            if b is r:
                s_full[0, block(p), :] = re.astype(BF)
                s_full[1, block(p), :] = im.astype(BF)
            else:
                r_out[0] = re.astype(BF)
                r_out[1] = im.astype(BF)

    zeros_pad = jnp.zeros((PAD, cols), BF)

    @pl.when(p == 0)
    def _():
        for b in range(RHS):
            for c in range(2):
                ext[b, c, 0:PAD, :] = zeros_pad

    @pl.when(p == n_c - 1)
    def _():
        for b in range(RHS):
            for c in range(2):
                ext[b, c, PAD + rows : PAD + rows + PAD, :] = zeros_pad

    met = (
        2 * n_c - 1
        + has_outward.astype(jnp.int32)
        + sum(there.astype(jnp.int32) for _, there in links)
    )
    pl.semaphore_wait(barrier, met)

    def peer(d):
        return r * group + (h + d) % group

    def half(b, i):
        return pl.ds(pl.multiple_of(b * rows + i * half_block, half_block), half_block)

    def rx_copy(i):
        return remote(
            r_out.at[:, pl.ds(i * half_block, half_block), :], s_full.at[:, half(p, i), :], rx_send.at[i], rx_recv.at[i],
            at(sec, q),
        )

    def rp_copy(d, k, i):
        here = s_full.at[:, half(row_block(k), i), :]
        return remote(here, here, rp_send.at[d, k, i], rp_recv.at[row_block(k), i], at(sec, peer(d)))

    def rp_arrival(b, i):
        here = s_full.at[:, half(b, i), :]
        return remote(here, here, rp_send.at[0, 0, i], rp_recv.at[b, i], at(sec, q))

    def all_peers():
        for b in groups():
            for i in range(HALVES):
                rp_arrival(b, i).wait_recv()

    def cx_copy(k, whose):
        part = pl.ds(pl.multiple_of(whose * rows + k * half_block, half_block), half_block)
        return remote(
            cross_ref.at[0, :, pl.ds(k * half_block, half_block), :], c2.at[:, part, :], cx_send.at[k], cx_recv.at[k], at(sec, q)
        )

    def ce_copy(d, k):
        b = row_block(k)
        return remote(
            c2.at[:, block(k), :], ce_full.at[:, block(b), :], ce_send.at[d, k], ce_recv.at[b], at(partner, peer(d))
        )

    def ce_arrival(b):
        return remote(
            ce_full.at[:, block(b), :], ce_full.at[:, block(b), :], ce_send.at[0, 0], ce_recv.at[b], at(partner, p)
        )

    def l_copy():
        return remote(line_ref.at[0], l_in, l_send, l_recv, at(partner, p))

    def y_copy(k):
        return remote(y_out.at[:, block(k), :], y_in.at[:, block(k), :], y_send.at[k], y_recv.at[k], at(partner, p))

    def bit(b, s):
        return pl.ds(pl.multiple_of(b * rows + s * piece, piece), piece)

    spread_into = (x_low, x_far, cl_full)
    LOW, FAR, MIX = range(3)

    def xs_copy(a, k, s):
        source = (y_out, xo, c_pair)[a]
        b = row_block(k)
        return remote(
            source.at[:, bit(k, s), :], spread_into[a].at[:, bit(b, s), :], xs_send.at[a, k, s], x_recv.at[a, b, s],
            at(jnp.minimum(sec + 2, n_s - 1), p),
        )

    def xf_copy(k, s):
        b = row_block(k)
        return remote(
            xo.at[:, bit(k, s), :], x_far.at[:, bit(b, s), :], xf_send.at[k, s], x_recv.at[FAR, b, s],
            at(jnp.minimum(sec + 4, n_s - 1), p),
        )

    def xp_copy(a, d, k, s):
        b = row_block(k)
        here = spread_into[a].at[:, bit(b, s), :]
        return remote(here, here, xp_send.at[a, d, k, s], x_recv.at[a, b, s], at(sec, peer(d)))

    def xe_copy(a, b, s):
        here = spread_into[a].at[:, bit(b, s), :]
        return remote(here, here, xe_send.at[a, b, s], x_recv.at[a, b, s], at(partner, p))

    def ls_copy():
        return remote(l_pair, ll_full, ls_send, ls_recv, at(jnp.minimum(sec + 2, n_s - 1), p))

    def le_copy():
        return remote(ll_full, ll_full, le_send, ls_recv, at(partner, p))

    center = pl.ds(PAD, rows)

    def ec_copy(whose):
        return remote(xo.at[:, block(1 - r), :], ext.at[whose, :, center, :], ec_send, ec_recv, at(sec, q))

    def edge(k, side):
        b = row_block(k)
        start = k * rows + (rows - PAD) * side
        to = b - 1 + 2 * side
        exists = to >= 0 if side == 0 else to < n_c
        return pl.ds(pl.multiple_of(start, PAD), PAD), jnp.clip(to, 0, n_c - 1), exists

    def pad_at(side):
        return pl.ds((rows + PAD) * (1 - side), PAD)

    def h_copy(k, side):
        source, to, _ = edge(k, side)
        return remote(
            xo.at[:, source, :], ext.at[r, :, pad_at(side), :], h_send.at[k, side], h_recv.at[r, side], at(sec, to)
        )

    def h_arrival(b, side):
        return remote(
            ext.at[b, :, pad_at(side), :], ext.at[b, :, pad_at(side), :], h_send.at[0, side], h_recv.at[b, side], at(sec, q)
        )

    def p_copy(way, j, b, c):
        return remote(
            p_out.at[b, c], p_in.at[way, b, c], p_send.at[way, j, c], p_recv.at[way, b, c],
            at(below if way == 0 else above, p),
        )

    def stacked(ref, where):
        part = ref[:, where, :]
        return part.reshape(2 * part.shape[1], part.shape[2])

    def product(out, left, right, length):
        tile = min(128, length)

        def some(i, _):
            where = pl.ds(pl.multiple_of(i * tile, tile), tile)
            re, im = times(stacked(left, where), right[0], right[1])
            out[0, where, :] = re.astype(out.dtype)
            out[1, where, :] = im.astype(out.dtype)
            return 0

        lax.fori_loop(0, length // tile, some, 0)

    class First:
        def __init__(self, ref):
            self.ref = ref

        def __getitem__(self, c):
            return self.ref[0, c]

    line = First(line_ref)
    splits = rows % 128 == 0

    def arrive(a):
        for k in range(RHS):
            for s in range(SUB):
                xe_copy(a, row_block(k), s).wait_recv()
                for d in range(1, group):
                    xp_copy(a, d, k, s).start()
                xe_copy(a, row_block(k), s).start()

    def arrive_peers(a):
        for b in groups():
            for s in range(SUB):
                xe_copy(a, b, s).wait_recv()
                xe_copy(a, b, s).start()

    def arrive_even(a):
        for b in range(n_c):
            for s in range(SUB):
                xe_copy(a, b, s).wait_recv()

    def add_on(left, right):
        for k in range(RHS):
            here = slice(k * rows, (k + 1) * rows)
            re, im = times(stacked(left, pl.ds(k * rows, rows)), right[0], right[1])
            y_acc[0, here, :] += re
            y_acc[1, here, :] += im

    def gather_product(a, mat):
        arrive(a)
        finish(a, mat)

    def finish(a, mat):
        if splits:
            own_part(mat, spread_into[a])
        arrive_peers(a)
        if splits:
            peer_part(mat, spread_into[a])
        else:
            product(t_buf, mat, spread_into[a], two)

    def own_part(mat, x_full):
        for i in range(RHS):
            here = pl.ds(i * rows, rows)
            w = [jnp.concatenate([x_full[c, block(row_block(k)), :] for k in range(RHS)], axis=0) for c in range(2)]
            left = jnp.concatenate(
                [jnp.concatenate([mat[c, here, block(row_block(k))] for k in range(RHS)], axis=1) for c in range(2)],
                axis=0,
            )
            re, im = times(left, w[0], w[1])
            t_acc[0, here, :] = re
            t_acc[1, here, :] = im

    def peer_part(mat, x_full):
        for i in range(RHS):
            here = pl.ds(i * rows, rows)
            re, im = t_acc[0, here, :], t_acc[1, here, :]
            for d in range(1, group):
                at_block = [k * group + (h + d) % group for k in range(RHS)]
                w = [jnp.concatenate([x_full[c, block(b), :] for b in at_block], axis=0) for c in range(2)]
                left = jnp.concatenate(
                    [jnp.concatenate([mat[c, here, block(b)] for b in at_block], axis=1) for c in range(2)], axis=0
                )
                more_re, more_im = times(left, w[0], w[1])
                re, im = re + more_re, im + more_im
            t_buf[0, here, :] = re.astype(BF)
            t_buf[1, here, :] = im.astype(BF)

    def groups():
        for d in range(1, group):
            for k in range(RHS):
                yield k * group + (h + d) % group

    def put(k):
        @pl.when(hands_on)
        def _():
            for s in range(SUB):
                xf_copy(k, s).start()
                xs_copy(FAR, k, s).start()

        @pl.when(k != r)
        def _():
            ec_copy(r).start()

        for side in range(2):
            @pl.when(edge(k, side)[2])
            def _():
                h_copy(k, side).start()

    def emit(left, right, base):
        for k in range(RHS):
            re, im = times(stacked(left, pl.ds(k * rows, rows)), right[0], right[1])
            if base:
                re, im = re + y_acc[0, k * rows : (k + 1) * rows, :], im + y_acc[1, k * rows : (k + 1) * rows, :]
            xo[0, k * rows : (k + 1) * rows, :] = re.astype(BF)
            xo[1, k * rows : (k + 1) * rows, :] = im.astype(BF)
            put(k)

    @pl.when(odd == 0)
    def _():
        for i in range(HALVES):
            rx_copy(i).start()
        for d in range(1, group):
            for k in range(RHS):
                @pl.when(k == r)
                def _():
                    for i in range(HALVES):
                        rp_copy(d, k, i).start()

        @pl.when(sec >= 2)
        def _():
            l_copy().start()

        for k in range(HALVES):
            cx_copy(k, r).start()
        for i in range(HALVES):
            rx_copy(i).wait_send()

        def ce_early(own):
            for k in range(RHS):
                @pl.when(jnp.logical_and(early, (k == r) == own))
                def _():
                    for d in range(group):
                        ce_copy(d, k).start()

        ce_early(True)
        for i in range(HALVES):
            rx_copy(i).wait_recv()
            for d in range(1, group):
                for k in range(RHS):
                    @pl.when(k != r)
                    def _():
                        rp_copy(d, k, i).start()
        cx_copy(0, 1 - r).wait_recv()
        pl.semaphore_signal(go, inc=1, device_id=at(partner, p), device_id_type=MESH)
        for k in range(1, HALVES):
            cx_copy(k, 1 - r).wait_recv()
        ce_early(False)
        all_peers()
        for k in range(RHS):
            re, im = times(stacked(c2, pl.ds(k * rows, rows)), s_full[0], s_full[1])
            here = slice(k * rows, (k + 1) * rows)
            y_acc[0, here, :] = re
            y_acc[1, here, :] = im
            y_out[0, here, :] = re.astype(BF)
            y_out[1, here, :] = im.astype(BF)
            y_copy(k).start()

        @pl.when(first)
        def _():
            for k in range(RHS):
                here = slice(k * rows, (k + 1) * rows)
                for c in range(2):
                    xo[c, here, :] = y_out[c, here, :]
                put(k)

        @pl.when(sec >= 2)
        def _():
            @pl.when(upper)
            def _():
                for d in range(group):
                    for k in range(RHS):
                        ce_copy(d, k).start()

            @pl.when(upper)
            def _():
                @pl.when(jnp.logical_not(begin))
                def _():
                    le_copy().wait_recv()
                    product(l_quad, ll_full, line, cols)
                    arrive_even(MIX)
                    product(c_quad, c2, cl_full, two)

                arrive_even(LOW)
                product(t_buf, c2, x_low, two)

                @pl.when(begin)
                def _():
                    emit(t_buf, line, True)

                @pl.when(jnp.logical_not(begin))
                def _():
                    add_on(t_buf, line)
                    arrive_even(FAR)
                    product(t_buf, c_quad, x_far, two)
                    emit(t_buf, l_quad, True)

            @pl.when(jnp.logical_not(upper))
            def _():
                arrive_even(FAR)
                product(t_buf, c2, x_far, two)
                emit(t_buf, line, True)

    @pl.when(odd == 1)
    def _():
        pl.semaphore_wait(go, 1)
        for i in range(HALVES):
            rx_copy(i).start()
        for k in range(HALVES):
            cx_copy(k, r).start()

        @pl.when(sec >= 2)
        def _():
            l_copy().wait_recv()
            product(l_pair, l_in, line, cols)

            @pl.when(spot == 1)
            def _():
                ls_copy().start()

        for i in range(HALVES):
            rx_copy(i).wait_recv()
        for k in range(RHS):
            y_copy(k).wait_recv()
            here = block(row_block(k))
            both = [
                (s_full[c, here, :].astype(jnp.float32) + y_in[c, k * rows : (k + 1) * rows, :].astype(jnp.float32)).astype(BF)
                for c in range(2)
            ]
            re, im = times(jnp.concatenate(both, axis=0), line[0], line[1])
            s_full[0, here, :] = re.astype(BF)
            s_full[1, here, :] = im.astype(BF)
            for d in range(1, group):
                for i in range(HALVES):
                    rp_copy(d, k, i).start()

        @pl.when(jnp.logical_and(tops, jnp.logical_not(begin)))
        def _():
            ls_copy().wait_recv()
            le_copy().start()
            product(l_quad, ll_full, l_pair, cols)

        for k in range(HALVES):
            cx_copy(k, 1 - r).wait_recv()

        @pl.when(early)
        def _():
            for b in range(n_c):
                ce_arrival(b).wait_recv()
            product(c_pair, c2, ce_full, two)
            for k in range(RHS):
                for s in range(SUB):
                    xs_copy(MIX, k, s).start()

        all_peers()

        @pl.when(spot == 1)
        def _():
            for k in range(RHS):
                re, im = times(stacked(c2, pl.ds(k * rows, rows)), s_full[0], s_full[1])
                here = slice(k * rows, (k + 1) * rows)
                y_acc[0, here, :] = re
                y_acc[1, here, :] = im
                y_out[0, here, :] = re.astype(BF)
                y_out[1, here, :] = im.astype(BF)
                for s in range(SUB):
                    xs_copy(LOW, k, s).start()

                @pl.when(first)
                def _():
                    for c in range(2):
                        xo[c, here, :] = y_out[c, here, :]
                    put(k)

        @pl.when(tops)
        def _():
            product(y_acc, c2, s_full, two)

        @pl.when(sec >= 2)
        def _():
            @pl.when(spot == 1)
            def _():
                gather_product(FAR, c_pair)
                emit(t_buf, l_pair, True)

            @pl.when(tops)
            def _():
                @pl.when(jnp.logical_not(begin))
                def _():
                    arrive(MIX)

                arrive(LOW)
                for b in range(n_c):
                    ce_arrival(b).wait_recv()
                product(c_pair, c2, ce_full, two)

                @pl.when(jnp.logical_not(begin))
                def _():
                    arrive_peers(MIX)
                    product(c_quad, c_pair, cl_full, two)

                finish(LOW, c_pair)

                @pl.when(begin)
                def _():
                    emit(t_buf, l_pair, True)

                @pl.when(jnp.logical_not(begin))
                def _():
                    add_on(t_buf, l_pair)
                    gather_product(FAR, c_quad)
                    emit(t_buf, l_quad, True)

    for c in range(2):
        ext[r, c, PAD : PAD + rows, :] = xo[c, block(r), :]

    column = lax.broadcasted_iota(jnp.int32, (rows, cols), 1)
    tall = rows + 2 * PAD

    def sideways(v):
        before = jnp.where(column == 0, 0.0, pltpu.roll(v, 1, 1))
        after = jnp.where(column == cols - 1, 0.0, pltpu.roll(v, cols - 1, 1))
        return before + after

    def plane(f):
        here = f[PAD : PAD + rows]
        updown = (pltpu.roll(f, 1, 0) + pltpu.roll(f, tall - 1, 0))[PAD : PAD + rows]
        faces = updown + sideways(here)
        corners = sideways(updown)
        return here, faces, corners

    def both_ways(make):
        @pl.when(odd == 0)
        def _():
            make(0, 1)

        @pl.when(odd == 1)
        def _():
            make(1, 0)

    def send_planes(j, b, c):
        def go_out(inner, outer):
            @pl.when(has_outward)
            def _():
                p_copy(outer, j, b, c).start()

            p_copy(inner, j, b, c).start()

        both_ways(go_out)

    for j in range(2):
        b = r if j == 0 else 1 - r
        if j == 1:
            ec_copy(1 - r).wait_recv()

        @pl.when(p > 0)
        def _():
            h_arrival(b, 1).wait_recv()

        @pl.when(p < n_c - 1)
        def _():
            h_arrival(b, 0).wait_recv()

        for c in range(2):
            here, faces, corners = plane(ext[b, c].astype(jnp.float32))
            sol_ref[c, 0, b] = here.astype(BF)
            p_out[b, c] = (FACE * here + EDGE * faces + CORNER * corners).astype(BF)
            near[c, b] = FACE * faces + EDGE * corners

            send_planes(j, b, c)

    line_at = lax.broadcasted_iota(jnp.int32, (1, cols), 1)
    distance = jnp.minimum(line_at, cols - 1 - line_at).astype(jnp.float32)
    depth = jnp.full((1, cols), depth_ref[0], jnp.int32).astype(jnp.float32)
    ramp = jnp.maximum(depth - distance, 0.0) / depth
    damping = SIGMA_TOP * ramp * ramp
    loads[3].wait()
    wave_real = slow_ref[0]
    wave_imag = wave_real * damping
    for b in range(RHS):
        re, im = (ext[b, c, PAD : PAD + rows, :].astype(jnp.float32) for c in range(2))
        near[0, b] += wave_real * re - wave_imag * im
        near[1, b] += wave_real * im + wave_imag * re

    for j in range(2):
        b = r if j == 0 else 1 - r
        for c in range(2):
            @pl.when(odd == 0)
            def _():
                p_copy(1, j, b, c).wait_recv()
                near[c, b] += p_in[1, b, c].astype(jnp.float32)

            @pl.when(sec > 0)
            def _():
                p_copy(0, j, b, c).wait_recv()
                near[c, b] += p_in[0, b, c].astype(jnp.float32)

            @pl.when(jnp.logical_and(odd == 1, sec < n_s - 1))
            def _():
                p_copy(1, j, b, c).wait_recv()
                near[c, b] += p_in[1, b, c].astype(jnp.float32)

            near_ref[c, 0, b] = near[c, b].astype(BF)

    for j in range(2):
        for c in range(2):
            @pl.when(sec > 0)
            def _():
                p_copy(1, j, r, c).wait_send()

            @pl.when(sec < n_s - 1)
            def _():
                p_copy(0, j, r, c).wait_send()

    @pl.when(odd == 1)
    def _():
        for i in range(HALVES):
            rx_copy(i).wait_send()

    for k in range(HALVES):
        cx_copy(k, r).wait_send()
    for d in range(1, group):
        for k in range(RHS):
            for i in range(HALVES):
                rp_copy(d, k, i).wait_send()
    ec_copy(r).wait_send()
    for k in range(RHS):
        for side in range(2):
            @pl.when(edge(k, side)[2])
            def _():
                h_copy(k, side).wait_send()

    @pl.when(odd == 0)
    def _():
        for k in range(RHS):
            y_copy(k).wait_send()

        @pl.when(sec >= 2)
        def _():
            l_copy().wait_send()
            for k in range(RHS):
                for d in range(group):
                    ce_copy(d, k).wait_send()

    def spread_sent(a):
        for s in range(SUB):
            for k in range(RHS):
                for d in range(1, group):
                    xp_copy(a, d, k, s).wait_send()
            for b in range(n_c):
                xe_copy(a, b, s).wait_send()

    def passed_on(a):
        for k in range(RHS):
            for s in range(SUB):
                xs_copy(a, k, s).wait_send()

    @pl.when(spot == 1)
    def _():
        passed_on(LOW)

        @pl.when(sec >= 2)
        def _():
            ls_copy().wait_send()
            passed_on(MIX)
            spread_sent(FAR)

    @pl.when(tops)
    def _():
        spread_sent(LOW)

        @pl.when(hands_on)
        def _():
            passed_on(FAR)
            for k in range(RHS):
                for s in range(SUB):
                    xf_copy(k, s).wait_send()

        @pl.when(jnp.logical_not(begin))
        def _():
            le_copy().wait_send()
            spread_sent(MIX)
            spread_sent(FAR)


def per_device(n_s, n_c, rhs_field, slowness, absorb_depth, line_inverse, cross_inverse):
    rows, cols = slowness.shape[1:]
    height = rows * n_c
    group = n_c // RHS
    two = RHS * rows
    tall = rows + 2 * PAD
    vmem = pl.BlockSpec(memory_space=pltpu.VMEM)
    hbm = pl.BlockSpec(memory_space=pl.ANY)
    dma = pltpu.SemaphoreType.DMA
    field, near = pl.pallas_call(
        functools.partial(kernel, n_s, n_c),
        out_shape=(
            jax.ShapeDtypeStruct(rhs_field.shape, BF),
            jax.ShapeDtypeStruct(rhs_field.shape, BF),
        ),
        in_specs=[hbm, hbm, pl.BlockSpec(memory_space=pltpu.SMEM), hbm, hbm],
        out_specs=(vmem, vmem),
        scratch_shapes=[
            pltpu.VMEM((2, RHS, rows, cols), jnp.float32),
            pltpu.VMEM(rhs_field.shape, jnp.float32),
            pltpu.VMEM(slowness.shape, jnp.float32),
            pltpu.VMEM(line_inverse.shape, BF),
            pltpu.VMEM(cross_inverse.shape, BF),
            pltpu.VMEM((2, rows, cols), BF),
            pltpu.VMEM((2, height, cols), BF),
            pltpu.VMEM((2, two, height), BF),
            pltpu.VMEM((2, height, height), BF),
            pltpu.VMEM((2, cols, cols), BF),
            pltpu.VMEM((2, cols, cols), BF),
            pltpu.VMEM((2, two, height), BF),
            pltpu.VMEM((2, two, cols), BF),
            pltpu.VMEM((2, two, cols), jnp.float32),
            pltpu.VMEM((2, two, cols), jnp.float32),
            pltpu.VMEM((2, two, cols), BF),
            pltpu.VMEM((2, two, cols), BF),
            pltpu.VMEM((2, height, cols), BF),
            pltpu.VMEM((2, height, cols), BF),
            pltpu.VMEM((2, height, height), BF),
            pltpu.VMEM((2, cols, cols), BF),
            pltpu.VMEM((2, cols, cols), BF),
            pltpu.VMEM((2, two, height), BF),
            pltpu.VMEM((2, two, cols), BF),
            pltpu.VMEM((RHS, 2, tall, cols), BF),
            pltpu.VMEM((RHS, 2, rows, cols), BF),
            pltpu.VMEM((2, RHS, 2, rows, cols), BF),
            pltpu.SemaphoreType.REGULAR,
            dma((HALVES,)), dma((HALVES,)),
            dma((group, RHS, HALVES)), dma((n_c, HALVES)),
            dma((HALVES,)), dma((HALVES,)),
            dma((group, RHS)), dma((n_c,)),
            dma, dma,
            dma((RHS,)), dma((RHS,)),
            dma, dma, dma,
            dma((3, RHS, SUB)), dma((RHS, SUB)), dma((3, group, RHS, SUB)), dma((3, n_c, SUB)), dma((3, n_c, SUB)),
            dma, dma,
            dma((RHS, 2)), dma((RHS, 2)),
            dma((2, 2, 2)), dma((2, RHS, 2)), dma((4,)),
        ],
        compiler_params=pltpu.CompilerParams(
            collective_id=0, has_side_effects=True, vmem_limit_bytes=56 * 1024 * 1024
        ),
        name="sweep",
    )(rhs_field, slowness, absorb_depth, line_inverse, cross_inverse)
    solved = field.astype(jnp.float32)
    return solved, rhs_field + (near.astype(jnp.float32) - CENTER * solved)


def solution(mesh):
    field = P(None, "sec", None, "cross", None)
    return jax.shard_map(
        functools.partial(per_device, mesh.shape["sec"], mesh.shape["cross"]),
        mesh=mesh,
        in_specs=(
            field,
            P("sec", "cross", None),
            P("sec"),
            P("sec", None, None, None),
            P("sec", None, "cross", None),
        ),
        out_specs=(field, field),
        check_vma=False,
    )
```

```python
import functools

import jax
import jax.numpy as jnp
from jax import lax
from jax.experimental import pallas as pl
from jax.experimental.pallas import tpu as pltpu
from jax.sharding import PartitionSpec as P

MESH = pl.DeviceIdType.MESH
SIGMA_TOP = 2.0
CENTER = 128.0 / 30.0
FACE = 14.0 / 30.0
EDGE = 3.0 / 30.0
CORNER = 1.0 / 30.0
PAD = 16
RHS = 2
SUB = 4
HALVES = 2
BF = jnp.bfloat16


def kernel(
    n_s, n_c,
    rhs_hbm, slow_hbm, depth_ref, line_hbm, cross_hbm,
    sol_ref, near_ref,
    near, rhs_ref, slow_ref, line_ref, cross_ref, r_out, s_full, c2, ce_full, l_in, l_pair, c_pair, t_buf, t_acc, y_acc, y_out, y_in, x_low, x_far, cl_full, ll_full, l_quad, c_quad, xo, ext,
    p_out, p_in,
    go, rx_send, rx_recv, rp_send, rp_recv, cx_send, cx_recv, ce_send, ce_recv, l_send, l_recv, y_send, y_recv,
    ls_send, le_send, ls_recv, xs_send, xf_send, xp_send, xe_send, x_recv, ec_send, ec_recv, h_send, h_recv,
    p_send, p_recv, in_sem,
):
    rows, cols = rhs_ref.shape[3], rhs_ref.shape[4]
    height = rows * n_c
    group = n_c // RHS
    two = RHS * rows
    piece = rows // SUB
    half_block = rows // HALVES
    sec = lax.axis_index("sec")
    p = lax.axis_index("cross")
    r = p // group
    h = p % group
    q = (p + group) % n_c
    odd = sec % 2
    partner = sec + 1 - 2 * odd
    spot = sec % 4
    upper = spot >= 2
    first = sec < 2
    begin = sec < 4
    early = jnp.logical_and(spot < 2, sec >= 2)
    below = jnp.minimum(sec + 1, n_s - 1)
    above = jnp.maximum(sec - 1, 0)

    def at(s, c):
        return {"sec": s, "cross": c}

    def remote(source, target, send, recv, where):
        return pltpu.make_async_remote_copy(
            src_ref=source, dst_ref=target, send_sem=send, recv_sem=recv,
            device_id=where, device_id_type=MESH,
        )

    loads = [
        pltpu.make_async_copy(source, target, in_sem.at[i])
        for i, (source, target) in enumerate(
            ((rhs_hbm, rhs_ref), (line_hbm, line_ref), (cross_hbm, cross_ref), (slow_hbm, slow_ref))
        )
    ]
    for load in loads:
        load.start()

    def times(left, w0, w1):
        one = jnp.dot(left, w0, preferred_element_type=jnp.float32)
        other = jnp.dot(left, w1, preferred_element_type=jnp.float32)
        half = left.shape[0] // 2
        return one[:half] - other[half:], other[:half] + one[half:]

    barrier = pltpu.get_barrier_semaphore()

    def greet(s, c):
        pl.semaphore_signal(barrier, inc=1, device_id=at(s, c), device_id_type=MESH)

    for d in range(1, n_c):
        greet(sec, (p + d) % n_c)
    for d in range(n_c):
        greet(partner, (p + d) % n_c)

    outward = jnp.where(odd == 1, below, above)
    has_outward = jnp.where(odd == 1, sec < n_s - 1, sec > 0)

    @pl.when(has_outward)
    def _():
        greet(outward, p)

    tops = spot == 3
    links = (
        (-2, jnp.logical_and(odd == 1, sec >= 2)),
        (2, jnp.logical_and(odd == 1, sec <= n_s - 3)),
        (-4, jnp.logical_and(tops, sec >= 4)),
        (4, jnp.logical_and(tops, sec <= n_s - 5)),
    )
    for way, there in links:
        @pl.when(there)
        def _():
            greet(sec + way, p)

    hands_on = jnp.logical_and(tops, sec <= n_s - 3)

    def block(b):
        return pl.ds(pl.multiple_of(b * rows, rows), rows)

    def row_block(k):
        return k * group + h

    for load in loads[:3]:
        load.wait()
    for c in range(2):
        c2[c, block(r), :] = cross_ref[0, c]

    @pl.when(odd == 1)
    def _():
        for c in range(2):
            r_out[c] = rhs_ref[c, 0, 1 - r].astype(BF)
            s_full[c, block(p), :] = rhs_ref[c, 0, r].astype(BF)

    @pl.when(odd == 0)
    def _():
        for b in (1 - r, r):
            left = jnp.concatenate([rhs_ref[c, 0, b].astype(BF) for c in range(2)], axis=0)
            re, im = times(left, line_ref[0, 0], line_ref[0, 1])
            if b is r:
                s_full[0, block(p), :] = re.astype(BF)
                s_full[1, block(p), :] = im.astype(BF)
            else:
                r_out[0] = re.astype(BF)
                r_out[1] = im.astype(BF)

    zeros_pad = jnp.zeros((PAD, cols), BF)

    @pl.when(p == 0)
    def _():
        for b in range(RHS):
            for c in range(2):
                ext[b, c, 0:PAD, :] = zeros_pad

    @pl.when(p == n_c - 1)
    def _():
        for b in range(RHS):
            for c in range(2):
                ext[b, c, PAD + rows : PAD + rows + PAD, :] = zeros_pad

    met = (
        2 * n_c - 1
        + has_outward.astype(jnp.int32)
        + sum(there.astype(jnp.int32) for _, there in links)
    )
    pl.semaphore_wait(barrier, met)

    def peer(d):
        return r * group + (h + d) % group

    def half(b, i):
        return pl.ds(pl.multiple_of(b * rows + i * half_block, half_block), half_block)

    def rx_copy(i):
        return remote(
            r_out.at[:, pl.ds(i * half_block, half_block), :], s_full.at[:, half(p, i), :], rx_send.at[i], rx_recv.at[i],
            at(sec, q),
        )

    def rp_copy(d, k, i):
        here = s_full.at[:, half(row_block(k), i), :]
        return remote(here, here, rp_send.at[d, k, i], rp_recv.at[row_block(k), i], at(sec, peer(d)))

    def rp_arrival(b, i):
        here = s_full.at[:, half(b, i), :]
        return remote(here, here, rp_send.at[0, 0, i], rp_recv.at[b, i], at(sec, q))

    def all_peers():
        for b in groups():
            for i in range(HALVES):
                rp_arrival(b, i).wait_recv()

    def cx_copy(k, whose):
        part = pl.ds(pl.multiple_of(whose * rows + k * half_block, half_block), half_block)
        return remote(
            cross_ref.at[0, :, pl.ds(k * half_block, half_block), :], c2.at[:, part, :], cx_send.at[k], cx_recv.at[k], at(sec, q)
        )

    def ce_copy(d, k):
        b = row_block(k)
        return remote(
            c2.at[:, block(k), :], ce_full.at[:, block(b), :], ce_send.at[d, k], ce_recv.at[b], at(partner, peer(d))
        )

    def ce_arrival(b):
        return remote(
            ce_full.at[:, block(b), :], ce_full.at[:, block(b), :], ce_send.at[0, 0], ce_recv.at[b], at(partner, p)
        )

    def l_copy():
        return remote(line_ref.at[0], l_in, l_send, l_recv, at(partner, p))

    def y_copy(k):
        return remote(y_out.at[:, block(k), :], y_in.at[:, block(k), :], y_send.at[k], y_recv.at[k], at(partner, p))

    def bit(b, s):
        return pl.ds(pl.multiple_of(b * rows + s * piece, piece), piece)

    spread_into = (x_low, x_far, cl_full)
    LOW, FAR, MIX = range(3)

    def xs_copy(a, k, s):
        source = (y_out, xo, c_pair)[a]
        b = row_block(k)
        return remote(
            source.at[:, bit(k, s), :], spread_into[a].at[:, bit(b, s), :], xs_send.at[a, k, s], x_recv.at[a, b, s],
            at(jnp.minimum(sec + 2, n_s - 1), p),
        )

    def xf_copy(k, s):
        b = row_block(k)
        return remote(
            xo.at[:, bit(k, s), :], x_far.at[:, bit(b, s), :], xf_send.at[k, s], x_recv.at[FAR, b, s],
            at(jnp.minimum(sec + 4, n_s - 1), p),
        )

    def xp_copy(a, d, k, s):
        b = row_block(k)
        here = spread_into[a].at[:, bit(b, s), :]
        return remote(here, here, xp_send.at[a, d, k, s], x_recv.at[a, b, s], at(sec, peer(d)))

    def xe_copy(a, b, s):
        here = spread_into[a].at[:, bit(b, s), :]
        return remote(here, here, xe_send.at[a, b, s], x_recv.at[a, b, s], at(partner, p))

    def ls_copy():
        return remote(l_pair, ll_full, ls_send, ls_recv, at(jnp.minimum(sec + 2, n_s - 1), p))

    def le_copy():
        return remote(ll_full, ll_full, le_send, ls_recv, at(partner, p))

    center = pl.ds(PAD, rows)

    def ec_copy(whose):
        return remote(xo.at[:, block(1 - r), :], ext.at[whose, :, center, :], ec_send, ec_recv, at(sec, q))

    def edge(k, side):
        b = row_block(k)
        start = k * rows + (rows - PAD) * side
        to = b - 1 + 2 * side
        exists = to >= 0 if side == 0 else to < n_c
        return pl.ds(pl.multiple_of(start, PAD), PAD), jnp.clip(to, 0, n_c - 1), exists

    def pad_at(side):
        return pl.ds((rows + PAD) * (1 - side), PAD)

    def h_copy(k, side):
        source, to, _ = edge(k, side)
        return remote(
            xo.at[:, source, :], ext.at[r, :, pad_at(side), :], h_send.at[k, side], h_recv.at[r, side], at(sec, to)
        )

    def h_arrival(b, side):
        return remote(
            ext.at[b, :, pad_at(side), :], ext.at[b, :, pad_at(side), :], h_send.at[0, side], h_recv.at[b, side], at(sec, q)
        )

    def p_copy(way, j, b, c):
        return remote(
            p_out.at[b, c], p_in.at[way, b, c], p_send.at[way, j, c], p_recv.at[way, b, c],
            at(below if way == 0 else above, p),
        )

    def stacked(ref, where):
        part = ref[:, where, :]
        return part.reshape(2 * part.shape[1], part.shape[2])

    def product(out, left, right, length):
        tile = min(128, length)

        def some(i, _):
            where = pl.ds(pl.multiple_of(i * tile, tile), tile)
            re, im = times(stacked(left, where), right[0], right[1])
            out[0, where, :] = re.astype(out.dtype)
            out[1, where, :] = im.astype(out.dtype)
            return 0

        lax.fori_loop(0, length // tile, some, 0)

    class First:
        def __init__(self, ref):
            self.ref = ref

        def __getitem__(self, c):
            return self.ref[0, c]

    line = First(line_ref)
    splits = rows % 128 == 0

    def arrive(a):
        for k in range(RHS):
            for s in range(SUB):
                xe_copy(a, row_block(k), s).wait_recv()
                for d in range(1, group):
                    xp_copy(a, d, k, s).start()
                xe_copy(a, row_block(k), s).start()

    def arrive_peers(a):
        for b in groups():
            for s in range(SUB):
                xe_copy(a, b, s).wait_recv()
                xe_copy(a, b, s).start()

    def arrive_even(a):
        for b in range(n_c):
            for s in range(SUB):
                xe_copy(a, b, s).wait_recv()

    def add_on(left, right):
        for k in range(RHS):
            here = slice(k * rows, (k + 1) * rows)
            re, im = times(stacked(left, pl.ds(k * rows, rows)), right[0], right[1])
            y_acc[0, here, :] += re
            y_acc[1, here, :] += im

    def gather_product(a, mat):
        arrive(a)
        finish(a, mat)

    def finish(a, mat):
        if splits:
            own_part(mat, spread_into[a])
        arrive_peers(a)
        if splits:
            peer_part(mat, spread_into[a])
        else:
            product(t_buf, mat, spread_into[a], two)

    def even_product(a, mat):
        if splits:
            for k in range(RHS):
                for s in range(SUB):
                    xe_copy(a, row_block(k), s).wait_recv()
            own_part(mat, spread_into[a])
            for b in groups():
                for s in range(SUB):
                    xe_copy(a, b, s).wait_recv()
            peer_part(mat, spread_into[a])
        else:
            arrive_even(a)
            product(t_buf, mat, spread_into[a], two)

    def own_part(mat, x_full):
        for i in range(RHS):
            here = pl.ds(i * rows, rows)
            w = [jnp.concatenate([x_full[c, block(row_block(k)), :] for k in range(RHS)], axis=0) for c in range(2)]
            left = jnp.concatenate(
                [jnp.concatenate([mat[c, here, block(row_block(k))] for k in range(RHS)], axis=1) for c in range(2)],
                axis=0,
            )
            re, im = times(left, w[0], w[1])
            t_acc[0, here, :] = re
            t_acc[1, here, :] = im

    def peer_part(mat, x_full):
        for i in range(RHS):
            here = pl.ds(i * rows, rows)
            re, im = t_acc[0, here, :], t_acc[1, here, :]
            for d in range(1, group):
                at_block = [k * group + (h + d) % group for k in range(RHS)]
                w = [jnp.concatenate([x_full[c, block(b), :] for b in at_block], axis=0) for c in range(2)]
                left = jnp.concatenate(
                    [jnp.concatenate([mat[c, here, block(b)] for b in at_block], axis=1) for c in range(2)], axis=0
                )
                more_re, more_im = times(left, w[0], w[1])
                re, im = re + more_re, im + more_im
            t_buf[0, here, :] = re.astype(BF)
            t_buf[1, here, :] = im.astype(BF)

    def groups():
        for d in range(1, group):
            for k in range(RHS):
                yield k * group + (h + d) % group

    def put(k):
        @pl.when(hands_on)
        def _():
            for s in range(SUB):
                xf_copy(k, s).start()
                xs_copy(FAR, k, s).start()

        @pl.when(k != r)
        def _():
            ec_copy(r).start()

        for side in range(2):
            @pl.when(edge(k, side)[2])
            def _():
                h_copy(k, side).start()

    def emit(left, right, base):
        for k in range(RHS):
            re, im = times(stacked(left, pl.ds(k * rows, rows)), right[0], right[1])
            if base:
                re, im = re + y_acc[0, k * rows : (k + 1) * rows, :], im + y_acc[1, k * rows : (k + 1) * rows, :]
            xo[0, k * rows : (k + 1) * rows, :] = re.astype(BF)
            xo[1, k * rows : (k + 1) * rows, :] = im.astype(BF)
            put(k)

    @pl.when(odd == 0)
    def _():
        for i in range(HALVES):
            rx_copy(i).start()
        for d in range(1, group):
            for k in range(RHS):
                @pl.when(k == r)
                def _():
                    for i in range(HALVES):
                        rp_copy(d, k, i).start()

        @pl.when(sec >= 2)
        def _():
            l_copy().start()

        for k in range(HALVES):
            cx_copy(k, r).start()
        for i in range(HALVES):
            rx_copy(i).wait_send()

        def ce_early(own):
            for k in range(RHS):
                @pl.when(jnp.logical_and(early, (k == r) == own))
                def _():
                    for d in range(group):
                        ce_copy(d, k).start()

        ce_early(True)
        for i in range(HALVES):
            rx_copy(i).wait_recv()
            for d in range(1, group):
                for k in range(RHS):
                    @pl.when(k != r)
                    def _():
                        rp_copy(d, k, i).start()
        cx_copy(0, 1 - r).wait_recv()
        pl.semaphore_signal(go, inc=1, device_id=at(partner, p), device_id_type=MESH)
        for k in range(1, HALVES):
            cx_copy(k, 1 - r).wait_recv()
        ce_early(False)
        all_peers()
        for k in range(RHS):
            re, im = times(stacked(c2, pl.ds(k * rows, rows)), s_full[0], s_full[1])
            here = slice(k * rows, (k + 1) * rows)
            y_acc[0, here, :] = re
            y_acc[1, here, :] = im
            y_out[0, here, :] = re.astype(BF)
            y_out[1, here, :] = im.astype(BF)
            y_copy(k).start()

        @pl.when(first)
        def _():
            for k in range(RHS):
                here = slice(k * rows, (k + 1) * rows)
                for c in range(2):
                    xo[c, here, :] = y_out[c, here, :]
                put(k)

        @pl.when(sec >= 2)
        def _():
            @pl.when(upper)
            def _():
                for d in range(group):
                    for k in range(RHS):
                        ce_copy(d, k).start()

            @pl.when(upper)
            def _():
                @pl.when(jnp.logical_not(begin))
                def _():
                    le_copy().wait_recv()
                    product(l_quad, ll_full, line, cols)
                    arrive_even(MIX)
                    product(c_quad, c2, cl_full, two)

                arrive_even(LOW)
                product(t_buf, c2, x_low, two)

                @pl.when(begin)
                def _():
                    emit(t_buf, line, True)

                @pl.when(jnp.logical_not(begin))
                def _():
                    add_on(t_buf, line)
                    even_product(FAR, c_quad)
                    emit(t_buf, l_quad, True)

            @pl.when(jnp.logical_not(upper))
            def _():
                even_product(FAR, c2)
                emit(t_buf, line, True)

    @pl.when(odd == 1)
    def _():
        pl.semaphore_wait(go, 1)
        for i in range(HALVES):
            rx_copy(i).start()
        for k in range(HALVES):
            cx_copy(k, r).start()

        @pl.when(sec >= 2)
        def _():
            l_copy().wait_recv()
            product(l_pair, l_in, line, cols)

            @pl.when(spot == 1)
            def _():
                ls_copy().start()

        for i in range(HALVES):
            rx_copy(i).wait_recv()
        for k in range(RHS):
            y_copy(k).wait_recv()
            here = block(row_block(k))
            both = [
                (s_full[c, here, :].astype(jnp.float32) + y_in[c, k * rows : (k + 1) * rows, :].astype(jnp.float32)).astype(BF)
                for c in range(2)
            ]
            re, im = times(jnp.concatenate(both, axis=0), line[0], line[1])
            s_full[0, here, :] = re.astype(BF)
            s_full[1, here, :] = im.astype(BF)
            for d in range(1, group):
                for i in range(HALVES):
                    rp_copy(d, k, i).start()

        @pl.when(jnp.logical_and(tops, jnp.logical_not(begin)))
        def _():
            ls_copy().wait_recv()
            le_copy().start()
            product(l_quad, ll_full, l_pair, cols)

        for k in range(HALVES):
            cx_copy(k, 1 - r).wait_recv()

        @pl.when(early)
        def _():
            for b in range(n_c):
                ce_arrival(b).wait_recv()
            product(c_pair, c2, ce_full, two)
            for k in range(RHS):
                for s in range(SUB):
                    xs_copy(MIX, k, s).start()

        all_peers()

        @pl.when(spot == 1)
        def _():
            for k in range(RHS):
                re, im = times(stacked(c2, pl.ds(k * rows, rows)), s_full[0], s_full[1])
                here = slice(k * rows, (k + 1) * rows)
                y_acc[0, here, :] = re
                y_acc[1, here, :] = im
                y_out[0, here, :] = re.astype(BF)
                y_out[1, here, :] = im.astype(BF)
                for s in range(SUB):
                    xs_copy(LOW, k, s).start()

                @pl.when(first)
                def _():
                    for c in range(2):
                        xo[c, here, :] = y_out[c, here, :]
                    put(k)

        @pl.when(tops)
        def _():
            product(y_acc, c2, s_full, two)

        @pl.when(sec >= 2)
        def _():
            @pl.when(spot == 1)
            def _():
                gather_product(FAR, c_pair)
                emit(t_buf, l_pair, True)

            @pl.when(tops)
            def _():
                @pl.when(jnp.logical_not(begin))
                def _():
                    arrive(MIX)

                arrive(LOW)
                for b in range(n_c):
                    ce_arrival(b).wait_recv()
                product(c_pair, c2, ce_full, two)

                @pl.when(jnp.logical_not(begin))
                def _():
                    arrive_peers(MIX)
                    product(c_quad, c_pair, cl_full, two)

                finish(LOW, c_pair)

                @pl.when(begin)
                def _():
                    emit(t_buf, l_pair, True)

                @pl.when(jnp.logical_not(begin))
                def _():
                    add_on(t_buf, l_pair)
                    gather_product(FAR, c_quad)
                    emit(t_buf, l_quad, True)

    for c in range(2):
        ext[r, c, PAD : PAD + rows, :] = xo[c, block(r), :]

    column = lax.broadcasted_iota(jnp.int32, (rows, cols), 1)
    tall = rows + 2 * PAD

    def sideways(v):
        before = jnp.where(column == 0, 0.0, pltpu.roll(v, 1, 1))
        after = jnp.where(column == cols - 1, 0.0, pltpu.roll(v, cols - 1, 1))
        return before + after

    def plane(f):
        here = f[PAD : PAD + rows]
        updown = (pltpu.roll(f, 1, 0) + pltpu.roll(f, tall - 1, 0))[PAD : PAD + rows]
        faces = updown + sideways(here)
        corners = sideways(updown)
        return here, faces, corners

    def both_ways(make):
        @pl.when(odd == 0)
        def _():
            make(0, 1)

        @pl.when(odd == 1)
        def _():
            make(1, 0)

    def send_planes(j, b, c):
        def go_out(inner, outer):
            @pl.when(has_outward)
            def _():
                p_copy(outer, j, b, c).start()

            p_copy(inner, j, b, c).start()

        both_ways(go_out)

    for j in range(2):
        b = r if j == 0 else 1 - r
        if j == 1:
            ec_copy(1 - r).wait_recv()

        @pl.when(p > 0)
        def _():
            h_arrival(b, 1).wait_recv()

        @pl.when(p < n_c - 1)
        def _():
            h_arrival(b, 0).wait_recv()

        for c in range(2):
            here, faces, corners = plane(ext[b, c].astype(jnp.float32))
            sol_ref[c, 0, b] = here.astype(BF)
            p_out[b, c] = (FACE * here + EDGE * faces + CORNER * corners).astype(BF)
            near[c, b] = FACE * faces + EDGE * corners

            send_planes(j, b, c)

    line_at = lax.broadcasted_iota(jnp.int32, (1, cols), 1)
    distance = jnp.minimum(line_at, cols - 1 - line_at).astype(jnp.float32)
    depth = jnp.full((1, cols), depth_ref[0], jnp.int32).astype(jnp.float32)
    ramp = jnp.maximum(depth - distance, 0.0) / depth
    damping = SIGMA_TOP * ramp * ramp
    loads[3].wait()
    wave_real = slow_ref[0]
    wave_imag = wave_real * damping
    for b in range(RHS):
        re, im = (ext[b, c, PAD : PAD + rows, :].astype(jnp.float32) for c in range(2))
        near[0, b] += wave_real * re - wave_imag * im
        near[1, b] += wave_real * im + wave_imag * re

    for j in range(2):
        b = r if j == 0 else 1 - r
        for c in range(2):
            @pl.when(odd == 0)
            def _():
                p_copy(1, j, b, c).wait_recv()
                near[c, b] += p_in[1, b, c].astype(jnp.float32)

            @pl.when(sec > 0)
            def _():
                p_copy(0, j, b, c).wait_recv()
                near[c, b] += p_in[0, b, c].astype(jnp.float32)

            @pl.when(jnp.logical_and(odd == 1, sec < n_s - 1))
            def _():
                p_copy(1, j, b, c).wait_recv()
                near[c, b] += p_in[1, b, c].astype(jnp.float32)

            near_ref[c, 0, b] = near[c, b].astype(BF)

    for j in range(2):
        for c in range(2):
            @pl.when(sec > 0)
            def _():
                p_copy(1, j, r, c).wait_send()

            @pl.when(sec < n_s - 1)
            def _():
                p_copy(0, j, r, c).wait_send()

    @pl.when(odd == 1)
    def _():
        for i in range(HALVES):
            rx_copy(i).wait_send()

    for k in range(HALVES):
        cx_copy(k, r).wait_send()
    for d in range(1, group):
        for k in range(RHS):
            for i in range(HALVES):
                rp_copy(d, k, i).wait_send()
    ec_copy(r).wait_send()
    for k in range(RHS):
        for side in range(2):
            @pl.when(edge(k, side)[2])
            def _():
                h_copy(k, side).wait_send()

    @pl.when(odd == 0)
    def _():
        for k in range(RHS):
            y_copy(k).wait_send()

        @pl.when(sec >= 2)
        def _():
            l_copy().wait_send()
            for k in range(RHS):
                for d in range(group):
                    ce_copy(d, k).wait_send()

    def spread_sent(a):
        for s in range(SUB):
            for k in range(RHS):
                for d in range(1, group):
                    xp_copy(a, d, k, s).wait_send()
            for b in range(n_c):
                xe_copy(a, b, s).wait_send()

    def passed_on(a):
        for k in range(RHS):
            for s in range(SUB):
                xs_copy(a, k, s).wait_send()

    @pl.when(spot == 1)
    def _():
        passed_on(LOW)

        @pl.when(sec >= 2)
        def _():
            ls_copy().wait_send()
            passed_on(MIX)
            spread_sent(FAR)

    @pl.when(tops)
    def _():
        spread_sent(LOW)

        @pl.when(hands_on)
        def _():
            passed_on(FAR)
            for k in range(RHS):
                for s in range(SUB):
                    xf_copy(k, s).wait_send()

        @pl.when(jnp.logical_not(begin))
        def _():
            le_copy().wait_send()
            spread_sent(MIX)
            spread_sent(FAR)


def per_device(n_s, n_c, rhs_field, slowness, absorb_depth, line_inverse, cross_inverse):
    rows, cols = slowness.shape[1:]
    height = rows * n_c
    group = n_c // RHS
    two = RHS * rows
    tall = rows + 2 * PAD
    vmem = pl.BlockSpec(memory_space=pltpu.VMEM)
    hbm = pl.BlockSpec(memory_space=pl.ANY)
    dma = pltpu.SemaphoreType.DMA
    field, near = pl.pallas_call(
        functools.partial(kernel, n_s, n_c),
        out_shape=(
            jax.ShapeDtypeStruct(rhs_field.shape, BF),
            jax.ShapeDtypeStruct(rhs_field.shape, BF),
        ),
        in_specs=[hbm, hbm, pl.BlockSpec(memory_space=pltpu.SMEM), hbm, hbm],
        out_specs=(vmem, vmem),
        scratch_shapes=[
            pltpu.VMEM((2, RHS, rows, cols), jnp.float32),
            pltpu.VMEM(rhs_field.shape, jnp.float32),
            pltpu.VMEM(slowness.shape, jnp.float32),
            pltpu.VMEM(line_inverse.shape, BF),
            pltpu.VMEM(cross_inverse.shape, BF),
            pltpu.VMEM((2, rows, cols), BF),
            pltpu.VMEM((2, height, cols), BF),
            pltpu.VMEM((2, two, height), BF),
            pltpu.VMEM((2, height, height), BF),
            pltpu.VMEM((2, cols, cols), BF),
            pltpu.VMEM((2, cols, cols), BF),
            pltpu.VMEM((2, two, height), BF),
            pltpu.VMEM((2, two, cols), BF),
            pltpu.VMEM((2, two, cols), jnp.float32),
            pltpu.VMEM((2, two, cols), jnp.float32),
            pltpu.VMEM((2, two, cols), BF),
            pltpu.VMEM((2, two, cols), BF),
            pltpu.VMEM((2, height, cols), BF),
            pltpu.VMEM((2, height, cols), BF),
            pltpu.VMEM((2, height, height), BF),
            pltpu.VMEM((2, cols, cols), BF),
            pltpu.VMEM((2, cols, cols), BF),
            pltpu.VMEM((2, two, height), BF),
            pltpu.VMEM((2, two, cols), BF),
            pltpu.VMEM((RHS, 2, tall, cols), BF),
            pltpu.VMEM((RHS, 2, rows, cols), BF),
            pltpu.VMEM((2, RHS, 2, rows, cols), BF),
            pltpu.SemaphoreType.REGULAR,
            dma((HALVES,)), dma((HALVES,)),
            dma((group, RHS, HALVES)), dma((n_c, HALVES)),
            dma((HALVES,)), dma((HALVES,)),
            dma((group, RHS)), dma((n_c,)),
            dma, dma,
            dma((RHS,)), dma((RHS,)),
            dma, dma, dma,
            dma((3, RHS, SUB)), dma((RHS, SUB)), dma((3, group, RHS, SUB)), dma((3, n_c, SUB)), dma((3, n_c, SUB)),
            dma, dma,
            dma((RHS, 2)), dma((RHS, 2)),
            dma((2, 2, 2)), dma((2, RHS, 2)), dma((4,)),
        ],
        compiler_params=pltpu.CompilerParams(
            collective_id=0, has_side_effects=True, vmem_limit_bytes=56 * 1024 * 1024
        ),
        name="sweep",
    )(rhs_field, slowness, absorb_depth, line_inverse, cross_inverse)
    solved = field.astype(jnp.float32)
    return solved, rhs_field + (near.astype(jnp.float32) - CENTER * solved)


def solution(mesh):
    field = P(None, "sec", None, "cross", None)
    return jax.shard_map(
        functools.partial(per_device, mesh.shape["sec"], mesh.shape["cross"]),
        mesh=mesh,
        in_specs=(
            field,
            P("sec", "cross", None),
            P("sec"),
            P("sec", None, None, None),
            P("sec", None, "cross", None),
        ),
        out_specs=(field, field),
        check_vma=False,
    )
```

```python
import functools

import jax
import jax.numpy as jnp
from jax import lax
from jax.experimental import pallas as pl
from jax.experimental.pallas import tpu as pltpu
from jax.sharding import PartitionSpec as P

MESH = pl.DeviceIdType.MESH
SIGMA_TOP = 2.0
CENTER = 128.0 / 30.0
FACE = 14.0 / 30.0
EDGE = 3.0 / 30.0
CORNER = 1.0 / 30.0
PAD = 16
RHS = 2
SUB = 4
HALVES = 2
BF = jnp.bfloat16


def kernel(
    n_s, n_c,
    rhs_hbm, slow_hbm, depth_ref, line_hbm, cross_hbm,
    sol_ref, near_ref,
    near, rhs_ref, slow_ref, line_ref, cross_ref, r_out, s_full, c2, ce_full, l_in, l_pair, c_pair, t_buf, t_acc, y_acc, y_out, y_in, x_low, x_far, cl_full, ll_full, l_quad, c_quad, xo, ext,
    p_out, p_in,
    go, rx_send, rx_recv, rp_send, rp_recv, cx_send, cx_recv, ce_send, ce_recv, l_send, l_recv, y_send, y_recv,
    ls_send, le_send, ls_recv, xs_send, xf_send, xp_send, xe_send, x_recv, ec_send, ec_recv, h_send, h_recv,
    p_send, p_recv, in_sem,
):
    rows, cols = rhs_ref.shape[3], rhs_ref.shape[4]
    height = rows * n_c
    group = n_c // RHS
    two = RHS * rows
    piece = rows // SUB
    half_block = rows // HALVES
    sec = lax.axis_index("sec")
    p = lax.axis_index("cross")
    r = p // group
    h = p % group
    q = (p + group) % n_c
    odd = sec % 2
    partner = sec + 1 - 2 * odd
    spot = sec % 4
    upper = spot >= 2
    first = sec < 2
    begin = sec < 4
    early = jnp.logical_and(spot < 2, sec >= 2)
    below = jnp.minimum(sec + 1, n_s - 1)
    above = jnp.maximum(sec - 1, 0)

    def at(s, c):
        return {"sec": s, "cross": c}

    def remote(source, target, send, recv, where):
        return pltpu.make_async_remote_copy(
            src_ref=source, dst_ref=target, send_sem=send, recv_sem=recv,
            device_id=where, device_id_type=MESH,
        )

    loads = [
        pltpu.make_async_copy(source, target, in_sem.at[i])
        for i, (source, target) in enumerate(
            ((rhs_hbm, rhs_ref), (line_hbm, line_ref), (cross_hbm, cross_ref), (slow_hbm, slow_ref))
        )
    ]
    for load in loads:
        load.start()

    def times(left, w0, w1):
        one = jnp.dot(left, w0, preferred_element_type=jnp.float32)
        other = jnp.dot(left, w1, preferred_element_type=jnp.float32)
        half = left.shape[0] // 2
        return one[:half] - other[half:], other[:half] + one[half:]

    barrier = pltpu.get_barrier_semaphore()

    def greet(s, c):
        pl.semaphore_signal(barrier, inc=1, device_id=at(s, c), device_id_type=MESH)

    for d in range(1, n_c):
        greet(sec, (p + d) % n_c)
    for d in range(n_c):
        greet(partner, (p + d) % n_c)

    outward = jnp.where(odd == 1, below, above)
    has_outward = jnp.where(odd == 1, sec < n_s - 1, sec > 0)

    @pl.when(has_outward)
    def _():
        greet(outward, p)

    tops = spot == 3
    links = (
        (-2, jnp.logical_and(odd == 1, sec >= 2)),
        (2, jnp.logical_and(odd == 1, sec <= n_s - 3)),
        (-4, jnp.logical_and(tops, sec >= 4)),
        (4, jnp.logical_and(tops, sec <= n_s - 5)),
    )
    for way, there in links:
        @pl.when(there)
        def _():
            greet(sec + way, p)

    hands_on = jnp.logical_and(tops, sec <= n_s - 3)

    def block(b):
        return pl.ds(pl.multiple_of(b * rows, rows), rows)

    def row_block(k):
        return k * group + h

    for load in loads[:3]:
        load.wait()
    for c in range(2):
        c2[c, block(r), :] = cross_ref[0, c]

    @pl.when(odd == 1)
    def _():
        for c in range(2):
            r_out[c] = rhs_ref[c, 0, 1 - r].astype(BF)
            s_full[c, block(p), :] = rhs_ref[c, 0, r].astype(BF)

    @pl.when(odd == 0)
    def _():
        for b in (1 - r, r):
            left = jnp.concatenate([rhs_ref[c, 0, b].astype(BF) for c in range(2)], axis=0)
            re, im = times(left, line_ref[0, 0], line_ref[0, 1])
            if b is r:
                s_full[0, block(p), :] = re.astype(BF)
                s_full[1, block(p), :] = im.astype(BF)
            else:
                r_out[0] = re.astype(BF)
                r_out[1] = im.astype(BF)

    zeros_pad = jnp.zeros((PAD, cols), BF)

    @pl.when(p == 0)
    def _():
        for b in range(RHS):
            for c in range(2):
                ext[b, c, 0:PAD, :] = zeros_pad

    @pl.when(p == n_c - 1)
    def _():
        for b in range(RHS):
            for c in range(2):
                ext[b, c, PAD + rows : PAD + rows + PAD, :] = zeros_pad

    met = (
        2 * n_c - 1
        + has_outward.astype(jnp.int32)
        + sum(there.astype(jnp.int32) for _, there in links)
    )
    pl.semaphore_wait(barrier, met)

    def peer(d):
        return r * group + (h + d) % group

    def half(b, i):
        return pl.ds(pl.multiple_of(b * rows + i * half_block, half_block), half_block)

    def rx_copy(i):
        return remote(
            r_out.at[:, pl.ds(i * half_block, half_block), :], s_full.at[:, half(p, i), :], rx_send.at[i], rx_recv.at[i],
            at(sec, q),
        )

    def rp_copy(d, k, i):
        here = s_full.at[:, half(row_block(k), i), :]
        return remote(here, here, rp_send.at[d, k, i], rp_recv.at[row_block(k), i], at(sec, peer(d)))

    def rp_arrival(b, i):
        here = s_full.at[:, half(b, i), :]
        return remote(here, here, rp_send.at[0, 0, i], rp_recv.at[b, i], at(sec, q))

    def all_peers():
        for b in groups():
            for i in range(HALVES):
                rp_arrival(b, i).wait_recv()

    def cx_copy(k, whose):
        part = pl.ds(pl.multiple_of(whose * rows + k * half_block, half_block), half_block)
        return remote(
            cross_ref.at[0, :, pl.ds(k * half_block, half_block), :], c2.at[:, part, :], cx_send.at[k], cx_recv.at[k], at(sec, q)
        )

    def ce_copy(d, k):
        b = row_block(k)
        return remote(
            c2.at[:, block(k), :], ce_full.at[:, block(b), :], ce_send.at[d, k], ce_recv.at[b], at(partner, peer(d))
        )

    def ce_arrival(b):
        return remote(
            ce_full.at[:, block(b), :], ce_full.at[:, block(b), :], ce_send.at[0, 0], ce_recv.at[b], at(partner, p)
        )

    def l_copy():
        return remote(line_ref.at[0], l_in, l_send, l_recv, at(partner, p))

    def y_copy(k):
        return remote(y_out.at[:, block(k), :], y_in.at[:, block(k), :], y_send.at[k], y_recv.at[k], at(partner, p))

    def bit(b, s):
        return pl.ds(pl.multiple_of(b * rows + s * piece, piece), piece)

    spread_into = (x_low, x_far, cl_full)
    LOW, FAR, MIX = range(3)

    def xs_copy(a, k, s):
        source = (y_out, xo, c_pair)[a]
        b = row_block(k)
        return remote(
            source.at[:, bit(k, s), :], spread_into[a].at[:, bit(b, s), :], xs_send.at[a, k, s], x_recv.at[a, b, s],
            at(jnp.minimum(sec + 2, n_s - 1), p),
        )

    def xf_copy(k, s):
        b = row_block(k)
        return remote(
            xo.at[:, bit(k, s), :], x_far.at[:, bit(b, s), :], xf_send.at[k, s], x_recv.at[FAR, b, s],
            at(jnp.minimum(sec + 4, n_s - 1), p),
        )

    def xp_copy(a, d, k, s):
        b = row_block(k)
        here = spread_into[a].at[:, bit(b, s), :]
        return remote(here, here, xp_send.at[a, d, k, s], x_recv.at[a, b, s], at(sec, peer(d)))

    def xe_copy(a, b, s):
        here = spread_into[a].at[:, bit(b, s), :]
        return remote(here, here, xe_send.at[a, b, s], x_recv.at[a, b, s], at(partner, p))

    def ls_copy():
        return remote(l_pair, ll_full, ls_send, ls_recv, at(jnp.minimum(sec + 2, n_s - 1), p))

    def le_copy():
        return remote(ll_full, ll_full, le_send, ls_recv, at(partner, p))

    center = pl.ds(PAD, rows)

    def ec_copy(whose):
        return remote(xo.at[:, block(1 - r), :], ext.at[whose, :, center, :], ec_send, ec_recv, at(sec, q))

    def edge(k, side):
        b = row_block(k)
        start = k * rows + (rows - PAD) * side
        to = b - 1 + 2 * side
        exists = to >= 0 if side == 0 else to < n_c
        return pl.ds(pl.multiple_of(start, PAD), PAD), jnp.clip(to, 0, n_c - 1), exists

    def pad_at(side):
        return pl.ds((rows + PAD) * (1 - side), PAD)

    def h_copy(k, side):
        source, to, _ = edge(k, side)
        return remote(
            xo.at[:, source, :], ext.at[r, :, pad_at(side), :], h_send.at[k, side], h_recv.at[r, side], at(sec, to)
        )

    def h_arrival(b, side):
        return remote(
            ext.at[b, :, pad_at(side), :], ext.at[b, :, pad_at(side), :], h_send.at[0, side], h_recv.at[b, side], at(sec, q)
        )

    def p_copy(way, j, b, c):
        return remote(
            p_out.at[b, c], p_in.at[way, b, c], p_send.at[way, j, c], p_recv.at[way, b, c],
            at(below if way == 0 else above, p),
        )

    def stacked(ref, where):
        part = ref[:, where, :]
        return part.reshape(2 * part.shape[1], part.shape[2])

    def product(out, left, right, length):
        tile = min(128, length)

        def some(i, _):
            where = pl.ds(pl.multiple_of(i * tile, tile), tile)
            re, im = times(stacked(left, where), right[0], right[1])
            out[0, where, :] = re.astype(out.dtype)
            out[1, where, :] = im.astype(out.dtype)
            return 0

        lax.fori_loop(0, length // tile, some, 0)

    class First:
        def __init__(self, ref):
            self.ref = ref

        def __getitem__(self, c):
            return self.ref[0, c]

    line = First(line_ref)
    splits = rows % 128 == 0

    def arrive(a):
        for k in range(RHS):
            for s in range(SUB):
                xe_copy(a, row_block(k), s).wait_recv()
                for d in range(1, group):
                    xp_copy(a, d, k, s).start()
                xe_copy(a, row_block(k), s).start()

    def arrive_peers(a):
        for b in groups():
            for s in range(SUB):
                xe_copy(a, b, s).wait_recv()
                xe_copy(a, b, s).start()

    def arrive_even(a):
        for b in range(n_c):
            for s in range(SUB):
                xe_copy(a, b, s).wait_recv()

    def add_on(left, right):
        for k in range(RHS):
            here = slice(k * rows, (k + 1) * rows)
            re, im = times(stacked(left, pl.ds(k * rows, rows)), right[0], right[1])
            y_acc[0, here, :] += re
            y_acc[1, here, :] += im

    def gather_product(a, mat):
        arrive(a)
        finish(a, mat)

    def finish(a, mat):
        if splits:
            own_part(mat, spread_into[a])
        arrive_peers(a)
        if splits:
            peer_part(mat, spread_into[a])
        else:
            product(t_buf, mat, spread_into[a], two)

    def even_product(a, mat):
        if splits:
            for k in range(RHS):
                for s in range(SUB):
                    xe_copy(a, row_block(k), s).wait_recv()
            own_part(mat, spread_into[a])
            for b in groups():
                for s in range(SUB):
                    xe_copy(a, b, s).wait_recv()
            peer_part(mat, spread_into[a])
        else:
            arrive_even(a)
            product(t_buf, mat, spread_into[a], two)

    def own_part(mat, x_full):
        for i in range(RHS):
            here = pl.ds(i * rows, rows)
            w = [jnp.concatenate([x_full[c, block(row_block(k)), :] for k in range(RHS)], axis=0) for c in range(2)]
            left = jnp.concatenate(
                [jnp.concatenate([mat[c, here, block(row_block(k))] for k in range(RHS)], axis=1) for c in range(2)],
                axis=0,
            )
            re, im = times(left, w[0], w[1])
            t_acc[0, here, :] = re
            t_acc[1, here, :] = im

    def peer_part(mat, x_full):
        for i in range(RHS):
            here = pl.ds(i * rows, rows)
            re, im = t_acc[0, here, :], t_acc[1, here, :]
            for d in range(1, group):
                at_block = [k * group + (h + d) % group for k in range(RHS)]
                w = [jnp.concatenate([x_full[c, block(b), :] for b in at_block], axis=0) for c in range(2)]
                left = jnp.concatenate(
                    [jnp.concatenate([mat[c, here, block(b)] for b in at_block], axis=1) for c in range(2)], axis=0
                )
                more_re, more_im = times(left, w[0], w[1])
                re, im = re + more_re, im + more_im
            t_buf[0, here, :] = re.astype(BF)
            t_buf[1, here, :] = im.astype(BF)

    def groups():
        for d in range(1, group):
            for k in range(RHS):
                yield k * group + (h + d) % group

    def put(k):
        @pl.when(hands_on)
        def _():
            for s in range(SUB):
                xf_copy(k, s).start()
                xs_copy(FAR, k, s).start()

        @pl.when(k != r)
        def _():
            ec_copy(r).start()

        for side in range(2):
            @pl.when(edge(k, side)[2])
            def _():
                h_copy(k, side).start()

    def emit(left, right, base):
        for k in range(RHS):
            re, im = times(stacked(left, pl.ds(k * rows, rows)), right[0], right[1])
            if base:
                re, im = re + y_acc[0, k * rows : (k + 1) * rows, :], im + y_acc[1, k * rows : (k + 1) * rows, :]
            xo[0, k * rows : (k + 1) * rows, :] = re.astype(BF)
            xo[1, k * rows : (k + 1) * rows, :] = im.astype(BF)
            put(k)

    @pl.when(odd == 0)
    def _():
        for i in range(HALVES):
            rx_copy(i).start()
        for d in range(1, group):
            for k in range(RHS):
                @pl.when(k == r)
                def _():
                    for i in range(HALVES):
                        rp_copy(d, k, i).start()

        @pl.when(sec >= 2)
        def _():
            l_copy().start()

        for k in range(HALVES):
            cx_copy(k, r).start()
        for i in range(HALVES):
            rx_copy(i).wait_send()

        def ce_early(own):
            for k in range(RHS):
                @pl.when(jnp.logical_and(early, (k == r) == own))
                def _():
                    for d in range(group):
                        ce_copy(d, k).start()

        ce_early(True)
        for i in range(HALVES):
            rx_copy(i).wait_recv()
            for d in range(1, group):
                for k in range(RHS):
                    @pl.when(k != r)
                    def _():
                        rp_copy(d, k, i).start()
        cx_copy(0, 1 - r).wait_recv()
        pl.semaphore_signal(go, inc=1, device_id=at(partner, p), device_id_type=MESH)
        for k in range(1, HALVES):
            cx_copy(k, 1 - r).wait_recv()
        ce_early(False)
        all_peers()
        for k in range(RHS):
            re, im = times(stacked(c2, pl.ds(k * rows, rows)), s_full[0], s_full[1])
            here = slice(k * rows, (k + 1) * rows)
            y_acc[0, here, :] = re
            y_acc[1, here, :] = im
            y_out[0, here, :] = re.astype(BF)
            y_out[1, here, :] = im.astype(BF)
            y_copy(k).start()

        @pl.when(first)
        def _():
            for k in range(RHS):
                here = slice(k * rows, (k + 1) * rows)
                for c in range(2):
                    xo[c, here, :] = y_out[c, here, :]
                put(k)

        @pl.when(sec >= 2)
        def _():
            @pl.when(upper)
            def _():
                for d in range(group):
                    for k in range(RHS):
                        ce_copy(d, k).start()

            @pl.when(upper)
            def _():
                @pl.when(jnp.logical_not(begin))
                def _():
                    le_copy().wait_recv()
                    product(l_quad, ll_full, line, cols)
                    arrive_even(MIX)
                    product(c_quad, c2, cl_full, two)

                arrive_even(LOW)
                product(t_buf, c2, x_low, two)

                @pl.when(begin)
                def _():
                    emit(t_buf, line, True)

                @pl.when(jnp.logical_not(begin))
                def _():
                    add_on(t_buf, line)
                    even_product(FAR, c_quad)
                    emit(t_buf, l_quad, True)

            @pl.when(jnp.logical_not(upper))
            def _():
                even_product(FAR, c2)
                emit(t_buf, line, True)

    @pl.when(odd == 1)
    def _():
        pl.semaphore_wait(go, 1)
        for i in range(HALVES):
            rx_copy(i).start()
        for k in range(HALVES):
            cx_copy(k, r).start()

        @pl.when(sec >= 2)
        def _():
            l_copy().wait_recv()
            product(l_pair, l_in, line, cols)

            @pl.when(spot == 1)
            def _():
                ls_copy().start()

        for i in range(HALVES):
            rx_copy(i).wait_recv()
        for k in range(RHS):
            y_copy(k).wait_recv()
            here = block(row_block(k))
            both = [
                (s_full[c, here, :].astype(jnp.float32) + y_in[c, k * rows : (k + 1) * rows, :].astype(jnp.float32)).astype(BF)
                for c in range(2)
            ]
            re, im = times(jnp.concatenate(both, axis=0), line[0], line[1])
            s_full[0, here, :] = re.astype(BF)
            s_full[1, here, :] = im.astype(BF)
            for d in range(1, group):
                for i in range(HALVES):
                    rp_copy(d, k, i).start()

        @pl.when(jnp.logical_and(tops, jnp.logical_not(begin)))
        def _():
            ls_copy().wait_recv()
            le_copy().start()
            product(l_quad, ll_full, l_pair, cols)

        for k in range(HALVES):
            cx_copy(k, 1 - r).wait_recv()

        @pl.when(early)
        def _():
            for b in range(n_c):
                ce_arrival(b).wait_recv()
            product(c_pair, c2, ce_full, two)
            for k in range(RHS):
                for s in range(SUB):
                    xs_copy(MIX, k, s).start()

        all_peers()

        @pl.when(spot == 1)
        def _():
            for k in range(RHS):
                re, im = times(stacked(c2, pl.ds(k * rows, rows)), s_full[0], s_full[1])
                here = slice(k * rows, (k + 1) * rows)
                y_acc[0, here, :] = re
                y_acc[1, here, :] = im
                y_out[0, here, :] = re.astype(BF)
                y_out[1, here, :] = im.astype(BF)
                for s in range(SUB):
                    xs_copy(LOW, k, s).start()

                @pl.when(first)
                def _():
                    for c in range(2):
                        xo[c, here, :] = y_out[c, here, :]
                    put(k)

        @pl.when(tops)
        def _():
            product(y_acc, c2, s_full, two)

        @pl.when(sec >= 2)
        def _():
            @pl.when(spot == 1)
            def _():
                gather_product(FAR, c_pair)
                emit(t_buf, l_pair, True)

            @pl.when(tops)
            def _():
                @pl.when(jnp.logical_not(begin))
                def _():
                    arrive(MIX)

                arrive(LOW)
                for b in range(n_c):
                    ce_arrival(b).wait_recv()
                product(c_pair, c2, ce_full, two)

                @pl.when(jnp.logical_not(begin))
                def _():
                    arrive_peers(MIX)
                    product(c_quad, c_pair, cl_full, two)

                finish(LOW, c_pair)

                @pl.when(begin)
                def _():
                    emit(t_buf, l_pair, True)

                @pl.when(jnp.logical_not(begin))
                def _():
                    add_on(t_buf, l_pair)
                    gather_product(FAR, c_quad)
                    emit(t_buf, l_quad, True)

    for c in range(2):
        ext[r, c, PAD : PAD + rows, :] = xo[c, block(r), :]

    column = lax.broadcasted_iota(jnp.int32, (rows, cols), 1)
    tall = rows + 2 * PAD

    def sideways(v):
        before = jnp.where(column == 0, 0.0, pltpu.roll(v, 1, 1))
        after = jnp.where(column == cols - 1, 0.0, pltpu.roll(v, cols - 1, 1))
        return before + after

    def plane(f):
        here = f[PAD : PAD + rows]
        updown = (pltpu.roll(f, 1, 0) + pltpu.roll(f, tall - 1, 0))[PAD : PAD + rows]
        faces = updown + sideways(here)
        corners = sideways(updown)
        return here, faces, corners

    def both_ways(make):
        @pl.when(odd == 0)
        def _():
            make(0, 1)

        @pl.when(odd == 1)
        def _():
            make(1, 0)

    def send_planes(j, b, c):
        def go_out(inner, outer):
            @pl.when(has_outward)
            def _():
                p_copy(outer, j, b, c).start()

            p_copy(inner, j, b, c).start()

        both_ways(go_out)

    for j in range(2):
        b = r if j == 0 else 1 - r
        if j == 1:
            ec_copy(1 - r).wait_recv()

        @pl.when(p > 0)
        def _():
            h_arrival(b, 1).wait_recv()

        @pl.when(p < n_c - 1)
        def _():
            h_arrival(b, 0).wait_recv()

        for c in range(2):
            here, faces, corners = plane(ext[b, c].astype(jnp.float32))
            sol_ref[c, 0, b] = here.astype(BF)
            p_out[b, c] = (FACE * here + EDGE * faces + CORNER * corners).astype(BF)
            near[c, b] = FACE * faces + EDGE * corners

            send_planes(j, b, c)

    line_at = lax.broadcasted_iota(jnp.int32, (1, cols), 1)
    distance = jnp.minimum(line_at, cols - 1 - line_at).astype(jnp.float32)
    depth = jnp.full((1, cols), depth_ref[0], jnp.int32).astype(jnp.float32)
    ramp = jnp.maximum(depth - distance, 0.0) / depth
    damping = SIGMA_TOP * ramp * ramp
    loads[3].wait()
    wave_real = slow_ref[0]
    wave_imag = wave_real * damping
    for b in range(RHS):
        re, im = (ext[b, c, PAD : PAD + rows, :].astype(jnp.float32) for c in range(2))
        near[0, b] += wave_real * re - wave_imag * im
        near[1, b] += wave_real * im + wave_imag * re

    for j in range(2):
        b = r if j == 0 else 1 - r
        for c in range(2):
            @pl.when(odd == 0)
            def _():
                p_copy(1, j, b, c).wait_recv()
                near[c, b] += p_in[1, b, c].astype(jnp.float32)

            @pl.when(sec > 0)
            def _():
                p_copy(0, j, b, c).wait_recv()
                near[c, b] += p_in[0, b, c].astype(jnp.float32)

            @pl.when(jnp.logical_and(odd == 1, sec < n_s - 1))
            def _():
                p_copy(1, j, b, c).wait_recv()
                near[c, b] += p_in[1, b, c].astype(jnp.float32)

            near_ref[c, 0, b] = near[c, b].astype(BF)

    for j in range(2):
        for c in range(2):
            @pl.when(sec > 0)
            def _():
                p_copy(1, j, r, c).wait_send()

            @pl.when(sec < n_s - 1)
            def _():
                p_copy(0, j, r, c).wait_send()

    @pl.when(odd == 1)
    def _():
        for i in range(HALVES):
            rx_copy(i).wait_send()

    for k in range(HALVES):
        cx_copy(k, r).wait_send()
    for d in range(1, group):
        for k in range(RHS):
            for i in range(HALVES):
                rp_copy(d, k, i).wait_send()
    ec_copy(r).wait_send()
    for k in range(RHS):
        for side in range(2):
            @pl.when(edge(k, side)[2])
            def _():
                h_copy(k, side).wait_send()

    @pl.when(odd == 0)
    def _():
        for k in range(RHS):
            y_copy(k).wait_send()

        @pl.when(sec >= 2)
        def _():
            l_copy().wait_send()
            for k in range(RHS):
                for d in range(group):
                    ce_copy(d, k).wait_send()

    def spread_sent(a):
        for s in range(SUB):
            for k in range(RHS):
                for d in range(1, group):
                    xp_copy(a, d, k, s).wait_send()
            for b in range(n_c):
                xe_copy(a, b, s).wait_send()

    def passed_on(a):
        for k in range(RHS):
            for s in range(SUB):
                xs_copy(a, k, s).wait_send()

    @pl.when(spot == 1)
    def _():
        passed_on(LOW)

        @pl.when(sec >= 2)
        def _():
            ls_copy().wait_send()
            passed_on(MIX)
            spread_sent(FAR)

    @pl.when(tops)
    def _():
        spread_sent(LOW)

        @pl.when(hands_on)
        def _():
            passed_on(FAR)
            for k in range(RHS):
                for s in range(SUB):
                    xf_copy(k, s).wait_send()

        @pl.when(jnp.logical_not(begin))
        def _():
            le_copy().wait_send()
            spread_sent(MIX)
            spread_sent(FAR)


def per_device(n_s, n_c, rhs_field, slowness, absorb_depth, line_inverse, cross_inverse):
    rows, cols = slowness.shape[1:]
    height = rows * n_c
    group = n_c // RHS
    two = RHS * rows
    tall = rows + 2 * PAD
    vmem = pl.BlockSpec(memory_space=pltpu.VMEM)
    hbm = pl.BlockSpec(memory_space=pl.ANY)
    dma = pltpu.SemaphoreType.DMA
    field, near = pl.pallas_call(
        functools.partial(kernel, n_s, n_c),
        out_shape=(
            jax.ShapeDtypeStruct(rhs_field.shape, BF),
            jax.ShapeDtypeStruct(rhs_field.shape, BF),
        ),
        in_specs=[hbm, hbm, pl.BlockSpec(memory_space=pltpu.SMEM), hbm, hbm],
        out_specs=(vmem, vmem),
        scratch_shapes=[
            pltpu.VMEM((2, RHS, rows, cols), jnp.float32),
            pltpu.VMEM(rhs_field.shape, jnp.float32),
            pltpu.VMEM(slowness.shape, jnp.float32),
            pltpu.VMEM(line_inverse.shape, BF),
            pltpu.VMEM(cross_inverse.shape, BF),
            pltpu.VMEM((2, rows, cols), BF),
            pltpu.VMEM((2, height, cols), BF),
            pltpu.VMEM((2, two, height), BF),
            pltpu.VMEM((2, height, height), BF),
            pltpu.VMEM((2, cols, cols), BF),
            pltpu.VMEM((2, cols, cols), BF),
            pltpu.VMEM((2, two, height), BF),
            pltpu.VMEM((2, two, cols), BF),
            pltpu.VMEM((2, two, cols), jnp.float32),
            pltpu.VMEM((2, two, cols), jnp.float32),
            pltpu.VMEM((2, two, cols), BF),
            pltpu.VMEM((2, two, cols), BF),
            pltpu.VMEM((2, height, cols), BF),
            pltpu.VMEM((2, height, cols), BF),
            pltpu.VMEM((2, height, height), BF),
            pltpu.VMEM((2, cols, cols), BF),
            pltpu.VMEM((2, cols, cols), BF),
            pltpu.VMEM((2, two, height), BF),
            pltpu.VMEM((2, two, cols), BF),
            pltpu.VMEM((RHS, 2, tall, cols), BF),
            pltpu.VMEM((RHS, 2, rows, cols), BF),
            pltpu.VMEM((2, RHS, 2, rows, cols), BF),
            pltpu.SemaphoreType.REGULAR,
            dma((HALVES,)), dma((HALVES,)),
            dma((group, RHS, HALVES)), dma((n_c, HALVES)),
            dma((HALVES,)), dma((HALVES,)),
            dma((group, RHS)), dma((n_c,)),
            dma, dma,
            dma((RHS,)), dma((RHS,)),
            dma, dma, dma,
            dma((3, RHS, SUB)), dma((RHS, SUB)), dma((3, group, RHS, SUB)), dma((3, n_c, SUB)), dma((3, n_c, SUB)),
            dma, dma,
            dma((RHS, 2)), dma((RHS, 2)),
            dma((2, 2, 2)), dma((2, RHS, 2)), dma((4,)),
        ],
        compiler_params=pltpu.CompilerParams(
            collective_id=0, has_side_effects=True, vmem_limit_bytes=52 * 1024 * 1024
        ),
        name="sweep",
    )(rhs_field, slowness, absorb_depth, line_inverse, cross_inverse)
    solved = field.astype(jnp.float32)
    return solved, rhs_field + (near.astype(jnp.float32) - CENTER * solved)


def solution(mesh):
    field = P(None, "sec", None, "cross", None)
    return jax.shard_map(
        functools.partial(per_device, mesh.shape["sec"], mesh.shape["cross"]),
        mesh=mesh,
        in_specs=(
            field,
            P("sec", "cross", None),
            P("sec"),
            P("sec", None, None, None),
            P("sec", None, "cross", None),
        ),
        out_specs=(field, field),
        check_vma=False,
    )
```
